32 devices in a mesh: member: 2 (over x), sub: 8 (over z, y), var: 2 (over core).
Axes of the slice: x: 2, y: 2, z: 4, core: 2. Of those that a mesh axis runs over, the one named last changes fastest.
Arguments:
- innovations: float32 [8, 65536], P('var', ('member', 'sub')), parts along dimension 1, may hold values from -6 to 6
- obs_owner: int32 [65536, 1], P(('member', 'sub')), parts along dimension 0, may hold values from 0 to 7; in each aligned block of 4096 rows (0 to 4095, 4096 to 8191, ...) at most 1024 rows name the same one
- obs_local: int32 [65536], P(('member', 'sub')), parts along dimension 0, may hold values from 0 to 2047
- obs_level: int32 [65536, 1], P(('member', 'sub')), parts along dimension 0, may hold values from 0 to 63; in each aligned block of 4096 rows (0 to 4095, 4096 to 8191, ...) at most 128 rows name the same one
- band_width: int32 [64], replicated, may hold values from 2 to 16
- vert_scale: float32 [8, 64], P('var'), may hold values from 1 to 4
- sigma: float32 [8, 64], P('var'), may hold values from 0.5 to 2
- balance: float32 [8, 8], P('var')
Outputs:
- increment: float32 [8, 64, 64, 512], P('var', None, ('member', 'sub')), parts along dimension 2
The draws below stay inside these ranges and needn't reach their ends.
There are 2 independent parts, one for each index of `member`. The reference program is written for one: setup_inputs(seed, part) draws one part's arguments, and reference() takes and returns one part's arrays. A program takes and returns all parts, laid end to end along the dimension named above; an argument that names none is the same for every part. Nothing has to cross between parts.
Inputs may be any that keep to these rules, and one draw needn't show every extreme that they name: `obs_owner`: in the rows of one device no subdomain is named more than 1024 times, a bound that some block reaches. `obs_level`: in the rows of one device no level is named more than 128 times, a bound that some block reaches.
All inputs are finite; a program needn't handle non-finite values.
Results may differ from the reference program's by a relative error of at most 0.00008.
Values sent between devices are 32-bit elements; how exact they have to be, the bound alone decides.
No kernel may reach another device: no remote copies, remote signals or barrier semaphores. Data moves between devices by JAX's collectives and lax.ppermute only.
A program may use at most 192 MiB of HBM per device.

```python
import math
import jax
import jax.numpy as jnp
import numpy as np
from jax import lax

V = 8
LEV = 64
VB = 6
NX_DEV = 4
NY = 512
OBS_DEV = 4096
NX = 32
OBS = 32768
CAP = 1024
LCAP = 128
N_SUB = 8


def draw_balance(key, part):
    noise = jax.random.normal(key, (V, V), jnp.float32)
    index = jnp.arange(V)
    eye = (index[:, None] == index[None, :]).astype(jnp.float32)
    return eye + 0.3 * noise


def with_ends(drawn, stream_key, smallest, top_value):
    longest = drawn.shape.index(max(drawn.shape))
    spots = []
    for shift in (0, 1):
        where = [jax.random.randint(jax.random.fold_in(stream_key, axis), (), 0, length) for axis, length in enumerate(drawn.shape)]
        where[longest] = (where[longest] + shift) % drawn.shape[longest]
        spots.append(tuple(where))
    return drawn.at[spots[0]].set(smallest).at[spots[1]].set(top_value)


def block_levels(rng, dims, shards, low, largest):
    level, own = 1.0, jax.random.fold_in(rng, 6)
    for dim, shards_of in shards:
        heights = jnp.exp(jax.random.uniform(jax.random.fold_in(own, dim), (shards_of,), jnp.float32, low / len(shards), largest / len(shards)))
        level = level * jnp.repeat(heights, dims[dim] // shards_of).reshape([-1 if axis == dim else 1 for axis in range(len(dims))])
    return level


def deal_out(stream_key, own, number, rows, number_of, top, reach, skew):
    ranking = jax.random.permutation(stream_key, number_of)
    heavy_load, common = shares(number_of, rows * top, reach, skew, True), shares(number_of, rows * top, reach, skew, False)
    places = jnp.arange(number_of)

    def named(lengths, offset_by):
        used = int((lengths > 0).sum())
        fixed = max(1, used // 4)
        moved = fixed + (places - fixed + offset_by * (used - fixed)) % max(1, number_of - fixed)
        return jnp.zeros((number_of,), jnp.int32).at[ranking[jnp.where(places < fixed, places, moved)]].set(jnp.asarray(lengths, jnp.int32))

    lengths = jnp.where(number % 4 == 0, named(heavy_load, number // 4), named(common, number - number // 4 - 1))
    mixed = jax.random.permutation(jax.random.fold_in(own, 3), number_of)
    giver, receiver = mixed[0:number_of // 2 * 2:2], mixed[1:number_of // 2 * 2:2]
    room = jnp.minimum(lengths[giver] - 1, reach - lengths[receiver]) // 2
    room = jnp.where((giver == ranking[0]) | (receiver == ranking[0]) | (lengths[receiver] == 0), 0, jnp.maximum(room, 0))
    moved = jax.random.randint(jax.random.fold_in(own, 4), (number_of // 2,), 0, 1 << 20) % (room + 1)
    lengths = lengths.at[giver].add(-moved).at[receiver].add(moved)
    items = jnp.searchsorted(jnp.cumsum(lengths), jnp.arange(rows * top), side="right").astype(jnp.int32)
    grid = items.reshape(top, rows).T
    grid = grid[jax.random.permutation(jax.random.fold_in(own, 1), rows)]
    offset_by = jax.random.randint(jax.random.fold_in(own, 2), (rows, 1), 0, top)
    return jnp.take_along_axis(grid, (jnp.arange(top)[None, :] + offset_by) % top, axis=1)


def shares(amount, total, most, slope, full):
    loads = [(1 << 20) // math.isqrt(standing ** slope) + 1 for standing in range(1, amount + 1)]
    largest = most if full else min(most, max(-(-total // amount), total * loads[0] // sum(loads)))
    least = 1 if total - largest >= amount - 1 else 0
    holding, spare = [largest] + [least] * (amount - 1), total - largest - least * (amount - 1)
    while spare > 0:
        free = [i for i in range(1, amount) if holding[i] < largest] or [i for i in range(1, amount) if holding[i] < most]
        pool, remaining = sum([loads[i] for i in free]), spare
        for i in free:
            addition = min(most - holding[i], max(1, remaining * loads[i] // pool), spare)
            holding[i] = holding[i] + addition
            spare = spare - addition
    return np.array(holding)


def gaussian(stream_key, extent, scale, reach, split=(), held_as=jnp.bfloat16):
    factor_of = block_levels(stream_key, extent, split, -0.22, 0.18) if split else 1.0
    drawn = jax.random.normal(stream_key, extent, jnp.float32) * scale * factor_of
    return jnp.minimum(jnp.maximum(drawn, -reach), reach).astype(held_as)


def setup_inputs(seed: int = 0, part: int = 0) -> dict:
    streams_of = jax.random.split(jax.random.key(seed), 9)
    part_splits = jax.random.split(jax.random.fold_in(streams_of[8], part), 9)
    innovations = gaussian(part_splits[0], (V, OBS), 1.0, 6.0, ((0, 2), (1, 8)), jnp.float32)
    obs_owner_keys = jax.random.split(jax.random.fold_in(part_splits[1], 1), OBS // OBS_DEV)
    obs_owner_turns = jax.random.permutation(jax.random.fold_in(part_splits[1], 3), OBS // OBS_DEV)
    obs_owner = jax.vmap(lambda own, number: deal_out(jax.random.fold_in(part_splits[1], 2), own, number, OBS_DEV, N_SUB, 1, CAP, 2))(obs_owner_keys, obs_owner_turns).reshape((OBS, 1))
    obs_local = with_ends(jax.random.randint(part_splits[2], (OBS,), 0, NX_DEV * NY), jax.random.fold_in(part_splits[2], 1), 0, (NX_DEV * NY) - 1).astype(jnp.int32)
    obs_level_keys = jax.random.split(jax.random.fold_in(part_splits[3], 1), OBS // OBS_DEV)
    obs_level_turns = jax.random.permutation(jax.random.fold_in(part_splits[3], 3), OBS // OBS_DEV)
    obs_level = jax.vmap(lambda own, number: deal_out(jax.random.fold_in(part_splits[3], 2), own, number, OBS_DEV, LEV, 1, LCAP, 1))(obs_level_keys, obs_level_turns).reshape((OBS, 1))
    band_width = with_ends(jax.random.randint(streams_of[4], (LEV,), 2, 4 * NX_DEV + 1), jax.random.fold_in(streams_of[4], 1), 2, 4 * NX_DEV).astype(jnp.int32)
    vert_scale = jnp.clip(jnp.exp(math.log(4.0) - 1.3862944 * jax.random.uniform(streams_of[5], (V, LEV), jnp.float32) ** block_levels(streams_of[5], (V, LEV), ((0, 2),), -0.2, 0.2)), 1.0, 4.0)
    sigma = jnp.clip(jnp.exp(math.log(2.0) - 1.3862944 * jax.random.uniform(streams_of[6], (V, LEV), jnp.float32) ** block_levels(streams_of[6], (V, LEV), ((0, 2),), -0.2, 0.2)), 0.5, 2.0)
    balance = draw_balance(jax.random.fold_in(streams_of[8], 71), part)
    return {"innovations": innovations, "obs_owner": obs_owner, "obs_local": obs_local, "obs_level": obs_level, "band_width": band_width, "vert_scale": vert_scale, "sigma": sigma, "balance": balance}


def filter_matrix(width, count):
    rate = width.astype(jnp.float32)[:, None, None]
    index = jnp.arange(count)
    dist = jnp.abs(index[:, None] - index[None, :]).astype(jnp.float32)
    far = (count - jnp.maximum(index[:, None], index[None, :])).astype(jnp.float32)
    return jnp.exp(-dist / rate) * (1.0 - jnp.exp(-2.0 * far / rate))


def vertical_matrix(scale):
    index = jnp.arange(LEV)
    dist = (index[:, None] - index[None, :]).astype(jnp.float32)
    corr = jnp.exp(-dist * dist / (2.0 * scale[:, :, None] * scale[:, None, :]))
    return jnp.where(jnp.abs(dist) <= VB, corr, jnp.float32(0.0))


def reference(innovations, obs_owner, obs_local, obs_level, band_width, vert_scale, sigma, balance):
    column_x = obs_owner[:, 0] * NX_DEV + obs_local // NY
    column_y = obs_local % NY
    flat = ((obs_level[:, 0] * NX + column_x) * NY + column_y).astype(jnp.int32)
    adjoint = jnp.zeros((V, LEV * NX * NY), jnp.float32).at[:, flat].add(innovations)
    adjoint = adjoint.reshape(V, LEV, NX, NY)
    across = filter_matrix(band_width, NX)
    along = filter_matrix(band_width, NY)
    high = lax.Precision.HIGHEST

    def per_level(packed):
        mat_x, mat_y, field = packed
        part = jnp.einsum("ij,vjy->viy", mat_x, field, precision=high)
        return jnp.einsum("vxj,yj->vxy", part, mat_y, precision=high)

    smoothed = lax.map(per_level, (across, along, jnp.transpose(adjoint, (1, 0, 2, 3))))
    smoothed = jnp.transpose(smoothed, (1, 0, 2, 3))
    corr = vertical_matrix(vert_scale)
    correlated = jnp.einsum("vlm,vmxy->vlxy", corr, smoothed, precision=high)
    mixed = jnp.einsum("vu,ulxy->vlxy", balance, correlated, precision=high)
    return mixed * sigma[:, :, None, None]
```

```python
import functools

import jax
import jax.numpy as jnp
from jax import lax
from jax.experimental import pallas as pl
from jax.experimental.pallas import tpu as pltpu
from jax.sharding import PartitionSpec as P

VB = 6
NX_DEV = 4
NY = 512
LANES = 128
HALF = 256
F32 = jnp.float32
BF16 = jnp.bfloat16


def nt_dot(a, b):
    return lax.dot_general(a, b, (((1,), (1,)), ((), ())), preferred_element_type=F32)


def nn_dot(a, b):
    return jnp.dot(a, b, preferred_element_type=F32)


def iota(shape, dim):
    return lax.broadcasted_iota(jnp.int32, shape, dim)


def route_kernel(inn, level, owner, local, pay, hot, pre, dest, left, right):
    nvar, nobs = inn.shape
    chunks = nobs // LANES
    levels = hot.shape[0] // chunks
    rows = iota((levels, LANES), 0)
    for c in range(chunks):
        hit = jnp.where(rows == level[c : c + 1, :], 1.0, 0.0)
        hot[c * levels : (c + 1) * levels, :] = hit.astype(BF16)
    before = iota((LANES, 2 * LANES), 0) < iota((LANES, 2 * LANES), 1)
    pre[...] = nn_dot(hot[...], jnp.where(before, 1.0, 0.0).astype(BF16))
    count = jnp.zeros((levels, LANES), F32)
    for c in range(chunks):
        count = count + pre[c * levels : (c + 1) * levels, LANES:]
    lower = iota((levels, levels), 1) < iota((levels, levels), 0)
    base = nn_dot(jnp.where(lower, 1.0, 0.0).astype(BF16), count.astype(BF16))
    lane = iota((levels, LANES), 1)
    starts = jnp.sum(jnp.where(lane == rows, base, 0.0), 0, keepdims=True)
    starts = jnp.where(iota((8, LANES), 1) < levels, starts, float(nobs))
    for c in range(chunks):
        part = pre[c * levels : (c + 1) * levels, :]
        slot = jnp.where(rows == level[c : c + 1, :], part[:, :LANES] + base, 0.0)
        dest[c : c + 1, :] = jnp.sum(slot, 0, keepdims=True).astype(jnp.int32)
        base = base + part[:, LANES:]
    place = owner[...] * (NX_DEV * NY) + local[...]
    rows_hi, rows_lo = iota((chunks, LANES), 0), iota((LANES, LANES), 0)
    for c in range(chunks):
        at = slice(c * LANES, (c + 1) * LANES)
        slot = dest[c : c + 1, :]
        mask = rows_hi == slot // LANES
        right[:, at] = jnp.where(rows_lo == slot % LANES, 1.0, 0.0).astype(BF16)
        pieces = []
        for v in range(nvar):
            value = inn[v : v + 1, at]
            high = value.astype(BF16).astype(F32)
            pieces += [high, value - high]
        spot = place[c : c + 1, :]
        pieces += [(spot // HALF).astype(F32), (spot % HALF).astype(F32)]
        for q, piece in enumerate(pieces):
            left[q * chunks : (q + 1) * chunks, at] = jnp.where(mask, piece, 0.0).astype(BF16)
    packed = nt_dot(left[...], right[...])
    for v in range(nvar):
        both = packed[2 * v * chunks : (2 * v + 1) * chunks] + packed[(2 * v + 1) * chunks : (2 * v + 2) * chunks]
        pay[pl.ds(v, chunks, stride=nvar), :] = both
    high, low = packed[2 * nvar * chunks : (2 * nvar + 1) * chunks], packed[(2 * nvar + 1) * chunks :]
    pay[nvar * chunks : (nvar + 1) * chunks, :] = high * float(HALF) + low
    pay[(nvar + 1) * chunks :, :] = starts


def route(innovations, owner, level, local, levels):
    nvar, nobs = innovations.shape
    chunks = nobs // LANES
    pieces = 2 * nvar + 2
    return pl.pallas_call(
        route_kernel,
        out_shape=jax.ShapeDtypeStruct(((nvar + 1) * chunks + 8, LANES), F32),
        scratch_shapes=[
            pltpu.VMEM((chunks * levels, LANES), BF16),
            pltpu.VMEM((chunks * levels, 2 * LANES), F32),
            pltpu.VMEM((chunks, LANES), jnp.int32),
            pltpu.VMEM((pieces * chunks, nobs), BF16),
            pltpu.VMEM((LANES, nobs), BF16),
        ],
        compiler_params=pltpu.CompilerParams(vmem_limit_bytes=32 << 20),
        name="route",
    )(innovations, level.reshape(chunks, LANES), owner.reshape(chunks, LANES), local.reshape(chunks, LANES))


def table_kernel(width, high, low):
    depth = high.shape[0]
    row, col = iota((LANES, LANES), 0), iota((LANES, LANES), 1)
    near = jnp.abs(row - col).astype(F32)
    far = jnp.where(col < LANES // 2, LANES - row, row + 1).astype(F32)
    for k in range(depth):
        rate = width[pl.program_id(0) * depth + k].astype(F32)
        for at, dist in ((0, near), (LANES, far)):
            full = jnp.exp(-dist / rate)
            top = full.astype(BF16)
            high[k, :, at : at + LANES] = top
            low[k, :, at : at + LANES] = (full - top.astype(F32)).astype(BF16)


def tables(band_width):
    levels = band_width.shape[0]
    depth = 8
    spec = pl.BlockSpec((depth, LANES, 2 * LANES), lambda i: (i, 0, 0))
    shape = jax.ShapeDtypeStruct((levels, LANES, 2 * LANES), BF16)
    return pl.pallas_call(
        table_kernel,
        grid=(levels // depth,),
        in_specs=[pl.BlockSpec(memory_space=pltpu.SMEM)],
        out_specs=(spec, spec),
        out_shape=(shape, shape),
        name="tables",
    )(band_width)


def mix_matrix(scale, sigma, balance):
    nvar, levels = scale.shape
    index = jnp.arange(levels)
    dist = index[:, None] - jnp.repeat(index, nvar)[None, :]
    own = jnp.tile(scale.T, (1, levels))
    gap = dist.astype(F32)
    corr = jnp.exp(-gap * gap / (2.0 * own * scale.T.reshape(1, -1)))
    corr = jnp.where(jnp.abs(dist) <= VB, corr, F32(0.0))
    mix = sigma[:, :, None] * jnp.tile(balance, (1, levels))[:, None, :] * corr[None]
    mix = mix.reshape(-1, levels * nvar)
    high = lax.reduce_precision(mix, 8, 7)
    return high.astype(BF16), (mix - high).astype(BF16)


def field_kernel(sources, wide, nvar, width, first, *refs):
    own, oth, marks = refs[:sources], refs[sources : 2 * sources], refs[2 * sources : 3 * sources]
    high, low, mix_high, mix_low, out, vals, spots, left, right, slab = refs[3 * sources :]
    step = pl.program_id(0)
    depth = high.shape[0]
    chunks = (own[0].shape[0] - 8) // (nvar + 1)
    lane8 = iota((8, LANES), 1)
    sub8 = iota((8, LANES), 0)

    @pl.when(step == 0)
    def _():
        for s in range(sources):
            for c in range(0, chunks, 2):
                here, there = own[s][4 * c : 4 * c + 8, :], oth[s][4 * c : 4 * c + 8, :]
                vals[s, 8 * c : 8 * c + 8, :] = jnp.where(sub8 < 4, here, pltpu.roll(there, 4, 0))
                vals[s, 8 * c + 8 : 8 * c + 16, :] = jnp.where(sub8 < 4, pltpu.roll(here, 4, 0), there)
            vals[s, 8 * chunks :, :] = jnp.zeros((8, LANES), F32)
            spots[s, :chunks, :] = own[s][nvar * chunks : (nvar + 1) * chunks, :]
            spots[s, chunks:, :] = jnp.zeros((8, LANES), F32)

    col = first[0] + sub8 % 4
    reach = jnp.where(sub8 < 4, col, 2 * wide - col).astype(F32)
    tall = iota((HALF, LANES), 0).astype(F32).astype(BF16)
    one, zero = jnp.ones((HALF, LANES), BF16), jnp.zeros((HALF, LANES), BF16)
    line = iota((8, LANES), 1).astype(F32)

    def per_level(k, carry):
        lev = step * depth + k
        rate = width[lev].astype(F32)
        slope = -1.0 / jnp.full((8, LANES), rate, F32)
        for s in range(sources):
            start = marks[s][0, lev].astype(jnp.int32)
            size = marks[s][0, lev + 1].astype(jnp.int32) - start
            c, off = start // LANES, start % LANES
            back = lax.rem(LANES - off, LANES)
            row = pl.multiple_of(8 * c, 8)
            value = jnp.where(lane8 >= off, vals[s, pl.ds(row, 8), :], vals[s, pl.ds(row + 8, 8), :])
            value = pltpu.roll(value, back, 1)
            spot = jnp.where(lane8[:1] >= off, spots[s, pl.ds(c, 1), :], spots[s, pl.ds(c + 1, 1), :])
            spot = pltpu.roll(jnp.broadcast_to(spot, (8, LANES)), back, 1).astype(jnp.int32)
            xpos = (spot // (2 * HALF)).astype(F32)
            side = ((spot // HALF) % 2).astype(F32)
            ypos = (spot % HALF).astype(F32)
            gain = jnp.exp(jnp.abs(reach - xpos) * slope)
            gain = gain - pltpu.roll(gain, 4, 0)
            gain = jnp.where(lane8 < size, gain, 0.0)
            upper = jnp.concatenate([side, side], 0).astype(BF16)
            lower = jnp.concatenate([1.0 - side, 1.0 - side], 0).astype(BF16)
            at = slice(s * LANES, (s + 1) * LANES)
            for x in range(NX_DEV):
                term = value * jnp.broadcast_to(gain[x : x + 1, :], (8, LANES))
                top = term.astype(BF16).astype(F32)
                pair = jnp.concatenate([top, term - top], 0).astype(BF16)
                left[32 * x : 32 * x + 16, at] = pair * lower
                left[32 * x + 16 : 32 * x + 32, at] = pair * upper
            mark = jnp.broadcast_to(ypos[:1], (HALF, LANES)).astype(BF16)
            right[:, at] = jnp.where(tall == mark, one, zero)
        both = nt_dot(left[...], right[...])
        blocks = []
        for x in range(NX_DEV):
            for h in range(2):
                row = 32 * x + 16 * h
                total = both[row : row + 8] + both[row + 8 : row + 16]
                blocks += [total[:, :LANES], total[:, LANES:]]
        field = jnp.concatenate(blocks, 0)
        top = field.astype(BF16)
        rest = (field - top.astype(F32)).astype(BF16)
        mat = high[k]
        done = nn_dot(top, mat) + nn_dot(rest, mat) + nn_dot(top, low[k])
        rise = jnp.exp(line * slope)
        fall = jnp.exp((LANES - 1.0 - line) * slope)
        edge = jnp.exp((LANES - line) * slope)
        hop = jnp.exp(LANES * slope)
        for x in range(NX_DEV):
            ahead, behind, here = [], [], []
            for b in range(4):
                row = (4 * x + b) * 8
                here.append(done[row : row + 8, :LANES])
                moments = done[row : row + 8, LANES:]
                turned = pltpu.roll(moments, LANES // 2, 1)
                ahead.append(jnp.where(lane8 < LANES // 2, moments, turned))
                behind.append(jnp.where(lane8 < LANES // 2, turned, moments))
            run = ahead[0]
            for b in range(1, 4):
                here[b] = here[b] + rise * run
                run = ahead[b] + hop * run
            bound = edge * run
            run = behind[3]
            for b in (2, 1, 0):
                here[b] = here[b] + fall * run
                run = behind[b] + hop * run
            for b in (3, 2, 1, 0):
                slab[4 * x + b, pl.ds(pl.multiple_of(8 * lev, 8), 8), :] = here[b] - bound
                bound = bound * hop
        return carry

    lax.fori_loop(0, depth, per_level, 0)

    @pl.when(step == pl.num_programs(0) - 1)
    def _():
        for x in range(NX_DEV):
            for h in range(2):
                part = jnp.concatenate([slab[4 * x + 2 * h], slab[4 * x + 2 * h + 1]], 1)
                top = part.astype(BF16)
                rest = (part - top.astype(F32)).astype(BF16)
                total = nn_dot(mix_high[...], top) + nn_dot(mix_high[...], rest) + nn_dot(mix_low[...], top)
                out[:, x, h * HALF : (h + 1) * HALF] = total


def field(own, oth, band_width, first, high, low, mix_high, mix_low, nvar, levels, wide):
    sources = len(own)
    rows = own[0].shape[0]
    chunks = (rows - 8) // (nvar + 1)
    depth = 8
    whole = pl.BlockSpec((rows, LANES), lambda i: (0, 0))
    marks = pl.BlockSpec((8, LANES), lambda i: (rows // 8 - 1, 0), memory_space=pltpu.SMEM)
    table = pl.BlockSpec((depth, LANES, 2 * LANES), lambda i: (i, 0, 0))
    matrix = pl.BlockSpec(mix_high.shape, lambda i: (0, 0))
    smem = pl.BlockSpec(memory_space=pltpu.SMEM)
    out_shape = (mix_high.shape[0], NX_DEV, NY)
    return pl.pallas_call(
        functools.partial(field_kernel, sources, wide, nvar),
        grid=(levels // depth,),
        in_specs=[smem, smem] + [whole] * (2 * sources) + [marks] * sources + [table, table, matrix, matrix],
        out_specs=pl.BlockSpec(out_shape, lambda i: (0, 0, 0)),
        out_shape=jax.ShapeDtypeStruct(out_shape, F32),
        scratch_shapes=[
            pltpu.VMEM((sources, 8 * chunks + 8, LANES), F32),
            pltpu.VMEM((sources, chunks + 8, LANES), F32),
            pltpu.VMEM((32 * NX_DEV, sources * LANES), BF16),
            pltpu.VMEM((HALF, sources * LANES), BF16),
            pltpu.VMEM((4 * NX_DEV, 8 * levels, LANES), F32),
        ],
        compiler_params=pltpu.CompilerParams(vmem_limit_bytes=48 << 20),
        name="field",
    )(band_width, first, *own, *oth, *own, high, low, mix_high, mix_low)


def on_device(innovations, obs_owner, obs_local, obs_level, band_width, vert_scale, sigma, balance):
    groups = lax.axis_size("sub")
    nvar, _ = innovations.shape
    levels = band_width.shape[0]
    swap = [(0, 1), (1, 0)]
    unit = route(innovations, obs_owner, obs_level, obs_local, levels)
    own = [unit]
    for k in range(2, groups, 2):
        own.append(lax.ppermute(unit, "sub", [(i, (i + k) % groups) for i in range(groups)]))
    own += [lax.ppermute(held, "sub", [(i, i ^ 1) for i in range(groups)]) for held in own]
    oth = [lax.ppermute(held, "var", swap) for held in own]
    scale = jnp.concatenate([vert_scale, lax.ppermute(vert_scale, "var", swap)], 0)
    weights = jnp.where(lax.axis_index("var") == 0, balance, jnp.roll(balance, nvar, 1))
    mix_high, mix_low = mix_matrix(scale, sigma, weights)
    high, low = tables(band_width)
    first = (lax.axis_index("sub") * NX_DEV).astype(jnp.int32).reshape(1)
    out = field(own, oth, band_width, first, high, low, mix_high, mix_low, nvar, levels, NX_DEV * groups)
    return out.reshape(nvar, levels, NX_DEV, NY)


def solution(mesh):
    in_specs = (
        P("var", ("member", "sub")),
        P(("member", "sub"), None),
        P(("member", "sub")),
        P(("member", "sub"), None),
        P(),
        P("var", None),
        P("var", None),
        P("var", None),
    )
    out_specs = P("var", None, ("member", "sub"), None)
    return jax.shard_map(on_device, mesh=mesh, in_specs=in_specs, out_specs=out_specs, check_vma=False)
```

```python
import functools

import jax
import jax.numpy as jnp
from jax import lax
from jax.experimental import pallas as pl
from jax.experimental.pallas import tpu as pltpu
from jax.sharding import PartitionSpec as P

VB = 6
NX_DEV = 4
NY = 512
LANES = 128
HALF = 256
F32 = jnp.float32
BF16 = jnp.bfloat16


def nt_dot(a, b):
    return lax.dot_general(a, b, (((1,), (1,)), ((), ())), preferred_element_type=F32)


def nn_dot(a, b):
    return jnp.dot(a, b, preferred_element_type=F32)


def iota(shape, dim):
    return lax.broadcasted_iota(jnp.int32, shape, dim)


def route_kernel(inn, level, owner, local, pay, hot, pre, dest, left, right):
    nvar, nobs = inn.shape
    chunks = nobs // LANES
    levels = hot.shape[0] // chunks
    rows = iota((levels, LANES), 0)
    for c in range(chunks):
        hit = jnp.where(rows == level[c : c + 1, :], 1.0, 0.0)
        hot[c * levels : (c + 1) * levels, :] = hit.astype(BF16)
    before = iota((LANES, 2 * LANES), 0) < iota((LANES, 2 * LANES), 1)
    pre[...] = nn_dot(hot[...], jnp.where(before, 1.0, 0.0).astype(BF16))
    count = jnp.zeros((levels, LANES), F32)
    for c in range(chunks):
        count = count + pre[c * levels : (c + 1) * levels, LANES:]
    lower = iota((levels, levels), 1) < iota((levels, levels), 0)
    base = nn_dot(jnp.where(lower, 1.0, 0.0).astype(BF16), count.astype(BF16))
    lane = iota((levels, LANES), 1)
    starts = jnp.sum(jnp.where(lane == rows, base, 0.0), 0, keepdims=True)
    starts = jnp.where(iota((8, LANES), 1) < levels, starts, float(nobs))
    for c in range(chunks):
        part = pre[c * levels : (c + 1) * levels, :]
        slot = jnp.where(rows == level[c : c + 1, :], part[:, :LANES] + base, 0.0)
        dest[c : c + 1, :] = jnp.sum(slot, 0, keepdims=True).astype(jnp.int32)
        base = base + part[:, LANES:]
    place = owner[...] * (NX_DEV * NY) + local[...]
    rows_hi, rows_lo = iota((chunks, LANES), 0), iota((LANES, LANES), 0)
    for c in range(chunks):
        at = slice(c * LANES, (c + 1) * LANES)
        slot = dest[c : c + 1, :]
        mask = rows_hi == slot // LANES
        right[:, at] = jnp.where(rows_lo == slot % LANES, 1.0, 0.0).astype(BF16)
        pieces = []
        for v in range(nvar):
            value = inn[v : v + 1, at]
            high = value.astype(BF16).astype(F32)
            pieces += [high, value - high]
        spot = place[c : c + 1, :]
        pieces += [(spot // HALF).astype(F32), (spot % HALF).astype(F32)]
        for q, piece in enumerate(pieces):
            left[q * chunks : (q + 1) * chunks, at] = jnp.where(mask, piece, 0.0).astype(BF16)
    packed = nt_dot(left[...], right[...])
    for v in range(nvar):
        both = packed[2 * v * chunks : (2 * v + 1) * chunks] + packed[(2 * v + 1) * chunks : (2 * v + 2) * chunks]
        pay[pl.ds(v, chunks, stride=nvar), :] = both
    high, low = packed[2 * nvar * chunks : (2 * nvar + 1) * chunks], packed[(2 * nvar + 1) * chunks :]
    pay[nvar * chunks : (nvar + 1) * chunks, :] = high * float(HALF) + low
    pay[(nvar + 1) * chunks :, :] = starts


def route(innovations, owner, level, local, levels):
    nvar, nobs = innovations.shape
    chunks = nobs // LANES
    pieces = 2 * nvar + 2
    return pl.pallas_call(
        route_kernel,
        out_shape=jax.ShapeDtypeStruct(((nvar + 1) * chunks + 8, LANES), F32),
        scratch_shapes=[
            pltpu.VMEM((chunks * levels, LANES), BF16),
            pltpu.VMEM((chunks * levels, 2 * LANES), F32),
            pltpu.VMEM((chunks, LANES), jnp.int32),
            pltpu.VMEM((pieces * chunks, nobs), BF16),
            pltpu.VMEM((LANES, nobs), BF16),
        ],
        compiler_params=pltpu.CompilerParams(vmem_limit_bytes=32 << 20),
        name="route",
    )(innovations, level.reshape(chunks, LANES), owner.reshape(chunks, LANES), local.reshape(chunks, LANES))


def table_kernel(width, base, high, low):
    depth = high.shape[0]
    row, col = iota((LANES, LANES), 0), iota((LANES, LANES), 1)
    near = jnp.abs(row - col).astype(F32)
    far = jnp.where(col < LANES // 2, LANES - row, row + 1).astype(F32)
    for k in range(depth):
        rate = width[base[0] + pl.program_id(0) * depth + k].astype(F32)
        for at, dist in ((0, near), (LANES, far)):
            full = jnp.exp(-dist / rate)
            top = full.astype(BF16)
            high[k, :, at : at + LANES] = top
            low[k, :, at : at + LANES] = (full - top.astype(F32)).astype(BF16)


def tables(band_width, base, levels):
    depth = 8
    spec = pl.BlockSpec((depth, LANES, 2 * LANES), lambda i: (i, 0, 0))
    shape = jax.ShapeDtypeStruct((levels, LANES, 2 * LANES), BF16)
    return pl.pallas_call(
        table_kernel,
        grid=(levels // depth,),
        in_specs=[pl.BlockSpec(memory_space=pltpu.SMEM)] * 2,
        out_specs=(spec, spec),
        out_shape=(shape, shape),
        name="tables",
    )(band_width, base)


def mix_matrix(scale, sigma, weights, base, depth):
    nvar, levels = scale.shape
    level = base + jnp.arange(depth)
    dist = jnp.arange(levels)[:, None] - jnp.repeat(level, nvar)[None, :]
    own = jnp.tile(scale.T, (1, depth))
    other = lax.dynamic_slice_in_dim(scale, base, depth, 1).T.reshape(1, -1)
    gap = dist.astype(F32)
    corr = jnp.exp(-gap * gap / (2.0 * own * other))
    corr = jnp.where(jnp.abs(dist) <= VB, corr, F32(0.0))
    mix = sigma[:, :, None] * jnp.tile(weights, (1, depth))[:, None, :] * corr[None]
    mix = mix.reshape(-1, depth * nvar)
    high = lax.reduce_precision(mix, 8, 7)
    return high.astype(BF16), (mix - high).astype(BF16)


def gather_levels(sources, nvar, chunks, base, levels, own, oth, marks, vals, spots, queue, queue_spot, level_of, total):
    lane = iota((8, LANES), 1)
    sub = iota((8, LANES), 0)
    for s in range(sources):
        for c in range(0, chunks, 2):
            here, there = own[s][4 * c : 4 * c + 8, :], oth[s][4 * c : 4 * c + 8, :]
            vals[s, 8 * c : 8 * c + 8, :] = jnp.where(sub < 4, here, pltpu.roll(there, 4, 0))
            vals[s, 8 * c + 8 : 8 * c + 16, :] = jnp.where(sub < 4, pltpu.roll(here, 4, 0), there)
        vals[s, 8 * chunks :, :] = jnp.zeros((8, LANES), F32)
        spots[s, :chunks, :] = own[s][nvar * chunks : (nvar + 1) * chunks, :]
        spots[s, chunks:, :] = jnp.zeros((8, LANES), F32)
    nothing = jnp.zeros((8, LANES), F32)

    def rows(chunk):
        return pl.ds(pl.multiple_of(8 * chunk, 8), 8)

    def per_level(k, pair):
        lev = base + k
        held, held_spot = nothing, nothing
        end = jnp.int32(0)
        for s in range(sources):
            start = marks[s][0, lev].astype(jnp.int32)
            size = marks[s][0, lev + 1].astype(jnp.int32) - start
            c, off = jnp.minimum(start >> 7, chunks - 1), start & (LANES - 1)
            put = end & (LANES - 1)
            turn = (put - off) & (LANES - 1)
            value = jnp.where(lane >= off, vals[s, rows(c), :], vals[s, rows(c + 1), :])
            value = pltpu.roll(value, turn, 1)
            spot = jnp.where(lane[:1] >= off, spots[s, pl.ds(c, 1), :], spots[s, pl.ds(c + 1, 1), :])
            spot = pltpu.roll(jnp.broadcast_to(spot, (8, LANES)), turn, 1)
            fresh = (lane >= put) & (lane < put + size)
            held = jnp.where(fresh, value, held)
            held_spot = jnp.where(fresh, spot, held_spot)
            at = rows(2 * pair + (end >> 7))
            queue[at, :] = held
            queue_spot[at, :] = held_spot
            over = put + size - LANES
            late = lane < over
            held = jnp.where(over >= 0, jnp.where(late, value, 0.0), held)
            held_spot = jnp.where(over >= 0, jnp.where(late, spot, 0.0), held_spot)
            end = end + size
        at = 2 * pair + (end >> 7)
        queue[rows(at), :] = held
        queue_spot[rows(at), :] = held_spot
        queue[rows(at + 1), :] = nothing
        queue_spot[rows(at + 1), :] = nothing
        pairs = (end + 2 * LANES - 1) >> 8

        def note(p, carry):
            level_of[pair + p] = k
            return carry

        lax.fori_loop(0, pairs, note, 0)
        return pair + pairs

    pair = lax.fori_loop(0, levels, per_level, jnp.int32(0))
    for p in range(UNROLL):
        level_of[pair + p] = levels
        for h in range(2):
            queue[rows(2 * (pair + p) + h), :] = nothing
            queue_spot[rows(2 * (pair + p) + h), :] = nothing
    total[0] = pair


UNROLL = 4


def spread(wide, levels, base, width, first, queue, queue_spot, level_of, total, field):
    sub = iota((8, LANES), 0)
    col = first[0] + sub % 4
    reach = jnp.where(sub < 4, col, 2 * wide - col).astype(F32)
    tall = iota((HALF, LANES), 0).astype(F32).astype(BF16)
    one, zero = jnp.ones((HALF, LANES), BF16), jnp.zeros((HALF, LANES), BF16)

    def clear(k, carry):
        field[k] = jnp.zeros(field.shape[1:], F32)
        return carry

    lax.fori_loop(0, levels + 1, clear, 0)

    def group(g, carry):
        for p in range(UNROLL):
            pair = g * UNROLL + p
            k = level_of[pair]
            rate = width[base + jnp.minimum(k, levels - 1)].astype(F32)
            slope = -1.0 / jnp.full((8, LANES), rate, F32)
            lefts, rights = [], []
            for h in range(2):
                at = pl.ds(pl.multiple_of(8 * (2 * pair + h), 8), 8)
                value = queue[at, :]
                spot = queue_spot[at, :].astype(jnp.int32)
                xpos = (spot >> 9).astype(F32)
                side = ((spot >> 8) & 1).astype(F32)
                ypos = (spot & (HALF - 1)).astype(F32)
                gain = jnp.exp(jnp.abs(reach - xpos) * slope)
                gain = gain - pltpu.roll(gain, 4, 0)
                upper = jnp.concatenate([side, side], 0).astype(BF16)
                lower = jnp.concatenate([1.0 - side, 1.0 - side], 0).astype(BF16)
                tiles = []
                for x in range(NX_DEV):
                    term = value * jnp.broadcast_to(gain[x : x + 1, :], (8, LANES))
                    top = term.astype(BF16).astype(F32)
                    both = jnp.concatenate([top, term - top], 0).astype(BF16)
                    tiles += [both * lower, both * upper]
                lefts.append(jnp.concatenate(tiles, 0))
                mark = jnp.broadcast_to(ypos[:1], (HALF, LANES)).astype(BF16)
                rights.append(jnp.where(tall == mark, one, zero))
            done = nt_dot(jnp.concatenate(lefts, 1), jnp.concatenate(rights, 1))
            parts = [done[16 * i : 16 * i + 8] + done[16 * i + 8 : 16 * i + 16] for i in range(2 * NX_DEV)]
            field[k] = field[k] + jnp.concatenate(parts, 0)
        return carry

    lax.fori_loop(0, (total[0] + UNROLL - 1) // UNROLL, group, 0)


def filter_levels(levels, base, width, high, low, field, slab):
    lane = iota((8, LANES), 1)
    line = lane.astype(F32)

    def one_level(k):
        slope = -1.0 / jnp.full((8, LANES), width[base + k].astype(F32), F32)
        grid = field[k]
        blocks = []
        for i in range(2 * NX_DEV):
            blocks += [grid[8 * i : 8 * i + 8, :LANES], grid[8 * i : 8 * i + 8, LANES:]]
        grid = jnp.concatenate(blocks, 0)
        top = grid.astype(BF16)
        rest = (grid - top.astype(F32)).astype(BF16)
        mat = high[k]
        done = nn_dot(jnp.concatenate([top, rest], 1), jnp.concatenate([mat, mat], 0)) + nn_dot(top, low[k])
        rise = jnp.exp(line * slope)
        fall = jnp.exp((LANES - 1.0 - line) * slope)
        edge = jnp.exp((LANES - line) * slope)
        hop = jnp.exp(LANES * slope)
        for x in range(NX_DEV):
            ahead, behind, here = [], [], []
            for b in range(4):
                row = (4 * x + b) * 8
                here.append(done[row : row + 8, :LANES])
                moments = done[row : row + 8, LANES:]
                turned = pltpu.roll(moments, LANES // 2, 1)
                ahead.append(jnp.where(lane < LANES // 2, moments, turned))
                behind.append(jnp.where(lane < LANES // 2, turned, moments))
            run = ahead[0]
            for b in range(1, 4):
                here[b] = here[b] + rise * run
                run = ahead[b] + hop * run
            bound = edge * run
            run = behind[3]
            for b in (2, 1, 0):
                here[b] = here[b] + fall * run
                run = behind[b] + hop * run
            for b in (3, 2, 1, 0):
                slab[4 * x + b, pl.ds(pl.multiple_of(8 * k, 8), 8), :] = here[b] - bound
                bound = bound * hop

    def group(g, carry):
        for p in range(2):
            one_level(2 * g + p)
        return carry

    lax.fori_loop(0, levels // 2, group, 0)


def field_kernel(sources, wide, nvar, width, first, start, *refs):
    own, oth, marks = refs[:sources], refs[sources : 2 * sources], refs[2 * sources : 3 * sources]
    high, low, slab, vals, spots, queue, queue_spot, level_of, total, field = refs[3 * sources :]
    chunks = (own[0].shape[0] - 8) // (nvar + 1)
    levels = high.shape[0]
    base = start[0]
    gather_levels(
        sources, nvar, chunks, base, levels, own, oth, marks, vals, spots, queue, queue_spot, level_of, total
    )
    spread(wide, levels, base, width, first, queue, queue_spot, level_of, total, field)
    filter_levels(levels, base, width, high, low, field, slab)


def make_field(own, oth, band_width, first, base, high, low, nvar, levels, wide):
    sources = len(own)
    rows = own[0].shape[0]
    chunks = (rows - 8) // (nvar + 1)
    whole = pl.BlockSpec(memory_space=pltpu.VMEM)
    marks = pl.BlockSpec((8, LANES), lambda i: (rows // 8 - 1, 0), memory_space=pltpu.SMEM)
    smem = pl.BlockSpec(memory_space=pltpu.SMEM)
    pairs = levels * sources // 2 + UNROLL + 1
    return pl.pallas_call(
        functools.partial(field_kernel, sources, wide, nvar),
        grid=(1,),
        in_specs=[smem] * 3 + [whole] * (2 * sources) + [marks] * sources + [whole] * 2,
        out_specs=whole,
        out_shape=jax.ShapeDtypeStruct((4 * NX_DEV, 2 * nvar * levels, LANES), F32),
        scratch_shapes=[
            pltpu.VMEM((sources, 8 * chunks + 8, LANES), F32),
            pltpu.VMEM((sources, chunks + 8, LANES), F32),
            pltpu.VMEM((16 * pairs, LANES), F32),
            pltpu.VMEM((16 * pairs, LANES), F32),
            pltpu.SMEM((pairs,), jnp.int32),
            pltpu.SMEM((1,), jnp.int32),
            pltpu.VMEM((levels + 1, 16 * NX_DEV, HALF), F32),
        ],
        compiler_params=pltpu.CompilerParams(vmem_limit_bytes=48 << 20),
        name="field",
    )(band_width, first, base, *own, *oth, *own, high, low)


def mix_kernel(own, oth, own_high, own_low, oth_high, oth_low, out):
    for x in range(NX_DEV):
        for h in range(2):
            total = None
            for slab, high, low in ((own, own_high, own_low), (oth, oth_high, oth_low)):
                part = jnp.concatenate([slab[4 * x + 2 * h], slab[4 * x + 2 * h + 1]], 1)
                top = part.astype(BF16)
                rest = (part - top.astype(F32)).astype(BF16)
                term = nn_dot(high[...], top) + nn_dot(high[...], rest) + nn_dot(low[...], top)
                total = term if total is None else total + term
            for g in range(2):
                rows = pl.ds(8 * h + 4 * g + x, total.shape[0], stride=4 * NX_DEV)
                out[rows, :] = total[:, g * LANES : (g + 1) * LANES]


def mix(own, oth, own_mats, oth_mats):
    rows = own_mats[0].shape[0]
    return pl.pallas_call(
        mix_kernel,
        out_shape=jax.ShapeDtypeStruct((rows * NX_DEV * NY // LANES, LANES), F32),
        compiler_params=pltpu.CompilerParams(vmem_limit_bytes=32 << 20),
        name="mix",
    )(own, oth, *own_mats, *oth_mats)


def on_device(innovations, obs_owner, obs_local, obs_level, band_width, vert_scale, sigma, balance):
    groups = lax.axis_size("sub")
    nvar, _ = innovations.shape
    levels = band_width.shape[0]
    swap = [(0, 1), (1, 0)]
    unit = route(innovations, obs_owner, obs_level, obs_local, levels)
    own = [unit]
    for k in range(2, groups, 2):
        own.append(lax.ppermute(unit, "sub", [(i, (i + k) % groups) for i in range(groups)]))
    own += [lax.ppermute(held, "sub", [(i, i ^ 1) for i in range(groups)]) for held in own]
    oth = [lax.ppermute(held, "var", swap) for held in own]
    side = lax.axis_index("var").astype(jnp.int32)
    half = levels // 2
    base, last = half * side, half * (1 - side)
    theirs = lax.ppermute(vert_scale, "var", swap)
    weights = jnp.where(side == 0, balance, jnp.roll(balance, nvar, 1))
    own_mats = mix_matrix(jnp.concatenate([vert_scale, theirs], 0), sigma, weights, base, half)
    oth_mats = mix_matrix(jnp.concatenate([theirs, vert_scale], 0), sigma, jnp.roll(weights, nvar, 1), last, half)
    first = (lax.axis_index("sub") * NX_DEV).astype(jnp.int32).reshape(1)
    base = base.reshape(1)
    high, low = tables(band_width, base, half)
    slab = make_field(own, oth, band_width, first, base, high, low, nvar, half, NX_DEV * groups)
    out = mix(slab, lax.ppermute(slab, "var", swap), own_mats, oth_mats)
    out = out.reshape(nvar, levels, NY // LANES, NX_DEV, LANES)
    return jnp.swapaxes(out, 2, 3).reshape(nvar, levels, NX_DEV, NY)


def solution(mesh):
    in_specs = (
        P("var", ("member", "sub")),
        P(("member", "sub"), None),
        P(("member", "sub")),
        P(("member", "sub"), None),
        P(),
        P("var", None),
        P("var", None),
        P("var", None),
    )
    out_specs = P("var", None, ("member", "sub"), None)
    return jax.shard_map(on_device, mesh=mesh, in_specs=in_specs, out_specs=out_specs, check_vma=False)
```

```python
import functools

import jax
import jax.numpy as jnp
from jax import lax
from jax.experimental import pallas as pl
from jax.experimental.pallas import tpu as pltpu
from jax.sharding import PartitionSpec as P

VB = 6
NX_DEV = 4
NY = 512
LANES = 128
HALF = 256
F32 = jnp.float32
BF16 = jnp.bfloat16


def nt_dot(a, b):
    return lax.dot_general(a, b, (((1,), (1,)), ((), ())), preferred_element_type=F32)


def nn_dot(a, b):
    return jnp.dot(a, b, preferred_element_type=F32)


def iota(shape, dim):
    return lax.broadcasted_iota(jnp.int32, shape, dim)


def route_kernel(inn_ref, level_ref, owner_ref, local_ref, pay, inn, level, owner, local, sems, hot, pre, dest, left, right):
    pairs = ((level_ref, level), (inn_ref, inn), (owner_ref, owner), (local_ref, local))
    copies = [pltpu.make_async_copy(src, dst, sems.at[k]) for k, (src, dst) in enumerate(pairs)]
    for copy in copies:
        copy.start()
    for copy in copies:
        copy.wait()
    nvar, nobs = inn.shape
    chunks = nobs // LANES
    levels = hot.shape[0] // chunks
    rows = iota((levels, LANES), 0)
    for c in range(chunks):
        hit = jnp.where(rows == level[c : c + 1, :], 1.0, 0.0)
        hot[c * levels : (c + 1) * levels, :] = hit.astype(BF16)
    before = iota((LANES, 2 * LANES), 0) < iota((LANES, 2 * LANES), 1)
    pre[...] = nn_dot(hot[...], jnp.where(before, 1.0, 0.0).astype(BF16))
    count = jnp.zeros((levels, LANES), F32)
    for c in range(chunks):
        count = count + pre[c * levels : (c + 1) * levels, LANES:]
    lower = iota((levels, levels), 1) < iota((levels, levels), 0)
    base = nn_dot(jnp.where(lower, 1.0, 0.0).astype(BF16), count.astype(BF16))
    lane = iota((levels, LANES), 1)
    starts = jnp.sum(jnp.where(lane == rows, base, 0.0), 0, keepdims=True)
    starts = jnp.where(iota((8, LANES), 1) < levels, starts, float(nobs))
    for c in range(chunks):
        part = pre[c * levels : (c + 1) * levels, :]
        slot = jnp.where(rows == level[c : c + 1, :], part[:, :LANES] + base, 0.0)
        dest[c : c + 1, :] = jnp.sum(slot, 0, keepdims=True).astype(jnp.int32)
        base = base + part[:, LANES:]
    place = owner[...] * (NX_DEV * NY) + local[...]
    rows_hi, rows_lo = iota((chunks, LANES), 0), iota((LANES, LANES), 0)
    for c in range(chunks):
        at = slice(c * LANES, (c + 1) * LANES)
        slot = dest[c : c + 1, :]
        mask = rows_hi == slot // LANES
        right[:, at] = jnp.where(rows_lo == slot % LANES, 1.0, 0.0).astype(BF16)
        pieces = []
        for v in range(nvar):
            value = inn[v : v + 1, at]
            high = value.astype(BF16).astype(F32)
            pieces += [high, value - high]
        spot = place[c : c + 1, :]
        pieces += [(spot // HALF).astype(F32), (spot % HALF).astype(F32)]
        for q, piece in enumerate(pieces):
            left[q * chunks : (q + 1) * chunks, at] = jnp.where(mask, piece, 0.0).astype(BF16)
    packed = nt_dot(left[...], right[...])
    for v in range(nvar):
        both = packed[2 * v * chunks : (2 * v + 1) * chunks] + packed[(2 * v + 1) * chunks : (2 * v + 2) * chunks]
        pay[pl.ds(v, chunks, stride=nvar), :] = both
    high, low = packed[2 * nvar * chunks : (2 * nvar + 1) * chunks], packed[(2 * nvar + 1) * chunks :]
    pay[nvar * chunks : (nvar + 1) * chunks, :] = high * float(HALF) + low
    pay[(nvar + 1) * chunks :, :] = starts


def route(innovations, owner, level, local, levels):
    nvar, nobs = innovations.shape
    chunks = nobs // LANES
    pieces = 2 * nvar + 2
    return pl.pallas_call(
        route_kernel,
        out_shape=jax.ShapeDtypeStruct(((nvar + 1) * chunks + 8, LANES), F32),
        in_specs=[pl.BlockSpec(memory_space=pltpu.HBM)] * 4,
        scratch_shapes=[
            pltpu.VMEM((nvar, nobs), F32),
            pltpu.VMEM((chunks, LANES), jnp.int32),
            pltpu.VMEM((chunks, LANES), jnp.int32),
            pltpu.VMEM((chunks, LANES), jnp.int32),
            pltpu.SemaphoreType.DMA((4,)),
            pltpu.VMEM((chunks * levels, LANES), BF16),
            pltpu.VMEM((chunks * levels, 2 * LANES), F32),
            pltpu.VMEM((chunks, LANES), jnp.int32),
            pltpu.VMEM((pieces * chunks, nobs), BF16),
            pltpu.VMEM((LANES, nobs), BF16),
        ],
        compiler_params=pltpu.CompilerParams(vmem_limit_bytes=60 << 20),
        name="route",
    )(innovations, level.reshape(chunks, LANES), owner.reshape(chunks, LANES), local.reshape(chunks, LANES))


def table_kernel(width, base, high, low):
    depth = high.shape[0]
    row, col = iota((LANES, LANES), 0), iota((LANES, LANES), 1)
    near = jnp.abs(row - col).astype(F32)
    far = jnp.where(col < LANES // 2, LANES - row, row + 1).astype(F32)
    for k in range(depth):
        rate = width[base[0] + pl.program_id(0) * depth + k].astype(F32)
        for at, dist in ((0, near), (LANES, far)):
            full = jnp.exp(-dist / rate)
            top = full.astype(BF16)
            high[k, :, at : at + LANES] = top
            low[k, :, at : at + LANES] = (full - top.astype(F32)).astype(BF16)


def tables(band_width, base, levels):
    depth = 8
    spec = pl.BlockSpec((depth, LANES, 2 * LANES), lambda i: (i, 0, 0))
    shape = jax.ShapeDtypeStruct((levels, LANES, 2 * LANES), BF16)
    return pl.pallas_call(
        table_kernel,
        grid=(levels // depth,),
        in_specs=[pl.BlockSpec(memory_space=pltpu.SMEM)] * 2,
        out_specs=(spec, spec),
        out_shape=(shape, shape),
        cost_estimate=pl.CostEstimate(flops=1 << 24, bytes_accessed=8 << 20, transcendentals=1 << 20),
        name="tables",
    )(band_width, base)


def mix_matrix(scale, sigma, weights, base, depth):
    nvar, levels = scale.shape
    level = base + jnp.arange(depth)
    dist = jnp.arange(levels)[:, None] - jnp.repeat(level, nvar)[None, :]
    own = jnp.tile(scale.T, (1, depth))
    other = lax.dynamic_slice_in_dim(scale, base, depth, 1).T.reshape(1, -1)
    gap = dist.astype(F32)
    corr = jnp.exp(-gap * gap / (2.0 * own * other))
    corr = jnp.where(jnp.abs(dist) <= VB, corr, F32(0.0))
    mix = sigma[:, :, None] * jnp.tile(weights, (1, depth))[:, None, :] * corr[None]
    mix = mix.reshape(-1, depth * nvar)
    high = lax.reduce_precision(mix, 8, 7)
    return high.astype(BF16), (mix - high).astype(BF16)


def gather_levels(sources, nvar, chunks, base, levels, own, oth, marks, vals, spots, queue, queue_spot, level_of, total):
    lane = iota((8, LANES), 1)
    sub = iota((8, LANES), 0)
    for s in range(sources):
        for c in range(0, chunks, 2):
            here, there = own[s, 4 * c : 4 * c + 8, :], oth[s, 4 * c : 4 * c + 8, :]
            vals[s, 8 * c : 8 * c + 8, :] = jnp.where(sub < 4, here, pltpu.roll(there, 4, 0))
            vals[s, 8 * c + 8 : 8 * c + 16, :] = jnp.where(sub < 4, pltpu.roll(here, 4, 0), there)
        vals[s, 8 * chunks :, :] = jnp.zeros((8, LANES), F32)
        spots[s, :chunks, :] = own[s, nvar * chunks : (nvar + 1) * chunks, :]
        spots[s, chunks:, :] = jnp.zeros((8, LANES), F32)
    nothing = jnp.zeros((8, LANES), F32)

    def rows(chunk):
        return pl.ds(pl.multiple_of(8 * chunk, 8), 8)

    def per_level(k, pair):
        lev = base + k
        held, held_spot = nothing, nothing
        end = jnp.int32(0)
        for s in range(sources):
            start = marks[s][0, lev].astype(jnp.int32)
            size = marks[s][0, lev + 1].astype(jnp.int32) - start
            c, off = jnp.minimum(start >> 7, chunks - 1), start & (LANES - 1)
            put = end & (LANES - 1)
            turn = (put - off) & (LANES - 1)
            value = jnp.where(lane >= off, vals[s, rows(c), :], vals[s, rows(c + 1), :])
            value = pltpu.roll(value, turn, 1)
            spot = jnp.where(lane[:1] >= off, spots[s, pl.ds(c, 1), :], spots[s, pl.ds(c + 1, 1), :])
            spot = pltpu.roll(jnp.broadcast_to(spot, (8, LANES)), turn, 1)
            fresh = (lane >= put) & (lane < put + size)
            held = jnp.where(fresh, value, held)
            held_spot = jnp.where(fresh, spot, held_spot)
            at = rows(2 * pair + (end >> 7))
            queue[at, :] = held
            queue_spot[at, :] = held_spot
            over = put + size - LANES
            late = lane < over
            held = jnp.where(over >= 0, jnp.where(late, value, 0.0), held)
            held_spot = jnp.where(over >= 0, jnp.where(late, spot, 0.0), held_spot)
            end = end + size
        at = 2 * pair + (end >> 7)
        queue[rows(at), :] = held
        queue_spot[rows(at), :] = held_spot
        queue[rows(at + 1), :] = nothing
        queue_spot[rows(at + 1), :] = nothing
        pairs = (end + 2 * LANES - 1) >> 8

        def note(p, carry):
            level_of[pair + p] = k
            return carry

        lax.fori_loop(0, pairs, note, 0)
        return pair + pairs

    def two_levels(k, pair):
        return per_level(2 * k + 1, per_level(2 * k, pair))

    pair = lax.fori_loop(0, levels // 2, two_levels, jnp.int32(0))
    for p in range(UNROLL):
        level_of[pair + p] = levels
        for h in range(2):
            queue[rows(2 * (pair + p) + h), :] = nothing
            queue_spot[rows(2 * (pair + p) + h), :] = nothing
    total[0] = pair


UNROLL = 8


def spread(wide, levels, base, width, first, queue, queue_spot, level_of, total, field):
    sub = iota((8, LANES), 0)
    col = first[0] + sub % 4
    reach = jnp.where(sub < 4, col, 2 * wide - col).astype(F32)
    tall = iota((HALF, LANES), 0).astype(F32).astype(BF16)
    one, zero = jnp.ones((HALF, LANES), BF16), jnp.zeros((HALF, LANES), BF16)

    def clear(k, carry):
        field[k] = jnp.zeros(field.shape[1:], F32)
        return carry

    lax.fori_loop(0, levels + 1, clear, 0)

    def group(g, carry):
        for p in range(UNROLL):
            pair = g * UNROLL + p
            k = level_of[pair]
            rate = width[base + jnp.minimum(k, levels - 1)].astype(F32)
            slope = -1.0 / jnp.full((8, LANES), rate, F32)
            lefts, rights = [], []
            for h in range(2):
                at = pl.ds(pl.multiple_of(8 * (2 * pair + h), 8), 8)
                value = queue[at, :]
                spot = queue_spot[at, :].astype(jnp.int32)
                xpos = (spot >> 9).astype(F32)
                side = ((spot >> 8) & 1).astype(F32)
                ypos = (spot & (HALF - 1)).astype(F32)
                gain = jnp.exp(jnp.abs(reach - xpos) * slope)
                gain = gain - pltpu.roll(gain, 4, 0)
                upper = jnp.concatenate([side, side], 0).astype(BF16)
                lower = jnp.concatenate([1.0 - side, 1.0 - side], 0).astype(BF16)
                tiles = []
                for x in range(NX_DEV):
                    term = value * jnp.broadcast_to(gain[x : x + 1, :], (8, LANES))
                    top = term.astype(BF16).astype(F32)
                    both = jnp.concatenate([top, term - top], 0).astype(BF16)
                    tiles += [both * lower, both * upper]
                lefts.append(jnp.concatenate(tiles, 0))
                mark = jnp.broadcast_to(ypos[:1], (HALF, LANES)).astype(BF16)
                rights.append(jnp.where(tall == mark, one, zero))
            done = nt_dot(jnp.concatenate(lefts, 1), jnp.concatenate(rights, 1))
            parts = [done[16 * i : 16 * i + 8] + done[16 * i + 8 : 16 * i + 16] for i in range(2 * NX_DEV)]
            field[k] = field[k] + jnp.concatenate(parts, 0)
        return carry

    lax.fori_loop(0, (total[0] + UNROLL - 1) // UNROLL, group, 0)


def filter_levels(levels, base, width, high, low, field, slab):
    lane = iota((8, LANES), 1)
    line = lane.astype(F32)

    def one_level(k):
        slope = -1.0 / jnp.full((8, LANES), width[base + k].astype(F32), F32)
        grid = field[k]
        blocks = []
        for i in range(2 * NX_DEV):
            blocks += [grid[8 * i : 8 * i + 8, :LANES], grid[8 * i : 8 * i + 8, LANES:]]
        grid = jnp.concatenate(blocks, 0)
        top = grid.astype(BF16)
        rest = (grid - top.astype(F32)).astype(BF16)
        mat = high[k]
        done = nn_dot(jnp.concatenate([top, rest], 1), jnp.concatenate([mat, mat], 0)) + nn_dot(top, low[k])
        rise = jnp.exp(line * slope)
        fall = jnp.exp((LANES - 1.0 - line) * slope)
        edge = jnp.exp((LANES - line) * slope)
        hop = jnp.exp(LANES * slope)
        for x in range(NX_DEV):
            ahead, behind, here = [], [], []
            for b in range(4):
                row = (4 * x + b) * 8
                here.append(done[row : row + 8, :LANES])
                moments = done[row : row + 8, LANES:]
                turned = pltpu.roll(moments, LANES // 2, 1)
                ahead.append(jnp.where(lane < LANES // 2, moments, turned))
                behind.append(jnp.where(lane < LANES // 2, turned, moments))
            run = ahead[0]
            for b in range(1, 4):
                here[b] = here[b] + rise * run
                run = ahead[b] + hop * run
            bound = edge * run
            run = behind[3]
            for b in (2, 1, 0):
                here[b] = here[b] + fall * run
                run = behind[b] + hop * run
            for b in (3, 2, 1, 0):
                slab[4 * x + b, pl.ds(pl.multiple_of(8 * k, 8), 8), :] = here[b] - bound
                bound = bound * hop

    def group(g, carry):
        for p in range(4):
            one_level(4 * g + p)
        return carry

    lax.fori_loop(0, levels // 4, group, 0)


def field_kernel(sources, wide, nvar, width, first, start, *refs):
    own, oth, *marks = refs[: 2 + sources]
    far_high, far_low, slab, high, low, sems, vals, spots, queue, queue_spot, level_of, total, field = refs[2 + sources :]
    chunks = (own.shape[1] - 8) // (nvar + 1)
    levels = high.shape[0]
    copies = [pltpu.make_async_copy(far_high, high, sems.at[0]), pltpu.make_async_copy(far_low, low, sems.at[1])]
    for copy in copies:
        copy.start()
    base = start[0]
    gather_levels(
        sources, nvar, chunks, base, levels, own, oth, marks, vals, spots, queue, queue_spot, level_of, total
    )
    spread(wide, levels, base, width, first, queue, queue_spot, level_of, total, field)
    for copy in copies:
        copy.wait()
    filter_levels(levels, base, width, high, low, field, slab)


def make_field(own, oth, band_width, first, base, high, low, nvar, levels, wide):
    sources, rows, _ = own.shape
    chunks = (rows - 8) // (nvar + 1)
    whole = pl.BlockSpec(memory_space=pltpu.VMEM)
    marks = [
        pl.BlockSpec((None, 8, LANES), functools.partial(lambda s, i: (s, rows // 8 - 1, 0), s), memory_space=pltpu.SMEM)
        for s in range(sources)
    ]
    smem = pl.BlockSpec(memory_space=pltpu.SMEM)
    pairs = levels * sources // 2 + UNROLL + 1
    return pl.pallas_call(
        functools.partial(field_kernel, sources, wide, nvar),
        grid=(1,),
        in_specs=[smem] * 3 + [whole] * 2 + marks + [pl.BlockSpec(memory_space=pltpu.HBM)] * 2,
        out_specs=whole,
        out_shape=jax.ShapeDtypeStruct((4 * NX_DEV, 2 * nvar * levels, LANES), F32),
        scratch_shapes=[
            pltpu.VMEM(high.shape, BF16),
            pltpu.VMEM(low.shape, BF16),
            pltpu.SemaphoreType.DMA((2,)),
            pltpu.VMEM((sources, 8 * chunks + 8, LANES), F32),
            pltpu.VMEM((sources, chunks + 8, LANES), F32),
            pltpu.VMEM((16 * pairs, LANES), F32),
            pltpu.VMEM((16 * pairs, LANES), F32),
            pltpu.SMEM((pairs,), jnp.int32),
            pltpu.SMEM((1,), jnp.int32),
            pltpu.VMEM((levels + 1, 16 * NX_DEV, HALF), F32),
        ],
        compiler_params=pltpu.CompilerParams(vmem_limit_bytes=56 << 20),
        name="field",
    )(band_width, first, base, own, oth, *([own] * sources), high, low)


def mix_kernel(slab, high, low, *refs):
    out = refs[-1]
    x = pl.program_id(0)
    for h in range(2):
        part = jnp.concatenate([slab[2 * h], slab[2 * h + 1]], 1)
        top = part.astype(BF16)
        rest = (part - top.astype(F32)).astype(BF16)
        term = nn_dot(high[...], top) + nn_dot(high[...], rest) + nn_dot(low[...], top)
        if len(refs) == 1:
            out[0, :, h * HALF : (h + 1) * HALF] = term
        else:
            term = term + refs[0][0, :, h * HALF : (h + 1) * HALF]
            for g in range(2):
                rows = pl.ds(8 * h + 4 * g + x, term.shape[0], stride=4 * NX_DEV)
                out[rows, :] = term[:, g * LANES : (g + 1) * LANES]


def mix(slab, mats, *before):
    rows, depth = mats[0].shape
    strip = pl.BlockSpec((4, depth, LANES), lambda i: (i, 0, 0))
    matrix = pl.BlockSpec((rows, depth), lambda i: (0, 0))
    partial = pl.BlockSpec((1, rows, NY), lambda i: (i, 0, 0))
    if before:
        shape = (rows * NX_DEV * NY // LANES, LANES)
        out_spec = pl.BlockSpec(shape, lambda i: (0, 0))
    else:
        shape = (NX_DEV, rows, NY)
        out_spec = partial
    return pl.pallas_call(
        mix_kernel,
        grid=(NX_DEV,),
        in_specs=[strip, matrix, matrix] + [partial] * len(before),
        out_specs=out_spec,
        out_shape=jax.ShapeDtypeStruct(shape, F32),
        compiler_params=pltpu.CompilerParams(vmem_limit_bytes=32 << 20),
        cost_estimate=pl.CostEstimate(flops=1 << 30, bytes_accessed=6 << 20, transcendentals=0),
        name="mix",
    )(slab, *mats, *before)


def on_device(innovations, obs_owner, obs_local, obs_level, band_width, vert_scale, sigma, balance):
    groups = lax.axis_size("sub")
    nvar, _ = innovations.shape
    levels = band_width.shape[0]
    swap = [(0, 1), (1, 0)]
    unit = route(innovations, obs_owner, obs_level, obs_local, levels)
    side = lax.axis_index("var").astype(jnp.int32)
    half = levels // 2
    base, last = half * side, half * (1 - side)
    theirs = lax.ppermute(vert_scale, "var", swap)
    weights = jnp.where(side == 0, balance, jnp.roll(balance, nvar, 1))
    own_mats = mix_matrix(jnp.concatenate([vert_scale, theirs], 0), sigma, weights, base, half)
    oth_mats = mix_matrix(jnp.concatenate([theirs, vert_scale], 0), sigma, jnp.roll(weights, nvar, 1), last, half)
    first = (lax.axis_index("sub") * NX_DEV).astype(jnp.int32).reshape(1)
    base = base.reshape(1)
    high, low = tables(band_width, base, half)
    own = [unit]
    for k in range(2, groups, 2):
        own.append(lax.ppermute(unit, "sub", [(i, (i + k) % groups) for i in range(groups)]))
    own[-1], high, low = lax.optimization_barrier((own[-1], high, low))
    own += [lax.ppermute(held, "sub", [(i, i ^ 1) for i in range(groups)]) for held in own]
    own[-1], own_mats, oth_mats = lax.optimization_barrier((own[-1], own_mats, oth_mats))
    own = jnp.stack(own)
    oth = lax.ppermute(own, "var", swap)
    slab = make_field(own, oth, band_width, first, base, high, low, nvar, half, NX_DEV * groups)
    swapped = lax.ppermute(slab, "var", swap)
    out = mix(swapped, oth_mats, mix(slab, own_mats))
    out = out.reshape(nvar, levels, NY // LANES, NX_DEV, LANES)
    return jnp.swapaxes(out, 2, 3).reshape(nvar, levels, NX_DEV, NY)


def solution(mesh):
    in_specs = (
        P("var", ("member", "sub")),
        P(("member", "sub"), None),
        P(("member", "sub")),
        P(("member", "sub"), None),
        P(),
        P("var", None),
        P("var", None),
        P("var", None),
    )
    out_specs = P("var", None, ("member", "sub"), None)
    return jax.shard_map(on_device, mesh=mesh, in_specs=in_specs, out_specs=out_specs, check_vma=False)
```

```python
import functools

import jax
import jax.numpy as jnp
from jax import lax
from jax.experimental import pallas as pl
from jax.experimental.pallas import tpu as pltpu
from jax.sharding import PartitionSpec as P

VB = 6
NX_DEV = 4
NY = 512
LANES = 128
HALF = 256
F32 = jnp.float32
BF16 = jnp.bfloat16


def nt_dot(a, b):
    return lax.dot_general(a, b, (((1,), (1,)), ((), ())), preferred_element_type=F32)


def nn_dot(a, b):
    return jnp.dot(a, b, preferred_element_type=F32)


def iota(shape, dim):
    return lax.broadcasted_iota(jnp.int32, shape, dim)


def route_kernel(inn_ref, level_ref, owner_ref, local_ref, pay, inn, level, owner, local, sems, hot, pre, dest, left, right):
    pairs = ((level_ref, level), (inn_ref, inn), (owner_ref, owner), (local_ref, local))
    copies = [pltpu.make_async_copy(src, dst, sems.at[k]) for k, (src, dst) in enumerate(pairs)]
    for copy in copies:
        copy.start()
    for copy in copies:
        copy.wait()
    nvar, nobs = inn.shape
    chunks = nobs // LANES
    levels = hot.shape[0] // chunks
    rows = iota((levels, LANES), 0)
    for c in range(chunks):
        hit = jnp.where(rows == level[c : c + 1, :], 1.0, 0.0)
        hot[c * levels : (c + 1) * levels, :] = hit.astype(BF16)
    before = iota((LANES, 2 * LANES), 0) < iota((LANES, 2 * LANES), 1)
    pre[...] = nn_dot(hot[...], jnp.where(before, 1.0, 0.0).astype(BF16))
    count = jnp.zeros((levels, LANES), F32)
    for c in range(chunks):
        count = count + pre[c * levels : (c + 1) * levels, LANES:]
    lower = iota((levels, levels), 1) < iota((levels, levels), 0)
    base = nn_dot(jnp.where(lower, 1.0, 0.0).astype(BF16), count.astype(BF16))
    lane = iota((levels, LANES), 1)
    starts = jnp.sum(jnp.where(lane == rows, base, 0.0), 0, keepdims=True)
    starts = jnp.where(iota((8, LANES), 1) < levels, starts, float(nobs))
    for c in range(chunks):
        part = pre[c * levels : (c + 1) * levels, :]
        slot = jnp.where(rows == level[c : c + 1, :], part[:, :LANES] + base, 0.0)
        dest[c : c + 1, :] = jnp.sum(slot, 0, keepdims=True).astype(jnp.int32)
        base = base + part[:, LANES:]
    place = owner[...] * (NX_DEV * NY) + local[...]
    rows_hi, rows_lo = iota((chunks, LANES), 0), iota((LANES, LANES), 0)
    for c in range(chunks):
        at = slice(c * LANES, (c + 1) * LANES)
        slot = dest[c : c + 1, :]
        mask = rows_hi == slot // LANES
        right[c] = jnp.where(rows_lo == slot % LANES, 1.0, 0.0).astype(BF16)
        pieces = []
        for v in range(nvar):
            value = inn[v : v + 1, at]
            high = value.astype(BF16).astype(F32)
            pieces += [high, value - high]
        spot = place[c : c + 1, :]
        pieces += [(spot // HALF).astype(F32), (spot % HALF).astype(F32)]
        for q, piece in enumerate(pieces):
            left[c, q * chunks : (q + 1) * chunks, :] = jnp.where(mask, piece, 0.0).astype(BF16)
    packed = nt_dot(
        jnp.concatenate([left[c] for c in range(chunks)], 1),
        jnp.concatenate([right[c] for c in range(chunks)], 1),
    )
    for v in range(nvar):
        both = packed[2 * v * chunks : (2 * v + 1) * chunks] + packed[(2 * v + 1) * chunks : (2 * v + 2) * chunks]
        pay[pl.ds(v, chunks, stride=nvar), :] = both
    high, low = packed[2 * nvar * chunks : (2 * nvar + 1) * chunks], packed[(2 * nvar + 1) * chunks :]
    pay[nvar * chunks : (nvar + 1) * chunks, :] = high * float(HALF) + low
    pay[(nvar + 1) * chunks :, :] = starts


def route(innovations, owner, level, local, levels):
    nvar, nobs = innovations.shape
    chunks = nobs // LANES
    pieces = 2 * nvar + 2
    return pl.pallas_call(
        route_kernel,
        out_shape=jax.ShapeDtypeStruct(((nvar + 1) * chunks + 8, LANES), F32),
        in_specs=[pl.BlockSpec(memory_space=pltpu.HBM)] * 4,
        scratch_shapes=[
            pltpu.VMEM((nvar, nobs), F32),
            pltpu.VMEM((chunks, LANES), jnp.int32),
            pltpu.VMEM((chunks, LANES), jnp.int32),
            pltpu.VMEM((chunks, LANES), jnp.int32),
            pltpu.SemaphoreType.DMA((4,)),
            pltpu.VMEM((chunks * levels, LANES), BF16),
            pltpu.VMEM((chunks * levels, 2 * LANES), F32),
            pltpu.VMEM((chunks, LANES), jnp.int32),
            pltpu.VMEM((chunks, pieces * chunks, LANES), BF16),
            pltpu.VMEM((chunks, LANES, LANES), BF16),
        ],
        compiler_params=pltpu.CompilerParams(vmem_limit_bytes=60 << 20),
        name="route",
    )(innovations, level.reshape(chunks, LANES), owner.reshape(chunks, LANES), local.reshape(chunks, LANES))


def table_kernel(width, base, table):
    depth = table.shape[0]
    row, col = iota((LANES, LANES), 0), iota((LANES, LANES), 1)
    near = jnp.abs(row - col).astype(F32)
    far = jnp.where(col < LANES // 2, LANES - row, row + 1).astype(F32)
    for k in range(depth):
        rate = width[base[0] + pl.program_id(0) * depth + k].astype(F32)
        for at, dist in ((0, near), (LANES, far)):
            full = jnp.exp(-dist / rate)
            top = full.astype(BF16)
            table[k, :LANES, at : at + LANES] = top
            table[k, LANES:, at : at + LANES] = (full - top.astype(F32)).astype(BF16)


def tables(band_width, base, levels):
    depth = 8
    spec = pl.BlockSpec((depth, 2 * LANES, 2 * LANES), lambda i: (i, 0, 0))
    shape = jax.ShapeDtypeStruct((levels, 2 * LANES, 2 * LANES), BF16)
    return pl.pallas_call(
        table_kernel,
        grid=(levels // depth,),
        in_specs=[pl.BlockSpec(memory_space=pltpu.SMEM)] * 2,
        out_specs=spec,
        out_shape=shape,
        cost_estimate=pl.CostEstimate(flops=1 << 24, bytes_accessed=8 << 20, transcendentals=1 << 20),
        name="tables",
    )(band_width, base)


def mix_matrix(scale, sigma, weights, base, depth):
    nvar, levels = scale.shape
    level = base + jnp.arange(depth)
    dist = jnp.arange(levels)[:, None] - jnp.repeat(level, nvar)[None, :]
    own = jnp.tile(scale.T, (1, depth))
    other = lax.dynamic_slice_in_dim(scale, base, depth, 1).T.reshape(1, -1)
    gap = dist.astype(F32)
    corr = jnp.exp(-gap * gap / (2.0 * own * other))
    corr = jnp.where(jnp.abs(dist) <= VB, corr, F32(0.0))
    mix = sigma[:, :, None] * jnp.tile(weights, (1, depth))[:, None, :] * corr[None]
    mix = mix.reshape(-1, depth * nvar)
    high = lax.reduce_precision(mix, 8, 7)
    return high.astype(BF16), (mix - high).astype(BF16)


CUES = 8


def make_cues(sources, starts_row, chunks, base, levels, own, cue):
    end = jnp.zeros((1, LANES), jnp.int32)
    for s in range(sources):
        start = own[s, starts_row : starts_row + 1, :]
        size = (pltpu.roll(start, LANES - 1, 1) - start).astype(jnp.int32)
        start = start.astype(jnp.int32)
        off, put = start & (LANES - 1), end & (LANES - 1)
        row = 8 * jnp.minimum(start >> 7, chunks - 1)
        for j, item in enumerate((row, off, put, put + size, (put - off) & (LANES - 1), 8 * (end >> 7))):
            cue[CUES * s + j : CUES * s + j + 1, :] = item
        end = end + size
    lane = iota((1, LANES), 1)
    pairs = jnp.where((lane >= base) & (lane < base + levels), (end + 2 * LANES - 1) >> 8, 0).astype(F32)
    earlier = jnp.where(iota((LANES, LANES), 0) < iota((LANES, LANES), 1), 1.0, 0.0).astype(BF16)
    before = nn_dot(jnp.broadcast_to(pairs, (8, LANES)).astype(BF16), earlier)[:1]
    count = jnp.sum(pairs, 1, keepdims=True)
    last = CUES * sources
    cue[last : last + 1, :] = before.astype(jnp.int32)
    cue[last + 1 : last + 2, :] = 8 * (end >> 7)
    cue[last + 2 : last + 3, :] = jnp.broadcast_to(count, (1, LANES)).astype(jnp.int32)


def gather_levels(sources, nvar, chunks, base, levels, own, oth, cue, scalar_cue, sem, vals, spots, queue, queue_spot, level_of):
    lane = iota((8, LANES), 1)
    sub = iota((8, LANES), 0)
    make_cues(sources, (nvar + 1) * chunks, chunks, base, levels, own, cue)
    copy = pltpu.make_async_copy(cue, scalar_cue, sem)
    copy.start()
    for s in range(sources):
        for c in range(0, chunks, 2):
            here, there = own[s, 4 * c : 4 * c + 8, :], oth[s, 4 * c : 4 * c + 8, :]
            vals[s, 8 * c : 8 * c + 8, :] = jnp.where(sub < 4, here, pltpu.roll(there, 4, 0))
            vals[s, 8 * c + 8 : 8 * c + 16, :] = jnp.where(sub < 4, pltpu.roll(here, 4, 0), there)
        vals[s, 8 * chunks :, :] = jnp.zeros((8, LANES), F32)
        for c in range(chunks):
            spot = own[s, nvar * chunks + c : nvar * chunks + c + 1, :]
            spots[s, 8 * c : 8 * c + 8, :] = jnp.broadcast_to(spot, (8, LANES))
        spots[s, 8 * chunks :, :] = jnp.zeros((8, LANES), F32)
    copy.wait()
    nothing = jnp.zeros((8, LANES), F32)
    last = CUES * sources

    def rows(start):
        return pl.ds(pl.multiple_of(start, 8), 8)

    def per_level(k):
        lev = base + k
        held, held_spot = nothing, nothing
        pair = scalar_cue[last, lev]
        for s in range(sources):
            row, off, put, stop, turn, at = (scalar_cue[CUES * s + j, lev] for j in range(6))
            first = lane >= off
            value = jnp.where(first, vals[s, rows(row), :], vals[s, rows(row + 8), :])
            value = pltpu.roll(value, turn, 1)
            spot = jnp.where(first, spots[s, rows(row), :], spots[s, rows(row + 8), :])
            spot = pltpu.roll(spot, turn, 1)
            fresh = (lane >= put) & (lane < stop)
            held = jnp.where(fresh, value, held)
            held_spot = jnp.where(fresh, spot, held_spot)
            queue[rows(16 * pair + at), :] = held
            queue_spot[rows(16 * pair + at), :] = held_spot
            late = lane < stop - LANES
            over = jnp.broadcast_to(stop, (8, LANES)) >= LANES
            held = jnp.where(over, jnp.where(late, value, 0.0), held)
            held_spot = jnp.where(over, jnp.where(late, spot, 0.0), held_spot)
        at = 16 * pair + scalar_cue[last + 1, lev]
        queue[rows(at), :] = held
        queue_spot[rows(at), :] = held_spot
        queue[rows(at + 8), :] = nothing
        queue_spot[rows(at + 8), :] = nothing
        for p in range(sources // 2):
            level_of[pair + p] = k

    def group(g, carry):
        for p in range(2):
            per_level(2 * g + p)
        return carry

    lax.fori_loop(0, levels // 2, group, 0)
    pair = scalar_cue[last + 2, 0]
    for p in range(UNROLL):
        level_of[pair + p] = levels
        for h in range(2):
            queue[rows(16 * (pair + p) + 8 * h), :] = nothing
            queue_spot[rows(16 * (pair + p) + 8 * h), :] = nothing
    return pair


UNROLL = 8


def spread(wide, levels, base, width, first, queue, queue_spot, level_of, count, field):
    sub = iota((8, LANES), 0)
    col = first[0] + sub % 4
    reach = jnp.where(sub < 4, col, 2 * wide - col).astype(F32)
    tall = iota((HALF, LANES), 0).astype(F32).astype(BF16)
    one, zero = jnp.ones((HALF, LANES), BF16), jnp.zeros((HALF, LANES), BF16)

    def clear(k, carry):
        field[k] = jnp.zeros(field.shape[1:], F32)
        return carry

    lax.fori_loop(0, levels + 1, clear, 0)

    def group(g, carry):
        for p in range(UNROLL):
            pair = g * UNROLL + p
            k = level_of[pair]
            rate = width[base + jnp.minimum(k, levels - 1)].astype(F32)
            slope = -1.0 / jnp.full((8, LANES), rate, F32)
            lefts, rights = [], []
            for h in range(2):
                at = pl.ds(pl.multiple_of(8 * (2 * pair + h), 8), 8)
                value = queue[at, :]
                spot = queue_spot[at, :].astype(jnp.int32)
                xpos = (spot >> 9).astype(F32)
                side = ((spot >> 8) & 1).astype(F32)
                ypos = (spot & (HALF - 1)).astype(F32)
                gain = jnp.exp(jnp.abs(reach - xpos) * slope)
                gain = gain - pltpu.roll(gain, 4, 0)
                upper = jnp.concatenate([side, side], 0).astype(BF16)
                lower = jnp.concatenate([1.0 - side, 1.0 - side], 0).astype(BF16)
                tiles = []
                for x in range(NX_DEV):
                    term = value * jnp.broadcast_to(gain[x : x + 1, :], (8, LANES))
                    top = term.astype(BF16).astype(F32)
                    both = jnp.concatenate([top, term - top], 0).astype(BF16)
                    tiles += [both * lower, both * upper]
                lefts.append(jnp.concatenate(tiles, 0))
                mark = jnp.broadcast_to(ypos[:1], (HALF, LANES)).astype(BF16)
                rights.append(jnp.where(tall == mark, one, zero))
            done = nt_dot(jnp.concatenate(lefts, 1), jnp.concatenate(rights, 1))
            parts = [done[16 * i : 16 * i + 8] + done[16 * i + 8 : 16 * i + 16] for i in range(2 * NX_DEV)]
            field[k] = field[k] + jnp.concatenate(parts, 0)
        return carry

    lax.fori_loop(0, (count + UNROLL - 1) // UNROLL, group, 0)


def filter_levels(levels, base, width, table, field, slab):
    lane = iota((8, LANES), 1)
    line = lane.astype(F32)

    def one_level(k):
        slope = -1.0 / jnp.full((8, LANES), width[base + k].astype(F32), F32)
        grid = field[k]
        blocks = []
        for i in range(2 * NX_DEV):
            blocks += [grid[8 * i : 8 * i + 8, :LANES], grid[8 * i : 8 * i + 8, LANES:]]
        grid = jnp.concatenate(blocks, 0)
        top = grid.astype(BF16)
        rest = (grid - top.astype(F32)).astype(BF16)
        mat = table[k, :LANES, :]
        done = nn_dot(jnp.concatenate([top, rest], 1), jnp.concatenate([mat, mat], 0)) + nn_dot(top, table[k, LANES:, :])
        rise = jnp.exp(line * slope)
        fall = jnp.exp((LANES - 1.0 - line) * slope)
        edge = jnp.exp((LANES - line) * slope)
        hop = jnp.exp(LANES * slope)
        for x in range(NX_DEV):
            ahead, behind, here = [], [], []
            for b in range(4):
                row = (4 * x + b) * 8
                here.append(done[row : row + 8, :LANES])
                moments = done[row : row + 8, LANES:]
                turned = pltpu.roll(moments, LANES // 2, 1)
                ahead.append(jnp.where(lane < LANES // 2, moments, turned))
                behind.append(jnp.where(lane < LANES // 2, turned, moments))
            run = ahead[0]
            for b in range(1, 4):
                here[b] = here[b] + rise * run
                run = ahead[b] + hop * run
            bound = edge * run
            run = behind[3]
            for b in (2, 1, 0):
                here[b] = here[b] + fall * run
                run = behind[b] + hop * run
            for b in (3, 2, 1, 0):
                slab[x, b, pl.ds(pl.multiple_of(8 * k, 8), 8), :] = here[b] - bound
                bound = bound * hop

    def group(g, carry):
        for p in range(4):
            one_level(4 * g + p)
        return carry

    lax.fori_loop(0, levels // 4, group, 0)


def field_kernel(sources, wide, nvar, width, first, start, own, oth, far_table, slab, *scratch):
    table, table_sem, cue, scalar_cue, sem, vals, spots, queue, queue_spot, level_of, field = scratch
    chunks = (own.shape[1] - 8) // (nvar + 1)
    levels = table.shape[0]
    base = start[0]
    fetch = pltpu.make_async_copy(far_table, table, table_sem)
    fetch.start()
    count = gather_levels(
        sources, nvar, chunks, base, levels, own, oth, cue, scalar_cue, sem, vals, spots, queue, queue_spot, level_of
    )
    spread(wide, levels, base, width, first, queue, queue_spot, level_of, count, field)
    fetch.wait()
    filter_levels(levels, base, width, table, field, slab)


def make_field(own, oth, band_width, first, base, table, nvar, levels, wide):
    sources, rows, _ = own.shape
    chunks = (rows - 8) // (nvar + 1)
    whole = pl.BlockSpec(memory_space=pltpu.VMEM)
    smem = pl.BlockSpec(memory_space=pltpu.SMEM)
    pairs = levels * sources // 2 + UNROLL + 1
    return pl.pallas_call(
        functools.partial(field_kernel, sources, wide, nvar),
        in_specs=[smem] * 3 + [whole] * 2 + [pl.BlockSpec(memory_space=pltpu.HBM)],
        out_specs=whole,
        out_shape=jax.ShapeDtypeStruct((NX_DEV, 4, 2 * nvar * levels, LANES), F32),
        scratch_shapes=[
            pltpu.VMEM(table.shape, BF16),
            pltpu.SemaphoreType.DMA,
            pltpu.VMEM((CUES * sources + 8, LANES), jnp.int32),
            pltpu.SMEM((CUES * sources + 8, LANES), jnp.int32),
            pltpu.SemaphoreType.DMA,
            pltpu.VMEM((sources, 8 * chunks + 8, LANES), F32),
            pltpu.VMEM((sources, 8 * chunks + 8, LANES), F32),
            pltpu.VMEM((16 * pairs, LANES), F32),
            pltpu.VMEM((16 * pairs, LANES), F32),
            pltpu.SMEM((pairs + sources,), jnp.int32),
            pltpu.VMEM((levels + 1, 16 * NX_DEV, HALF), F32),
        ],
        compiler_params=pltpu.CompilerParams(vmem_limit_bytes=50 << 20),
        name="field",
    )(band_width, first, base, own, oth, table)


def mix_kernel(slab, high, low, *refs):
    out = refs[-1]
    rows = high.shape[0]
    for x in range(NX_DEV):
        part = jnp.concatenate([slab[x, 0], slab[x, 1]], 1)
        top = part.astype(BF16)
        rest = (part - top.astype(F32)).astype(BF16)
        term = nn_dot(jnp.concatenate([high[...], low[...]], 0), top)
        term = term[:rows] + term[rows:] + nn_dot(high[...], rest)
        if len(refs) == 1:
            out[0, x] = term
        else:
            term = term + refs[0][0, x]
            flat = out.reshape(8 * term.shape[0], LANES)
            for g in range(2):
                flat[pl.ds(4 * g + x, term.shape[0], stride=8), :] = term[:, g * LANES : (g + 1) * LANES]


def mix(slab, mats, *before):
    rows, depth = mats[0].shape
    strip = pl.BlockSpec((NX_DEV, 2, depth, LANES), lambda i: (0, i, 0, 0))
    matrix = pl.BlockSpec((rows, depth), lambda i: (0, 0))
    partial = pl.BlockSpec((1, NX_DEV, rows, HALF), lambda i: (i, 0, 0, 0))
    if before:
        shape = (rows, 16, LANES)
        out_spec = pl.BlockSpec((rows, 8, LANES), lambda i: (0, i, 0))
    else:
        shape = (2, NX_DEV, rows, HALF)
        out_spec = partial
    return pl.pallas_call(
        mix_kernel,
        grid=(2,),
        in_specs=[strip, matrix, matrix] + [partial] * len(before),
        out_specs=out_spec,
        out_shape=jax.ShapeDtypeStruct(shape, F32),
        compiler_params=pltpu.CompilerParams(vmem_limit_bytes=16 << 20),
        cost_estimate=pl.CostEstimate(flops=1 << 30, bytes_accessed=6 << 20, transcendentals=0),
        name="mix",
    )(slab, *mats, *before)


def on_device(innovations, obs_owner, obs_local, obs_level, band_width, vert_scale, sigma, balance):
    groups = lax.axis_size("sub")
    nvar, _ = innovations.shape
    levels = band_width.shape[0]
    swap = [(0, 1), (1, 0)]
    unit = route(innovations, obs_owner, obs_level, obs_local, levels)
    side = lax.axis_index("var").astype(jnp.int32)
    half = levels // 2
    base, last = half * side, half * (1 - side)
    theirs = lax.ppermute(vert_scale, "var", swap)
    weights = jnp.where(side == 0, balance, jnp.roll(balance, nvar, 1))
    own_mats = mix_matrix(jnp.concatenate([vert_scale, theirs], 0), sigma, weights, base, half)
    oth_mats = mix_matrix(jnp.concatenate([theirs, vert_scale], 0), sigma, jnp.roll(weights, nvar, 1), last, half)
    first = (lax.axis_index("sub") * NX_DEV).astype(jnp.int32).reshape(1)
    base = base.reshape(1)
    own = [unit]
    for k in range(2, groups, 2):
        own.append(lax.ppermute(unit, "sub", [(i, (i + k) % groups) for i in range(groups)]))
    far = len(own) // 2
    own[far], own_mats, oth_mats, when = lax.optimization_barrier((own[far], own_mats, oth_mats, base))
    table = tables(band_width, when, half)
    own += [lax.ppermute(held, "sub", [(i, i ^ 1) for i in range(groups)]) for held in own]
    own[-1], table = lax.optimization_barrier((own[-1], table))
    own = jnp.stack(own)
    oth = lax.ppermute(own, "var", swap)
    slab = make_field(own, oth, band_width, first, base, table, nvar, half, NX_DEV * groups)
    swapped = lax.ppermute(slab, "var", swap)
    out = mix(swapped, oth_mats, mix(slab, own_mats))
    out = out.reshape(nvar, levels, NY // LANES, NX_DEV, LANES)
    return jnp.swapaxes(out, 2, 3).reshape(nvar, levels, NX_DEV, NY)


def solution(mesh):
    in_specs = (
        P("var", ("member", "sub")),
        P(("member", "sub"), None),
        P(("member", "sub")),
        P(("member", "sub"), None),
        P(),
        P("var", None),
        P("var", None),
        P("var", None),
    )
    out_specs = P("var", None, ("member", "sub"), None)
    return jax.shard_map(on_device, mesh=mesh, in_specs=in_specs, out_specs=out_specs, check_vma=False)
```

```python
import functools

import jax
import jax.numpy as jnp
from jax import lax
from jax.experimental import pallas as pl
from jax.experimental.pallas import tpu as pltpu
from jax.sharding import PartitionSpec as P

VB = 6
NX_DEV = 4
NY = 512
LANES = 128
HALF = 256
F32 = jnp.float32
BF16 = jnp.bfloat16


def nt_dot(a, b):
    return lax.dot_general(a, b, (((1,), (1,)), ((), ())), preferred_element_type=F32)


def nn_dot(a, b):
    return jnp.dot(a, b, preferred_element_type=F32)


def iota(shape, dim):
    return lax.broadcasted_iota(jnp.int32, shape, dim)


def route_kernel(inn_ref, level_ref, owner_ref, local_ref, pay, inn, level, owner, local, sems, hot, pre, dest, left, right):
    pairs = ((level_ref, level), (inn_ref, inn), (owner_ref, owner), (local_ref, local))
    copies = [pltpu.make_async_copy(src, dst, sems.at[k]) for k, (src, dst) in enumerate(pairs)]
    for copy in copies:
        copy.start()
    for copy in copies:
        copy.wait()
    nvar, nobs = inn.shape
    chunks = nobs // LANES
    levels = hot.shape[0] // chunks
    rows = iota((levels, LANES), 0)
    for c in range(chunks):
        hit = jnp.where(rows == level[c : c + 1, :], 1.0, 0.0)
        hot[c * levels : (c + 1) * levels, :] = hit.astype(BF16)
    before = iota((LANES, 2 * LANES), 0) < iota((LANES, 2 * LANES), 1)
    pre[...] = nn_dot(hot[...], jnp.where(before, 1.0, 0.0).astype(BF16))
    count = jnp.zeros((levels, LANES), F32)
    for c in range(chunks):
        count = count + pre[c * levels : (c + 1) * levels, LANES:]
    lower = iota((levels, levels), 1) < iota((levels, levels), 0)
    base = nn_dot(jnp.where(lower, 1.0, 0.0).astype(BF16), count.astype(BF16))
    lane = iota((levels, LANES), 1)
    starts = jnp.sum(jnp.where(lane == rows, base, 0.0), 0, keepdims=True)
    starts = jnp.where(iota((8, LANES), 1) < levels, starts, float(nobs))
    for c in range(chunks):
        part = pre[c * levels : (c + 1) * levels, :]
        slot = jnp.where(rows == level[c : c + 1, :], part[:, :LANES] + base, 0.0)
        dest[c : c + 1, :] = jnp.sum(slot, 0, keepdims=True).astype(jnp.int32)
        base = base + part[:, LANES:]
    place = owner[...] * (NX_DEV * NY) + local[...]
    rows_hi, rows_lo = iota((chunks, LANES), 0), iota((LANES, LANES), 0)
    for c in range(chunks):
        at = slice(c * LANES, (c + 1) * LANES)
        slot = dest[c : c + 1, :]
        mask = rows_hi == slot // LANES
        right[c] = jnp.where(rows_lo == slot % LANES, 1.0, 0.0).astype(BF16)
        pieces = []
        for v in range(nvar):
            value = inn[v : v + 1, at]
            high = value.astype(BF16).astype(F32)
            pieces += [high, value - high]
        spot = place[c : c + 1, :]
        pieces += [(spot // HALF).astype(F32), (spot % HALF).astype(F32)]
        for q, piece in enumerate(pieces):
            left[c, q * chunks : (q + 1) * chunks, :] = jnp.where(mask, piece, 0.0).astype(BF16)
    packed = nt_dot(
        jnp.concatenate([left[c] for c in range(chunks)], 1),
        jnp.concatenate([right[c] for c in range(chunks)], 1),
    )
    for v in range(nvar):
        both = packed[2 * v * chunks : (2 * v + 1) * chunks] + packed[(2 * v + 1) * chunks : (2 * v + 2) * chunks]
        pay[pl.ds(v, chunks, stride=nvar), :] = both
    high, low = packed[2 * nvar * chunks : (2 * nvar + 1) * chunks], packed[(2 * nvar + 1) * chunks :]
    pay[nvar * chunks : (nvar + 1) * chunks, :] = high * float(HALF) + low
    pay[(nvar + 1) * chunks :, :] = starts


def route(innovations, owner, level, local, levels):
    nvar, nobs = innovations.shape
    chunks = nobs // LANES
    pieces = 2 * nvar + 2
    return pl.pallas_call(
        route_kernel,
        out_shape=jax.ShapeDtypeStruct(((nvar + 1) * chunks + 8, LANES), F32),
        in_specs=[pl.BlockSpec(memory_space=pltpu.HBM)] * 4,
        scratch_shapes=[
            pltpu.VMEM((nvar, nobs), F32),
            pltpu.VMEM((chunks, LANES), jnp.int32),
            pltpu.VMEM((chunks, LANES), jnp.int32),
            pltpu.VMEM((chunks, LANES), jnp.int32),
            pltpu.SemaphoreType.DMA((4,)),
            pltpu.VMEM((chunks * levels, LANES), BF16),
            pltpu.VMEM((chunks * levels, 2 * LANES), F32),
            pltpu.VMEM((chunks, LANES), jnp.int32),
            pltpu.VMEM((chunks, pieces * chunks, LANES), BF16),
            pltpu.VMEM((chunks, LANES, LANES), BF16),
        ],
        compiler_params=pltpu.CompilerParams(vmem_limit_bytes=60 << 20),
        name="route",
    )(innovations, level.reshape(chunks, LANES), owner.reshape(chunks, LANES), local.reshape(chunks, LANES))


def table_kernel(width, base, table):
    depth = table.shape[0]
    row, col = iota((LANES, LANES), 0), iota((LANES, LANES), 1)
    near = jnp.abs(row - col).astype(F32)
    far = jnp.where(col < LANES // 2, LANES - row, row + 1).astype(F32)
    for k in range(depth):
        rate = width[base[0] + pl.program_id(0) * depth + k].astype(F32)
        for at, dist in ((0, near), (LANES, far)):
            full = jnp.exp(-dist / rate)
            top = full.astype(BF16)
            table[k, :LANES, at : at + LANES] = top
            table[k, LANES:, at : at + LANES] = (full - top.astype(F32)).astype(BF16)


def tables(band_width, base, levels):
    depth = 8
    spec = pl.BlockSpec((depth, 2 * LANES, 2 * LANES), lambda i: (i, 0, 0))
    shape = jax.ShapeDtypeStruct((levels, 2 * LANES, 2 * LANES), BF16)
    return pl.pallas_call(
        table_kernel,
        grid=(levels // depth,),
        in_specs=[pl.BlockSpec(memory_space=pltpu.SMEM)] * 2,
        out_specs=spec,
        out_shape=shape,
        cost_estimate=pl.CostEstimate(flops=1 << 24, bytes_accessed=8 << 20, transcendentals=1 << 20),
        name="tables",
    )(band_width, base)


def mix_matrix(scale, sigma, weights, base, depth):
    nvar, levels = scale.shape
    level = base + jnp.arange(depth)
    dist = jnp.arange(levels)[:, None] - jnp.repeat(level, nvar)[None, :]
    own = jnp.tile(scale.T, (1, depth))
    other = lax.dynamic_slice_in_dim(scale, base, depth, 1).T.reshape(1, -1)
    gap = dist.astype(F32)
    corr = jnp.exp(-gap * gap / (2.0 * own * other))
    corr = jnp.where(jnp.abs(dist) <= VB, corr, F32(0.0))
    mix = sigma[:, :, None] * jnp.tile(weights, (1, depth))[:, None, :] * corr[None]
    mix = mix.reshape(-1, depth * nvar)
    high = lax.reduce_precision(mix, 8, 7)
    return high.astype(BF16), (mix - high).astype(BF16)


CUES = 4


def make_cues(sources, starts_row, chunks, base, levels, own, cue):
    end = jnp.zeros((1, LANES), jnp.int32)
    goals = []
    for s in range(sources):
        start = own[s, starts_row : starts_row + 1, :]
        size = (pltpu.roll(start, LANES - 1, 1) - start).astype(jnp.int32)
        start = start.astype(jnp.int32)
        off, put = start & (LANES - 1), end & (LANES - 1)
        row = 16 * jnp.minimum(start >> 7, chunks - 1)
        for j, item in enumerate((row, (put - off) & (LANES - 1), off + (put << 7) + ((put + size) << 14))):
            cue[CUES * s + j : CUES * s + j + 1, :] = item
        goals.append(16 * (end >> 7))
        end = end + size
    lane = iota((1, LANES), 1)
    pairs = jnp.where((lane >= base) & (lane < base + levels), (end + 2 * LANES - 1) >> 8, 0).astype(F32)
    earlier = jnp.where(iota((LANES, LANES), 0) < iota((LANES, LANES), 1), 1.0, 0.0).astype(BF16)
    before = nn_dot(jnp.broadcast_to(pairs, (8, LANES)).astype(BF16), earlier)[:1].astype(jnp.int32)
    count = jnp.sum(pairs, 1, keepdims=True)
    for s, goal in enumerate(goals):
        cue[CUES * s + 3 : CUES * s + 4, :] = 32 * before + goal
    last = CUES * sources
    cue[last : last + 1, :] = before
    cue[last + 1 : last + 2, :] = 32 * before + 16 * (end >> 7)
    cue[last + 2 : last + 3, :] = jnp.broadcast_to(count, (1, LANES)).astype(jnp.int32)


def gather_levels(sources, nvar, chunks, base, levels, own, oth, cue, scalar_cue, sem, store, queue, level_of):
    lane = iota((8, LANES), 1)
    sub = iota((8, LANES), 0)
    make_cues(sources, (nvar + 1) * chunks, chunks, base, levels, own, cue)
    copy = pltpu.make_async_copy(cue, scalar_cue, sem)
    copy.start()
    nothing = jnp.zeros((8, LANES), F32)
    for s in range(sources):
        for c in range(0, chunks, 2):
            here, there = own[s, 4 * c : 4 * c + 8, :], oth[s, 4 * c : 4 * c + 8, :]
            store[s, 16 * c : 16 * c + 8, :] = jnp.where(sub < 4, here, pltpu.roll(there, 4, 0))
            store[s, 16 * c + 16 : 16 * c + 24, :] = jnp.where(sub < 4, pltpu.roll(here, 4, 0), there)
        for c in range(chunks):
            spot = own[s, nvar * chunks + c : nvar * chunks + c + 1, :]
            store[s, 16 * c + 8 : 16 * c + 16, :] = jnp.broadcast_to(spot, (8, LANES))
        store[s, 16 * chunks :, :] = jnp.zeros((16, LANES), F32)
    copy.wait()
    last = CUES * sources

    def tile(start, at):
        return pl.ds(pl.multiple_of(start, 16) + at, 8)

    def per_level(k):
        lev = base + k
        held, held_spot = nothing, nothing
        for s in range(sources):
            row, turn, word, at = (scalar_cue[CUES * s + j, lev] for j in range(4))
            word = jnp.full((8, LANES), word, jnp.int32)
            put, stop = (word >> 7) & (LANES - 1), word >> 14
            first = lane >= (word & (LANES - 1))
            value = jnp.where(first, store[s, tile(row, 0), :], store[s, tile(row, 16), :])
            value = pltpu.roll(value, turn, 1)
            spot = jnp.where(first, store[s, tile(row, 8), :], store[s, tile(row, 24), :])
            spot = pltpu.roll(spot, turn, 1)
            fresh = (lane >= put) & (lane < stop)
            held = jnp.where(fresh, value, held)
            held_spot = jnp.where(fresh, spot, held_spot)
            queue[tile(at, 0), :] = held
            queue[tile(at, 8), :] = held_spot
            late = lane < stop - LANES
            over = stop >= LANES
            held = jnp.where(over, jnp.where(late, value, 0.0), held)
            held_spot = jnp.where(over, jnp.where(late, spot, 0.0), held_spot)
        at = scalar_cue[last + 1, lev]
        queue[tile(at, 0), :] = held
        queue[tile(at, 8), :] = held_spot
        queue[tile(at, 16), :] = nothing
        queue[tile(at, 24), :] = nothing
        pair = scalar_cue[last, lev]
        for p in range(sources // 2):
            level_of[pair + p] = k

    def group(g, carry):
        for p in range(2):
            per_level(2 * g + p)
        return carry

    lax.fori_loop(0, levels // 2, group, 0)
    pair = scalar_cue[last + 2, 0]
    for p in range(UNROLL):
        level_of[pair + p] = levels
        for at in range(0, 32, 8):
            queue[tile(32 * (pair + p), at), :] = nothing
    return pair


UNROLL = 16
REST = 4


def spread(wide, levels, base, width, first, queue, level_of, count, field):
    sub = iota((8, LANES), 0)
    col = first[0] + sub % 4
    reach = jnp.where(sub < 4, col, 2 * wide - col).astype(F32)
    tall = iota((HALF, LANES), 0).astype(F32).astype(BF16)
    one, zero = jnp.ones((HALF, LANES), BF16), jnp.zeros((HALF, LANES), BF16)
    none = jnp.zeros((16, LANES), BF16)

    def clear(k, carry):
        field[k] = jnp.zeros(field.shape[1:], F32)
        return carry

    lax.fori_loop(0, levels + 1, clear, 0)

    def group(first_pair, size):
        for p in range(size):
            parts_of_y = 2 if p % 2 == 0 else 4
            length = NY // parts_of_y
            shift = length.bit_length() - 1
            pair = first_pair + p
            k = level_of[pair]
            rate = width[base + jnp.minimum(k, levels - 1)].astype(F32)
            slope = -1.0 / jnp.full((8, LANES), rate, F32)
            lefts, rights = [], []
            for h in range(2):
                start = pl.multiple_of(32 * pair + 16 * h, 16)
                value = queue[pl.ds(start, 8), :]
                spot = queue[pl.ds(start + 8, 8), :].astype(jnp.int32)
                xpos = (spot >> 9).astype(F32)
                section = ((spot >> shift) & (parts_of_y - 1)).astype(F32)
                ypos = (spot & (length - 1)).astype(F32)
                gain = jnp.exp(jnp.abs(reach - xpos) * slope)
                gain = gain - pltpu.roll(gain, 4, 0)
                section = jnp.concatenate([section, section], 0).astype(BF16)
                inside = [section == jnp.full((16, LANES), q, BF16) for q in range(parts_of_y)]
                tiles = []
                for x in range(NX_DEV):
                    term = value * jnp.broadcast_to(gain[x : x + 1, :], (8, LANES))
                    top = term.astype(BF16).astype(F32)
                    both = jnp.concatenate([top, term - top], 0).astype(BF16)
                    tiles += [jnp.where(inside[q], both, none) for q in range(parts_of_y)]
                lefts.append(jnp.concatenate(tiles, 0))
                mark = jnp.broadcast_to(ypos[:1], (length, LANES)).astype(BF16)
                rights.append(jnp.where(tall[:length] == mark, one[:length], zero[:length]))
            done = nt_dot(jnp.concatenate(lefts, 1), jnp.concatenate(rights, 1))
            parts = []
            for i in range(parts_of_y * NX_DEV):
                total = done[16 * i : 16 * i + 8] + done[16 * i + 8 : 16 * i + 16]
                parts += [total[:, at : at + LANES] for at in range(0, length, LANES)]
            field[k] = field[k] + jnp.concatenate(parts, 0)

    def long_group(g, carry):
        group(g * UNROLL, UNROLL)
        return carry

    def short_group(g, carry):
        group(done_pairs + g * REST, REST)
        return carry

    groups = count >> 4
    done_pairs = groups * UNROLL
    lax.fori_loop(0, groups, long_group, 0)
    lax.fori_loop(0, (count - done_pairs + REST - 1) >> 2, short_group, 0)


def filter_levels(levels, base, width, table, field, slab):
    lane = iota((8, LANES), 1)
    line = lane.astype(F32)

    def one_level(k):
        slope = -1.0 / jnp.full((8, LANES), width[base + k].astype(F32), F32)
        grid = field[k]
        top = grid.astype(BF16)
        rest = (grid - top.astype(F32)).astype(BF16)
        mat = table[k, :LANES, :]
        done = nn_dot(jnp.concatenate([top, rest], 1), jnp.concatenate([mat, mat], 0)) + nn_dot(top, table[k, LANES:, :])
        rise = jnp.exp(line * slope)
        fall = jnp.exp((LANES - 1.0 - line) * slope)
        edge = jnp.exp((LANES - line) * slope)
        hop = jnp.exp(LANES * slope)
        for x in range(NX_DEV):
            ahead, behind, here = [], [], []
            for b in range(4):
                row = (4 * x + b) * 8
                here.append(done[row : row + 8, :LANES])
                moments = done[row : row + 8, LANES:]
                turned = pltpu.roll(moments, LANES // 2, 1)
                ahead.append(jnp.where(lane < LANES // 2, moments, turned))
                behind.append(jnp.where(lane < LANES // 2, turned, moments))
            run = ahead[0]
            for b in range(1, 4):
                here[b] = here[b] + rise * run
                run = ahead[b] + hop * run
            bound = edge * run
            run = behind[3]
            for b in (2, 1, 0):
                here[b] = here[b] + fall * run
                run = behind[b] + hop * run
            for b in (3, 2, 1, 0):
                slab[x, b, pl.ds(pl.multiple_of(8 * k, 8), 8), :] = here[b] - bound
                bound = bound * hop

    def group(g, carry):
        for p in range(4):
            one_level(4 * g + p)
        return carry

    lax.fori_loop(0, levels // 4, group, 0)


def field_kernel(sources, wide, nvar, width, first, start, own, oth, far_table, slab, *scratch):
    table, table_sem, cue, scalar_cue, sem, store, queue, level_of, field = scratch
    chunks = (own.shape[1] - 8) // (nvar + 1)
    levels = table.shape[0]
    base = start[0]
    fetch = pltpu.make_async_copy(far_table, table, table_sem)
    fetch.start()
    count = gather_levels(
        sources, nvar, chunks, base, levels, own, oth, cue, scalar_cue, sem, store, queue, level_of
    )
    spread(wide, levels, base, width, first, queue, level_of, count, field)
    fetch.wait()
    filter_levels(levels, base, width, table, field, slab)


def make_field(own, oth, band_width, first, base, table, nvar, levels, wide):
    sources, rows, _ = own.shape
    chunks = (rows - 8) // (nvar + 1)
    whole = pl.BlockSpec(memory_space=pltpu.VMEM)
    smem = pl.BlockSpec(memory_space=pltpu.SMEM)
    pairs = levels * sources // 2 + UNROLL + 1
    return pl.pallas_call(
        functools.partial(field_kernel, sources, wide, nvar),
        in_specs=[smem] * 3 + [whole] * 2 + [pl.BlockSpec(memory_space=pltpu.HBM)],
        out_specs=whole,
        out_shape=jax.ShapeDtypeStruct((NX_DEV, 4, 2 * nvar * levels, LANES), F32),
        scratch_shapes=[
            pltpu.VMEM(table.shape, BF16),
            pltpu.SemaphoreType.DMA,
            pltpu.VMEM((CUES * sources + 8, LANES), jnp.int32),
            pltpu.SMEM((CUES * sources + 8, LANES), jnp.int32),
            pltpu.SemaphoreType.DMA,
            pltpu.VMEM((sources, 16 * chunks + 16, LANES), F32),
            pltpu.VMEM((32 * pairs, LANES), F32),
            pltpu.SMEM((pairs + sources,), jnp.int32),
            pltpu.VMEM((levels + 1, 32 * NX_DEV, LANES), F32),
        ],
        compiler_params=pltpu.CompilerParams(vmem_limit_bytes=50 << 20),
        name="field",
    )(band_width, first, base, own, oth, table)


def mix_kernel(slab, high, low, *refs):
    out = refs[-1]
    rows = high.shape[0]
    for x in range(NX_DEV):
        part = jnp.concatenate([slab[x, 0], slab[x, 1]], 1)
        top = part.astype(BF16)
        rest = (part - top.astype(F32)).astype(BF16)
        term = nn_dot(jnp.concatenate([high[...], low[...]], 0), top)
        term = term[:rows] + term[rows:] + nn_dot(high[...], rest)
        if len(refs) == 1:
            out[0, x] = term
        else:
            term = term + refs[0][0, x]
            flat = out.reshape(8 * term.shape[0], LANES)
            for g in range(2):
                flat[pl.ds(4 * g + x, term.shape[0], stride=8), :] = term[:, g * LANES : (g + 1) * LANES]


def mix(slab, mats, *before):
    rows, depth = mats[0].shape
    strip = pl.BlockSpec((NX_DEV, 2, depth, LANES), lambda i: (0, i, 0, 0))
    matrix = pl.BlockSpec((rows, depth), lambda i: (0, 0))
    partial = pl.BlockSpec((1, NX_DEV, rows, HALF), lambda i: (i, 0, 0, 0))
    if before:
        shape = (rows, 16, LANES)
        out_spec = pl.BlockSpec((rows, 8, LANES), lambda i: (0, i, 0))
    else:
        shape = (2, NX_DEV, rows, HALF)
        out_spec = partial
    return pl.pallas_call(
        mix_kernel,
        grid=(2,),
        in_specs=[strip, matrix, matrix] + [partial] * len(before),
        out_specs=out_spec,
        out_shape=jax.ShapeDtypeStruct(shape, F32),
        compiler_params=pltpu.CompilerParams(vmem_limit_bytes=16 << 20),
        cost_estimate=pl.CostEstimate(flops=1 << 30, bytes_accessed=6 << 20, transcendentals=0),
        name="mix",
    )(slab, *mats, *before)


def on_device(innovations, obs_owner, obs_local, obs_level, band_width, vert_scale, sigma, balance):
    groups = lax.axis_size("sub")
    nvar, _ = innovations.shape
    levels = band_width.shape[0]
    swap = [(0, 1), (1, 0)]
    unit = route(innovations, obs_owner, obs_level, obs_local, levels)
    side = lax.axis_index("var").astype(jnp.int32)
    half = levels // 2
    base, last = half * side, half * (1 - side)
    theirs = lax.ppermute(vert_scale, "var", swap)
    weights = jnp.where(side == 0, balance, jnp.roll(balance, nvar, 1))
    own_mats = mix_matrix(jnp.concatenate([vert_scale, theirs], 0), sigma, weights, base, half)
    oth_mats = mix_matrix(jnp.concatenate([theirs, vert_scale], 0), sigma, jnp.roll(weights, nvar, 1), last, half)
    first = (lax.axis_index("sub") * NX_DEV).astype(jnp.int32).reshape(1)
    base = base.reshape(1)
    own = [unit]
    for k in range(2, groups, 2):
        own.append(lax.ppermute(unit, "sub", [(i, (i + k) % groups) for i in range(groups)]))
    far = len(own) // 2
    own[far], own_mats, oth_mats, when = lax.optimization_barrier((own[far], own_mats, oth_mats, base))
    table = tables(band_width, when, half)
    own += [lax.ppermute(held, "sub", [(i, i ^ 1) for i in range(groups)]) for held in own]
    own[-1], table = lax.optimization_barrier((own[-1], table))
    own = jnp.stack(own)
    oth = lax.ppermute(own, "var", swap)
    slab = make_field(own, oth, band_width, first, base, table, nvar, half, NX_DEV * groups)
    swapped = lax.ppermute(slab, "var", swap)
    out = mix(swapped, oth_mats, mix(slab, own_mats))
    out = out.reshape(nvar, levels, NY // LANES, NX_DEV, LANES)
    return jnp.swapaxes(out, 2, 3).reshape(nvar, levels, NX_DEV, NY)


def solution(mesh):
    in_specs = (
        P("var", ("member", "sub")),
        P(("member", "sub"), None),
        P(("member", "sub")),
        P(("member", "sub"), None),
        P(),
        P("var", None),
        P("var", None),
        P("var", None),
    )
    out_specs = P("var", None, ("member", "sub"), None)
    return jax.shard_map(on_device, mesh=mesh, in_specs=in_specs, out_specs=out_specs, check_vma=False)
```

```python
import functools

import jax
import jax.numpy as jnp
from jax import lax
from jax.experimental import pallas as pl
from jax.experimental.pallas import tpu as pltpu
from jax.sharding import PartitionSpec as P

VB = 6
NX_DEV = 4
NY = 512
LANES = 128
HALF = 256
F32 = jnp.float32
BF16 = jnp.bfloat16


def nt_dot(a, b):
    return lax.dot_general(a, b, (((1,), (1,)), ((), ())), preferred_element_type=F32)


def nn_dot(a, b):
    return jnp.dot(a, b, preferred_element_type=F32)


def iota(shape, dim):
    return lax.broadcasted_iota(jnp.int32, shape, dim)


def route_kernel(inn_ref, level_ref, owner_ref, local_ref, pay, inn, level, owner, local, sems, hot, pre, dest, left, right):
    pairs = ((level_ref, level), (inn_ref, inn), (owner_ref, owner), (local_ref, local))
    copies = [pltpu.make_async_copy(src, dst, sems.at[k]) for k, (src, dst) in enumerate(pairs)]
    for copy in copies:
        copy.start()
    for copy in copies:
        copy.wait()
    nvar, nobs = inn.shape
    chunks = nobs // LANES
    levels = hot.shape[0] // chunks
    rows = iota((levels, LANES), 0)
    for c in range(chunks):
        hit = jnp.where(rows == level[c : c + 1, :], 1.0, 0.0)
        hot[c * levels : (c + 1) * levels, :] = hit.astype(BF16)
    before = iota((LANES, 2 * LANES), 0) < iota((LANES, 2 * LANES), 1)
    pre[...] = nn_dot(hot[...], jnp.where(before, 1.0, 0.0).astype(BF16))
    count = jnp.zeros((levels, LANES), F32)
    for c in range(chunks):
        count = count + pre[c * levels : (c + 1) * levels, LANES:]
    lower = iota((levels, levels), 1) < iota((levels, levels), 0)
    base = nn_dot(jnp.where(lower, 1.0, 0.0).astype(BF16), count.astype(BF16))
    lane = iota((levels, LANES), 1)
    starts = jnp.sum(jnp.where(lane == rows, base, 0.0), 0, keepdims=True)
    starts = jnp.where(iota((8, LANES), 1) < levels, starts, float(nobs))
    for c in range(chunks):
        part = pre[c * levels : (c + 1) * levels, :]
        slot = jnp.where(rows == level[c : c + 1, :], part[:, :LANES] + base, 0.0)
        dest[c : c + 1, :] = jnp.sum(slot, 0, keepdims=True).astype(jnp.int32)
        base = base + part[:, LANES:]
    place = owner[...] * (NX_DEV * NY) + local[...]
    rows_hi, rows_lo = iota((chunks, LANES), 0), iota((LANES, LANES), 0)
    for c in range(chunks):
        at = slice(c * LANES, (c + 1) * LANES)
        slot = dest[c : c + 1, :]
        mask = rows_hi == slot // LANES
        right[c] = jnp.where(rows_lo == slot % LANES, 1.0, 0.0).astype(BF16)
        pieces = []
        for v in range(nvar):
            value = inn[v : v + 1, at]
            high = value.astype(BF16).astype(F32)
            pieces += [high, value - high]
        spot = place[c : c + 1, :]
        pieces += [(spot // HALF).astype(F32), (spot % HALF).astype(F32)]
        for q, piece in enumerate(pieces):
            left[c, q * chunks : (q + 1) * chunks, :] = jnp.where(mask, piece, 0.0).astype(BF16)
    packed = nt_dot(
        jnp.concatenate([left[c] for c in range(chunks)], 1),
        jnp.concatenate([right[c] for c in range(chunks)], 1),
    )
    for v in range(nvar):
        both = packed[2 * v * chunks : (2 * v + 1) * chunks] + packed[(2 * v + 1) * chunks : (2 * v + 2) * chunks]
        pay[pl.ds(v, chunks, stride=nvar), :] = both
    high, low = packed[2 * nvar * chunks : (2 * nvar + 1) * chunks], packed[(2 * nvar + 1) * chunks :]
    pay[nvar * chunks : (nvar + 1) * chunks, :] = high * float(HALF) + low
    pay[(nvar + 1) * chunks :, :] = starts


def route(innovations, owner, level, local, levels):
    nvar, nobs = innovations.shape
    chunks = nobs // LANES
    pieces = 2 * nvar + 2
    return pl.pallas_call(
        route_kernel,
        out_shape=jax.ShapeDtypeStruct(((nvar + 1) * chunks + 8, LANES), F32),
        in_specs=[pl.BlockSpec(memory_space=pltpu.HBM)] * 4,
        scratch_shapes=[
            pltpu.VMEM((nvar, nobs), F32),
            pltpu.VMEM((chunks, LANES), jnp.int32),
            pltpu.VMEM((chunks, LANES), jnp.int32),
            pltpu.VMEM((chunks, LANES), jnp.int32),
            pltpu.SemaphoreType.DMA((4,)),
            pltpu.VMEM((chunks * levels, LANES), BF16),
            pltpu.VMEM((chunks * levels, 2 * LANES), F32),
            pltpu.VMEM((chunks, LANES), jnp.int32),
            pltpu.VMEM((chunks, pieces * chunks, LANES), BF16),
            pltpu.VMEM((chunks, LANES, LANES), BF16),
        ],
        compiler_params=pltpu.CompilerParams(vmem_limit_bytes=60 << 20),
        name="route",
    )(innovations, level.reshape(chunks, LANES), owner.reshape(chunks, LANES), local.reshape(chunks, LANES))


def table_kernel(width, base, table):
    depth = table.shape[0]
    row, col = iota((LANES, LANES), 0), iota((LANES, LANES), 1)
    near = jnp.abs(row - col).astype(F32)
    far = jnp.where(col < LANES // 2, LANES - row, row + 1).astype(F32)
    for k in range(depth):
        rate = width[base[0] + pl.program_id(0) * depth + k].astype(F32)
        for at, dist in ((0, near), (LANES, far)):
            full = jnp.exp(-dist / rate)
            top = full.astype(BF16)
            table[k, :LANES, at : at + LANES] = top
            table[k, LANES:, at : at + LANES] = (full - top.astype(F32)).astype(BF16)


def tables(band_width, base, levels):
    depth = 8
    spec = pl.BlockSpec((depth, 2 * LANES, 2 * LANES), lambda i: (i, 0, 0))
    shape = jax.ShapeDtypeStruct((levels, 2 * LANES, 2 * LANES), BF16)
    return pl.pallas_call(
        table_kernel,
        grid=(levels // depth,),
        in_specs=[pl.BlockSpec(memory_space=pltpu.SMEM)] * 2,
        out_specs=spec,
        out_shape=shape,
        cost_estimate=pl.CostEstimate(flops=1 << 24, bytes_accessed=8 << 20, transcendentals=1 << 20),
        name="tables",
    )(band_width, base)


def pick(table, chosen):
    return lax.dot_general(
        table, chosen, (((0,), (0,)), ((), ())), precision=lax.Precision.HIGHEST, preferred_element_type=F32
    )


def matrix_kernel(side, scale, theirs, sigma, balance, *outs):
    nvar, levels = scale.shape
    both = 2 * nvar
    cols = outs[0].shape[1]
    depth = cols // both
    for k in range(2):
        here = (side[0] + k) % 2
        scales = (scale, theirs) if k == 0 else (theirs, scale)
        unit = iota((nvar, cols), 1) % both
        pairs = [(held[...], jnp.where(unit == iota((nvar, cols), 0) + nvar * j, 1.0, 0.0)) for j, held in enumerate(scales)]
        own = sum(pick(held, chosen) for held, chosen in pairs)
        gap = iota((levels, cols), 0) - depth * here - iota((levels, cols), 1) // both
        other = jnp.sum(jnp.where(gap == 0, own, 0.0), 0, keepdims=True)
        dist = gap.astype(F32)
        corr = jnp.where(jnp.abs(gap) <= VB, jnp.exp(-dist * dist / (2.0 * own * other)), 0.0)
        order = (iota((both, cols), 1) + nvar * here) % both
        chosen = jnp.where(order == iota((both, cols), 0), 1.0, 0.0)
        weight = jnp.dot(balance[...], chosen, precision=lax.Precision.HIGHEST, preferred_element_type=F32)
        for v in range(nvar):
            spread_out = jnp.where(iota((nvar, cols), 0) == v, 1.0, 0.0)
            full = pick(sigma[...], spread_out) * weight[v : v + 1, :] * corr
            top = full.astype(BF16)
            rows = slice(v * levels, (v + 1) * levels)
            outs[2 * k][rows, :] = top
            outs[2 * k + 1][rows, :] = (full - top.astype(F32)).astype(BF16)


def mix_matrices(side, scale, theirs, sigma, balance):
    nvar, levels = scale.shape
    shape = jax.ShapeDtypeStruct((nvar * levels, nvar * levels), BF16)
    whole = pl.BlockSpec(memory_space=pltpu.VMEM)
    outs = pl.pallas_call(
        matrix_kernel,
        in_specs=[pl.BlockSpec(memory_space=pltpu.SMEM)] + [whole] * 4,
        out_specs=(whole,) * 4,
        out_shape=(shape,) * 4,
        compiler_params=pltpu.CompilerParams(vmem_limit_bytes=12 << 20),
        name="matrices",
    )(side, scale, theirs, sigma, balance)
    return outs[:2], outs[2:]


CUES = 4


def make_cues(sources, starts_row, chunks, base, levels, own, cue):
    end = jnp.zeros((1, LANES), jnp.int32)
    goals = []
    for s in range(sources):
        start = own[s, starts_row : starts_row + 1, :]
        size = (pltpu.roll(start, LANES - 1, 1) - start).astype(jnp.int32)
        start = start.astype(jnp.int32)
        off, put = start & (LANES - 1), end & (LANES - 1)
        row = 16 * jnp.minimum(start >> 7, chunks - 1)
        for j, item in enumerate((row, (put - off) & (LANES - 1), off + (put << 7) + ((put + size) << 14))):
            cue[CUES * s + j : CUES * s + j + 1, :] = item
        goals.append(16 * (end >> 7))
        end = end + size
    lane = iota((1, LANES), 1)
    pairs = jnp.where((lane >= base) & (lane < base + levels), (end + 2 * LANES - 1) >> 8, 0).astype(F32)
    earlier = jnp.where(iota((LANES, LANES), 0) < iota((LANES, LANES), 1), 1.0, 0.0).astype(BF16)
    before = nn_dot(jnp.broadcast_to(pairs, (8, LANES)).astype(BF16), earlier)[:1].astype(jnp.int32)
    count = jnp.sum(pairs, 1, keepdims=True)
    for s, goal in enumerate(goals):
        cue[CUES * s + 3 : CUES * s + 4, :] = 32 * before + goal
    last = CUES * sources
    cue[last : last + 1, :] = before
    cue[last + 1 : last + 2, :] = 32 * before + 16 * (end >> 7)
    cue[last + 2 : last + 3, :] = jnp.broadcast_to(count, (1, LANES)).astype(jnp.int32)


def gather_levels(sources, nvar, chunks, base, levels, own, oth, cue, scalar_cue, sem, store, queue, level_of):
    lane = iota((8, LANES), 1)
    sub = iota((8, LANES), 0)
    make_cues(sources, (nvar + 1) * chunks, chunks, base, levels, own, cue)
    copy = pltpu.make_async_copy(cue, scalar_cue, sem)
    copy.start()
    nothing = jnp.zeros((8, LANES), F32)
    for s in range(sources):
        for c in range(0, chunks, 2):
            here, there = own[s, 4 * c : 4 * c + 8, :], oth[s, 4 * c : 4 * c + 8, :]
            store[s, 16 * c : 16 * c + 8, :] = jnp.where(sub < 4, here, pltpu.roll(there, 4, 0))
            store[s, 16 * c + 16 : 16 * c + 24, :] = jnp.where(sub < 4, pltpu.roll(here, 4, 0), there)
        for c in range(chunks):
            spot = own[s, nvar * chunks + c : nvar * chunks + c + 1, :]
            store[s, 16 * c + 8 : 16 * c + 16, :] = jnp.broadcast_to(spot, (8, LANES))
        store[s, 16 * chunks :, :] = jnp.zeros((16, LANES), F32)
    copy.wait()
    last = CUES * sources

    def tile(start, at):
        return pl.ds(pl.multiple_of(start, 16) + at, 8)

    def per_level(k):
        lev = base + k
        held, held_spot = nothing, nothing
        for s in range(sources):
            row, turn, word, at = (scalar_cue[CUES * s + j, lev] for j in range(4))
            word = jnp.full((8, LANES), word, jnp.int32)
            put, stop = (word >> 7) & (LANES - 1), word >> 14
            first = lane >= (word & (LANES - 1))
            value = jnp.where(first, store[s, tile(row, 0), :], store[s, tile(row, 16), :])
            value = pltpu.roll(value, turn, 1)
            spot = jnp.where(first, store[s, tile(row, 8), :], store[s, tile(row, 24), :])
            spot = pltpu.roll(spot, turn, 1)
            fresh = (lane >= put) & (lane < stop)
            held = jnp.where(fresh, value, held)
            held_spot = jnp.where(fresh, spot, held_spot)
            queue[tile(at, 0), :] = held
            queue[tile(at, 8), :] = held_spot
            late = lane < stop - LANES
            over = stop >= LANES
            held = jnp.where(over, jnp.where(late, value, 0.0), held)
            held_spot = jnp.where(over, jnp.where(late, spot, 0.0), held_spot)
        at = scalar_cue[last + 1, lev]
        queue[tile(at, 0), :] = held
        queue[tile(at, 8), :] = held_spot
        queue[tile(at, 16), :] = nothing
        queue[tile(at, 24), :] = nothing
        pair = scalar_cue[last, lev]
        for p in range(sources // 2):
            level_of[pair + p] = k

    def group(g, carry):
        for p in range(2):
            per_level(2 * g + p)
        return carry

    lax.fori_loop(0, levels // 2, group, 0)
    pair = scalar_cue[last + 2, 0]
    for p in range(UNROLL):
        level_of[pair + p] = levels
        for at in range(0, 32, 8):
            queue[tile(32 * (pair + p), at), :] = nothing
    return pair


UNROLL = 16
REST = 4


def spread(wide, levels, base, width, first, queue, level_of, count, field):
    sub = iota((8, LANES), 0)
    col = first[0] + sub % 4
    reach = jnp.where(sub < 4, col, 2 * wide - col).astype(F32)
    tall = iota((HALF, LANES), 0).astype(F32).astype(BF16)
    one, zero = jnp.ones((HALF, LANES), BF16), jnp.zeros((HALF, LANES), BF16)
    none = jnp.zeros((16, LANES), BF16)

    def clear(k, carry):
        field[k] = jnp.zeros(field.shape[1:], F32)
        return carry

    lax.fori_loop(0, levels + 1, clear, 0)

    def group(first_pair, size):
        for p in range(size):
            parts_of_y = 2 if p % 2 == 0 else 4
            length = NY // parts_of_y
            shift = length.bit_length() - 1
            pair = first_pair + p
            k = level_of[pair]
            rate = width[base + jnp.minimum(k, levels - 1)].astype(F32)
            slope = -1.0 / jnp.full((8, LANES), rate, F32)
            lefts, rights = [], []
            for h in range(2):
                start = pl.multiple_of(32 * pair + 16 * h, 16)
                value = queue[pl.ds(start, 8), :]
                spot = queue[pl.ds(start + 8, 8), :].astype(jnp.int32)
                xpos = (spot >> 9).astype(F32)
                section = ((spot >> shift) & (parts_of_y - 1)).astype(F32)
                ypos = (spot & (length - 1)).astype(F32)
                gain = jnp.exp(jnp.abs(reach - xpos) * slope)
                gain = gain - pltpu.roll(gain, 4, 0)
                section = jnp.concatenate([section, section], 0).astype(BF16)
                inside = [section == jnp.full((16, LANES), q, BF16) for q in range(parts_of_y)]
                tiles = []
                for x in range(NX_DEV):
                    term = value * jnp.broadcast_to(gain[x : x + 1, :], (8, LANES))
                    top = term.astype(BF16).astype(F32)
                    both = jnp.concatenate([top, term - top], 0).astype(BF16)
                    tiles += [jnp.where(inside[q], both, none) for q in range(parts_of_y)]
                lefts.append(jnp.concatenate(tiles, 0))
                mark = jnp.broadcast_to(ypos[:1], (length, LANES)).astype(BF16)
                rights.append(jnp.where(tall[:length] == mark, one[:length], zero[:length]))
            done = nt_dot(jnp.concatenate(lefts, 1), jnp.concatenate(rights, 1))
            parts = []
            for i in range(parts_of_y * NX_DEV):
                total = done[16 * i : 16 * i + 8] + done[16 * i + 8 : 16 * i + 16]
                parts += [total[:, at : at + LANES] for at in range(0, length, LANES)]
            field[k] = field[k] + jnp.concatenate(parts, 0)

    def long_group(g, carry):
        group(g * UNROLL, UNROLL)
        return carry

    def short_group(g, carry):
        group(done_pairs + g * REST, REST)
        return carry

    groups = count >> 4
    done_pairs = groups * UNROLL
    lax.fori_loop(0, groups, long_group, 0)
    lax.fori_loop(0, (count - done_pairs + REST - 1) >> 2, short_group, 0)


def filter_levels(skip, levels, base, width, table, field, slab):
    lane = iota((8, LANES), 1)
    line = lane.astype(F32)

    def one_level(k):
        slope = -1.0 / jnp.full((8, LANES), width[base + skip + k].astype(F32), F32)
        grid = field[skip + k]
        top = grid.astype(BF16)
        rest = (grid - top.astype(F32)).astype(BF16)
        mat = table[k, :LANES, :]
        done = nn_dot(jnp.concatenate([top, rest], 1), jnp.concatenate([mat, mat], 0)) + nn_dot(top, table[k, LANES:, :])
        rise = jnp.exp(line * slope)
        fall = jnp.exp((LANES - 1.0 - line) * slope)
        edge = jnp.exp((LANES - line) * slope)
        hop = jnp.exp(LANES * slope)
        for x in range(NX_DEV):
            ahead, behind, here = [], [], []
            for b in range(4):
                row = (4 * x + b) * 8
                here.append(done[row : row + 8, :LANES])
                moments = done[row : row + 8, LANES:]
                turned = pltpu.roll(moments, LANES // 2, 1)
                ahead.append(jnp.where(lane < LANES // 2, moments, turned))
                behind.append(jnp.where(lane < LANES // 2, turned, moments))
            run = ahead[0]
            for b in range(1, 4):
                here[b] = here[b] + rise * run
                run = ahead[b] + hop * run
            bound = edge * run
            run = behind[3]
            for b in (2, 1, 0):
                here[b] = here[b] + fall * run
                run = behind[b] + hop * run
            for b in (3, 2, 1, 0):
                slab[x, b, pl.ds(pl.multiple_of(8 * k, 8), 8), :] = here[b] - bound
                bound = bound * hop

    def group(g, carry):
        for p in range(4):
            one_level(4 * g + p)
        return carry

    lax.fori_loop(0, levels // 4, group, 0)


def field_kernel(sources, wide, nvar, width, first, start, own, oth, far_table, slab, field, table_rest, *scratch):
    table, table_sems, cue, scalar_cue, sem, store, queue, level_of = scratch
    chunks = (own.shape[1] - 8) // (nvar + 1)
    levels, part = far_table.shape[0], table.shape[0]
    base = start[0]
    fetch = pltpu.make_async_copy(far_table.at[:part], table, table_sems.at[0])
    fetch_rest = pltpu.make_async_copy(far_table.at[part:], table_rest, table_sems.at[1])
    fetch.start()
    fetch_rest.start()
    count = gather_levels(
        sources, nvar, chunks, base, levels, own, oth, cue, scalar_cue, sem, store, queue, level_of
    )
    spread(wide, levels, base, width, first, queue, level_of, count, field)
    fetch.wait()
    fetch_rest.wait()
    filter_levels(0, part, base, width, table, field, slab)


def rest_kernel(width, start, field, table, slab):
    part = table.shape[0]
    filter_levels(part, part, start[0], width, table, field, slab)


def make_field(own, oth, band_width, first, base, table, nvar, levels, wide):
    sources, rows, _ = own.shape
    chunks = (rows - 8) // (nvar + 1)
    whole = pl.BlockSpec(memory_space=pltpu.VMEM)
    smem = pl.BlockSpec(memory_space=pltpu.SMEM)
    pairs = levels * sources // 2 + UNROLL + 1
    return pl.pallas_call(
        functools.partial(field_kernel, sources, wide, nvar),
        in_specs=[smem] * 3 + [whole] * 2 + [pl.BlockSpec(memory_space=pltpu.HBM)],
        out_specs=(whole, whole, whole),
        out_shape=(
            jax.ShapeDtypeStruct((NX_DEV, 4, nvar * levels, LANES), F32),
            jax.ShapeDtypeStruct((levels + 1, 32 * NX_DEV, LANES), F32),
            jax.ShapeDtypeStruct((levels // 2,) + table.shape[1:], BF16),
        ),
        scratch_shapes=[
            pltpu.VMEM((levels // 2,) + table.shape[1:], BF16),
            pltpu.SemaphoreType.DMA((2,)),
            pltpu.VMEM((CUES * sources + 8, LANES), jnp.int32),
            pltpu.SMEM((CUES * sources + 8, LANES), jnp.int32),
            pltpu.SemaphoreType.DMA,
            pltpu.VMEM((sources, 16 * chunks + 16, LANES), F32),
            pltpu.VMEM((32 * pairs, LANES), F32),
            pltpu.SMEM((pairs + sources,), jnp.int32),
        ],
        compiler_params=pltpu.CompilerParams(vmem_limit_bytes=46 << 20),
        name="field",
    )(band_width, first, base, own, oth, table)


def filter_rest(band_width, base, field, table, shape):
    whole = pl.BlockSpec(memory_space=pltpu.VMEM)
    smem = pl.BlockSpec(memory_space=pltpu.SMEM)
    return pl.pallas_call(
        rest_kernel,
        in_specs=[smem, smem, whole, whole],
        out_specs=whole,
        out_shape=jax.ShapeDtypeStruct(shape, F32),
        compiler_params=pltpu.CompilerParams(vmem_limit_bytes=16 << 20),
        cost_estimate=pl.CostEstimate(flops=1 << 33, bytes_accessed=32 << 20, transcendentals=0),
        name="rest",
    )(band_width, base, field, table)


def mix_kernel(slab, more, high, low, *refs):
    out = refs[-1]
    rows = high.shape[0]
    half = pl.program_id(0)
    for x in range(NX_DEV):
        part = jnp.concatenate([jnp.concatenate([some[x, 2 * half], some[x, 2 * half + 1]], 1) for some in (slab, more)], 0)
        top = part.astype(BF16)
        rest = (part - top.astype(F32)).astype(BF16)
        term = nn_dot(jnp.concatenate([high[...], low[...]], 0), top)
        term = term[:rows] + term[rows:] + nn_dot(high[...], rest)
        if len(refs) == 1:
            out[half, x] = term
        else:
            term = term + refs[0][half, x]
            flat = out.reshape(8 * term.shape[0], LANES)
            for g in range(2):
                flat[pl.ds(4 * g + x, term.shape[0], stride=8), :] = term[:, g * LANES : (g + 1) * LANES]


def mix(slab, more, mats, *before):
    rows = mats[0].shape[0]
    whole = pl.BlockSpec(memory_space=pltpu.VMEM)
    if before:
        shape = (rows, 16, LANES)
        out_spec = pl.BlockSpec((rows, 8, LANES), lambda i: (0, i, 0))
    else:
        shape = (2, NX_DEV, rows, HALF)
        out_spec = whole
    return pl.pallas_call(
        mix_kernel,
        grid=(2,),
        in_specs=[whole] * (4 + len(before)),
        out_specs=out_spec,
        out_shape=jax.ShapeDtypeStruct(shape, F32),
        compiler_params=pltpu.CompilerParams(vmem_limit_bytes=16 << 20),
        name="mix",
    )(slab, more, *mats, *before)


def on_device(innovations, obs_owner, obs_local, obs_level, band_width, vert_scale, sigma, balance):
    groups = lax.axis_size("sub")
    nvar, _ = innovations.shape
    levels = band_width.shape[0]
    swap = [(0, 1), (1, 0)]
    unit = route(innovations, obs_owner, obs_level, obs_local, levels)
    side = lax.axis_index("var").astype(jnp.int32)
    half = levels // 2
    base = half * side
    theirs = lax.ppermute(vert_scale, "var", swap)
    own_mats, oth_mats = mix_matrices(side.reshape(1), vert_scale, theirs, sigma, balance)
    first = (lax.axis_index("sub") * NX_DEV).astype(jnp.int32).reshape(1)
    base = base.reshape(1)
    own = [unit]
    for k in range(2, groups, 2):
        own.append(lax.ppermute(unit, "sub", [(i, (i + k) % groups) for i in range(groups)]))
    far = len(own) // 2
    beside = [(i, i ^ 1) for i in range(groups)]
    near = lax.ppermute(unit, "sub", beside)
    table = tables(band_width, base, half)
    own[far], near, own_mats, oth_mats, table = lax.optimization_barrier((own[far], near, own_mats, oth_mats, table))
    own += [near] + [lax.ppermute(held, "sub", beside) for held in own[1:]]
    own = jnp.stack(own)
    oth = lax.ppermute(own, "var", swap)
    slab, grids, table = make_field(own, oth, band_width, first, base, table, nvar, half, NX_DEV * groups)
    swapped = lax.ppermute(slab, "var", swap)
    more = filter_rest(band_width, base, grids, table, slab.shape)
    more_swapped = lax.ppermute(more, "var", swap)
    swapped, more = lax.optimization_barrier((swapped, more))
    out = mix(swapped, more_swapped, oth_mats, mix(slab, more, own_mats))
    out = out.reshape(nvar, levels, NY // LANES, NX_DEV, LANES)
    return jnp.swapaxes(out, 2, 3).reshape(nvar, levels, NX_DEV, NY)


def solution(mesh):
    in_specs = (
        P("var", ("member", "sub")),
        P(("member", "sub"), None),
        P(("member", "sub")),
        P(("member", "sub"), None),
        P(),
        P("var", None),
        P("var", None),
        P("var", None),
    )
    out_specs = P("var", None, ("member", "sub"), None)
    return jax.shard_map(on_device, mesh=mesh, in_specs=in_specs, out_specs=out_specs, check_vma=False)
```

```python
import functools

import jax
import jax.numpy as jnp
from jax import lax
from jax.experimental import pallas as pl
from jax.experimental.pallas import tpu as pltpu
from jax.sharding import PartitionSpec as P

VB = 6
NX_DEV = 4
NY = 512
LANES = 128
HALF = 256
F32 = jnp.float32
BF16 = jnp.bfloat16


def nt_dot(a, b):
    return lax.dot_general(a, b, (((1,), (1,)), ((), ())), preferred_element_type=F32)


def nn_dot(a, b):
    return jnp.dot(a, b, preferred_element_type=F32)


def iota(shape, dim):
    return lax.broadcasted_iota(jnp.int32, shape, dim)


def route_kernel(side, inn_ref, level_ref, owner_ref, local_ref, pay, inn, level, owner, local, sems, hot, pre, dest, left, right):
    pairs = ((level_ref, level), (inn_ref, inn), (owner_ref, owner), (local_ref, local))
    copies = [pltpu.make_async_copy(src, dst, sems.at[k]) for k, (src, dst) in enumerate(pairs)]
    for copy in copies:
        copy.start()
    for copy in copies:
        copy.wait()
    nvar, nobs = inn.shape
    chunks = nobs // LANES
    levels = hot.shape[0] // chunks
    rows = iota((levels, LANES), 0)
    for c in range(chunks):
        hit = jnp.where(rows == level[c : c + 1, :], 1.0, 0.0)
        hot[c * levels : (c + 1) * levels, :] = hit.astype(BF16)
    before = iota((LANES, 2 * LANES), 0) < iota((LANES, 2 * LANES), 1)
    pre[...] = nn_dot(hot[...], jnp.where(before, 1.0, 0.0).astype(BF16))
    count = jnp.zeros((levels, LANES), F32)
    for c in range(chunks):
        count = count + pre[c * levels : (c + 1) * levels, LANES:]
    lower = iota((levels, levels), 1) < iota((levels, levels), 0)
    base = nn_dot(jnp.where(lower, 1.0, 0.0).astype(BF16), count.astype(BF16))
    lane = iota((levels, LANES), 1)
    starts = jnp.sum(jnp.where(lane == rows, base, 0.0), 0, keepdims=True)
    starts = jnp.where(iota((8, LANES), 1) < levels, starts, float(nobs))
    for c in range(chunks):
        part = pre[c * levels : (c + 1) * levels, :]
        slot = jnp.where(rows == level[c : c + 1, :], part[:, :LANES] + base, 0.0)
        dest[c : c + 1, :] = jnp.sum(slot, 0, keepdims=True).astype(jnp.int32)
        base = base + part[:, LANES:]
    place = owner[...] * (NX_DEV * NY) + local[...]
    rows_hi, rows_lo = iota((chunks, LANES), 0), iota((LANES, LANES), 0)
    for c in range(chunks):
        at = slice(c * LANES, (c + 1) * LANES)
        slot = dest[c : c + 1, :]
        mask = rows_hi == slot // LANES
        right[c] = jnp.where(rows_lo == slot % LANES, 1.0, 0.0).astype(BF16)
        pieces = []
        for v in range(nvar):
            value = inn[v : v + 1, at]
            high = value.astype(BF16).astype(F32)
            pieces += [high, value - high]
        spot = place[c : c + 1, :]
        pieces += [(spot // HALF).astype(F32), (spot % HALF).astype(F32)]
        for q, piece in enumerate(pieces):
            left[c, q * chunks : (q + 1) * chunks, :] = jnp.where(mask, piece, 0.0).astype(BF16)
    packed = nt_dot(
        jnp.concatenate([left[c] for c in range(chunks)], 1),
        jnp.concatenate([right[c] for c in range(chunks)], 1),
    )
    for v in range(nvar):
        both = packed[2 * v * chunks : (2 * v + 1) * chunks] + packed[(2 * v + 1) * chunks : (2 * v + 2) * chunks]
        pay[pl.ds(v, chunks, stride=nvar), :] = both
    high, low = packed[2 * nvar * chunks : (2 * nvar + 1) * chunks], packed[(2 * nvar + 1) * chunks :]
    spots = high * float(HALF) + low
    part = chunks // 2
    low_side = jnp.full((part, LANES), side[0], jnp.int32) == 0
    pay[nvar * chunks : nvar * chunks + part, :] = jnp.where(low_side, spots[:part], spots[part:])
    pay[nvar * chunks + part :, :] = starts


def route(side, innovations, owner, level, local, levels):
    nvar, nobs = innovations.shape
    chunks = nobs // LANES
    pieces = 2 * nvar + 2
    return pl.pallas_call(
        route_kernel,
        out_shape=jax.ShapeDtypeStruct((nvar * chunks + chunks // 2 + 8, LANES), F32),
        in_specs=[pl.BlockSpec(memory_space=pltpu.SMEM)] + [pl.BlockSpec(memory_space=pltpu.HBM)] * 4,
        scratch_shapes=[
            pltpu.VMEM((nvar, nobs), F32),
            pltpu.VMEM((chunks, LANES), jnp.int32),
            pltpu.VMEM((chunks, LANES), jnp.int32),
            pltpu.VMEM((chunks, LANES), jnp.int32),
            pltpu.SemaphoreType.DMA((4,)),
            pltpu.VMEM((chunks * levels, LANES), BF16),
            pltpu.VMEM((chunks * levels, 2 * LANES), F32),
            pltpu.VMEM((chunks, LANES), jnp.int32),
            pltpu.VMEM((chunks, pieces * chunks, LANES), BF16),
            pltpu.VMEM((chunks, LANES, LANES), BF16),
        ],
        compiler_params=pltpu.CompilerParams(vmem_limit_bytes=60 << 20),
        name="route",
    )(side, innovations, level.reshape(chunks, LANES), owner.reshape(chunks, LANES), local.reshape(chunks, LANES))


def table_kernel(width, base, table):
    depth = table.shape[0]
    row, col = iota((LANES, LANES), 0), iota((LANES, LANES), 1)
    near = jnp.abs(row - col).astype(F32)
    far = jnp.where(col < LANES // 2, LANES - row, row + 1).astype(F32)
    for k in range(depth):
        rate = width[base[0] + pl.program_id(0) * depth + k].astype(F32)
        for at, dist in ((0, near), (LANES, far)):
            full = jnp.exp(-dist / rate)
            top = full.astype(BF16)
            table[k, :LANES, at : at + LANES] = top
            table[k, LANES:, at : at + LANES] = (full - top.astype(F32)).astype(BF16)


def tables(band_width, base, levels):
    depth = 8
    spec = pl.BlockSpec((depth, 2 * LANES, 2 * LANES), lambda i: (i, 0, 0))
    shape = jax.ShapeDtypeStruct((levels, 2 * LANES, 2 * LANES), BF16)
    return pl.pallas_call(
        table_kernel,
        grid=(levels // depth,),
        in_specs=[pl.BlockSpec(memory_space=pltpu.SMEM)] * 2,
        out_specs=spec,
        out_shape=shape,
        cost_estimate=pl.CostEstimate(flops=1 << 24, bytes_accessed=8 << 20, transcendentals=1 << 20),
        name="tables",
    )(band_width, base)


def pick(table, chosen):
    return lax.dot_general(
        table, chosen, (((0,), (0,)), ((), ())), precision=lax.Precision.HIGHEST, preferred_element_type=F32
    )


def matrix_kernel(side, scale, theirs, sigma, balance, *outs):
    nvar, levels = scale.shape
    both = 2 * nvar
    cols = outs[0].shape[1]
    depth = cols // both
    for k in range(2):
        here = (side[0] + k) % 2
        scales = (scale, theirs) if k == 0 else (theirs, scale)
        unit = iota((nvar, cols), 1) % both
        pairs = [(held[...], jnp.where(unit == iota((nvar, cols), 0) + nvar * j, 1.0, 0.0)) for j, held in enumerate(scales)]
        own = sum(pick(held, chosen) for held, chosen in pairs)
        gap = iota((levels, cols), 0) - depth * here - iota((levels, cols), 1) // both
        other = jnp.sum(jnp.where(gap == 0, own, 0.0), 0, keepdims=True)
        dist = gap.astype(F32)
        corr = jnp.where(jnp.abs(gap) <= VB, jnp.exp(-dist * dist / (2.0 * own * other)), 0.0)
        order = (iota((both, cols), 1) + nvar * here) % both
        chosen = jnp.where(order == iota((both, cols), 0), 1.0, 0.0)
        weight = jnp.dot(balance[...], chosen, precision=lax.Precision.HIGHEST, preferred_element_type=F32)
        for v in range(nvar):
            spread_out = jnp.where(iota((nvar, cols), 0) == v, 1.0, 0.0)
            full = pick(sigma[...], spread_out) * weight[v : v + 1, :] * corr
            top = full.astype(BF16)
            rows = slice(v * levels, (v + 1) * levels)
            outs[2 * k][rows, :] = top
            outs[2 * k + 1][rows, :] = (full - top.astype(F32)).astype(BF16)


def mix_matrices(side, scale, theirs, sigma, balance):
    nvar, levels = scale.shape
    shape = jax.ShapeDtypeStruct((nvar * levels, nvar * levels), BF16)
    whole = pl.BlockSpec(memory_space=pltpu.VMEM)
    outs = pl.pallas_call(
        matrix_kernel,
        in_specs=[pl.BlockSpec(memory_space=pltpu.SMEM)] + [whole] * 4,
        out_specs=(whole,) * 4,
        out_shape=(shape,) * 4,
        compiler_params=pltpu.CompilerParams(vmem_limit_bytes=12 << 20),
        name="matrices",
    )(side, scale, theirs, sigma, balance)
    return outs[:2], outs[2:]


CUES = 4


def make_cues(sources, starts_row, chunks, base, levels, own, cue):
    end = jnp.zeros((1, LANES), jnp.int32)
    goals = []
    for s in range(sources):
        start = own[s, starts_row : starts_row + 1, :]
        size = (pltpu.roll(start, LANES - 1, 1) - start).astype(jnp.int32)
        start = start.astype(jnp.int32)
        off, put = start & (LANES - 1), end & (LANES - 1)
        row = 16 * jnp.minimum(start >> 7, chunks - 1)
        for j, item in enumerate((row, (put - off) & (LANES - 1), off + (put << 7) + ((put + size) << 14))):
            cue[CUES * s + j : CUES * s + j + 1, :] = item
        goals.append(16 * (end >> 7))
        end = end + size
    lane = iota((1, LANES), 1)
    pairs = jnp.where((lane >= base) & (lane < base + levels), (end + 2 * LANES - 1) >> 8, 0).astype(F32)
    earlier = jnp.where(iota((LANES, LANES), 0) < iota((LANES, LANES), 1), 1.0, 0.0).astype(BF16)
    before = nn_dot(jnp.broadcast_to(pairs, (8, LANES)).astype(BF16), earlier)[:1].astype(jnp.int32)
    count = jnp.sum(pairs, 1, keepdims=True)
    for s, goal in enumerate(goals):
        cue[CUES * s + 3 : CUES * s + 4, :] = 32 * before + goal
    last = CUES * sources
    cue[last : last + 1, :] = before
    cue[last + 1 : last + 2, :] = 32 * before + 16 * (end >> 7)
    cue[last + 2 : last + 3, :] = jnp.broadcast_to(count, (1, LANES)).astype(jnp.int32)


def gather_levels(sources, nvar, chunks, base, levels, own, oth, cue, scalar_cue, sem, store, queue, level_of):
    lane = iota((8, LANES), 1)
    sub = iota((8, LANES), 0)
    make_cues(sources, nvar * chunks + chunks // 2, chunks, base, levels, own, cue)
    copy = pltpu.make_async_copy(cue, scalar_cue, sem)
    copy.start()
    nothing = jnp.zeros((8, LANES), F32)
    for s in range(sources):
        for c in range(0, chunks, 2):
            here, there = own[s, 4 * c : 4 * c + 8, :], oth[s, 4 * c : 4 * c + 8, :]
            store[s, 16 * c : 16 * c + 8, :] = jnp.where(sub < 4, here, pltpu.roll(there, 4, 0))
            store[s, 16 * c + 16 : 16 * c + 24, :] = jnp.where(sub < 4, pltpu.roll(here, 4, 0), there)
        part = chunks // 2
        halves = own[s, nvar * chunks : nvar * chunks + part, :], oth[s, nvar * chunks : nvar * chunks + part, :]
        low_side = jnp.full((part, LANES), base, jnp.int32) == 0
        for h in range(2):
            spot = jnp.where(low_side, halves[h], halves[1 - h])
            for c in range(part):
                at = 16 * (h * part + c) + 8
                store[s, at : at + 8, :] = jnp.broadcast_to(spot[c : c + 1, :], (8, LANES))
        store[s, 16 * chunks :, :] = jnp.zeros((16, LANES), F32)
    copy.wait()
    last = CUES * sources

    def tile(start, at):
        return pl.ds(pl.multiple_of(start, 16) + at, 8)

    def per_level(k):
        lev = base + k
        held, held_spot = nothing, nothing
        for s in range(sources):
            row, turn, word, at = (scalar_cue[CUES * s + j, lev] for j in range(4))
            word = jnp.full((8, LANES), word, jnp.int32)
            put, stop = (word >> 7) & (LANES - 1), word >> 14
            first = lane >= (word & (LANES - 1))
            value = jnp.where(first, store[s, tile(row, 0), :], store[s, tile(row, 16), :])
            value = pltpu.roll(value, turn, 1)
            spot = jnp.where(first, store[s, tile(row, 8), :], store[s, tile(row, 24), :])
            spot = pltpu.roll(spot, turn, 1)
            fresh = (lane >= put) & (lane < stop)
            held = jnp.where(fresh, value, held)
            held_spot = jnp.where(fresh, spot, held_spot)
            queue[tile(at, 0), :] = held
            queue[tile(at, 8), :] = held_spot
            late = lane < stop - LANES
            over = stop >= LANES
            held = jnp.where(over, jnp.where(late, value, 0.0), held)
            held_spot = jnp.where(over, jnp.where(late, spot, 0.0), held_spot)
        at = scalar_cue[last + 1, lev]
        queue[tile(at, 0), :] = held
        queue[tile(at, 8), :] = held_spot
        queue[tile(at, 16), :] = nothing
        queue[tile(at, 24), :] = nothing
        pair = scalar_cue[last, lev]
        for p in range(sources // 2):
            level_of[pair + p] = k

    def group(g, carry):
        for p in range(2):
            per_level(2 * g + p)
        return carry

    lax.fori_loop(0, levels // 2, group, 0)
    pair = scalar_cue[last + 2, 0]
    for p in range(UNROLL):
        level_of[pair + p] = levels
        for at in range(0, 32, 8):
            queue[tile(32 * (pair + p), at), :] = nothing
    return pair


UNROLL = 16
REST = 4


def spread(wide, levels, base, width, first, queue, level_of, count, field):
    sub = iota((8, LANES), 0)
    col = first[0] + sub % 4
    reach = jnp.where(sub < 4, col, 2 * wide - col).astype(F32)
    tall = iota((HALF, LANES), 0).astype(F32).astype(BF16)
    one, zero = jnp.ones((HALF, LANES), BF16), jnp.zeros((HALF, LANES), BF16)
    none = jnp.zeros((16, LANES), BF16)

    def clear(k, carry):
        field[k] = jnp.zeros(field.shape[1:], F32)
        return carry

    lax.fori_loop(0, levels + 1, clear, 0)

    def group(first_pair, size):
        for p in range(size):
            parts_of_y = 2 if p % 2 == 0 else 4
            length = NY // parts_of_y
            shift = length.bit_length() - 1
            pair = first_pair + p
            k = level_of[pair]
            rate = width[base + jnp.minimum(k, levels - 1)].astype(F32)
            slope = -1.0 / jnp.full((8, LANES), rate, F32)
            lefts, rights = [], []
            for h in range(2):
                start = pl.multiple_of(32 * pair + 16 * h, 16)
                value = queue[pl.ds(start, 8), :]
                spot = queue[pl.ds(start + 8, 8), :].astype(jnp.int32)
                xpos = (spot >> 9).astype(F32)
                section = ((spot >> shift) & (parts_of_y - 1)).astype(F32)
                ypos = (spot & (length - 1)).astype(F32)
                gain = jnp.exp(jnp.abs(reach - xpos) * slope)
                gain = gain - pltpu.roll(gain, 4, 0)
                section = jnp.concatenate([section, section], 0).astype(BF16)
                inside = [section == jnp.full((16, LANES), q, BF16) for q in range(parts_of_y)]
                tiles = []
                for x in range(NX_DEV):
                    term = value * jnp.broadcast_to(gain[x : x + 1, :], (8, LANES))
                    top = term.astype(BF16).astype(F32)
                    both = jnp.concatenate([top, term - top], 0).astype(BF16)
                    tiles += [jnp.where(inside[q], both, none) for q in range(parts_of_y)]
                lefts.append(jnp.concatenate(tiles, 0))
                mark = jnp.broadcast_to(ypos[:1], (length, LANES)).astype(BF16)
                rights.append(jnp.where(tall[:length] == mark, one[:length], zero[:length]))
            done = nt_dot(jnp.concatenate(lefts, 1), jnp.concatenate(rights, 1))
            parts = []
            for i in range(parts_of_y * NX_DEV):
                total = done[16 * i : 16 * i + 8] + done[16 * i + 8 : 16 * i + 16]
                parts += [total[:, at : at + LANES] for at in range(0, length, LANES)]
            field[k] = field[k] + jnp.concatenate(parts, 0)

    def long_group(g, carry):
        group(g * UNROLL, UNROLL)
        return carry

    def short_group(g, carry):
        group(done_pairs + g * REST, REST)
        return carry

    groups = count >> 4
    done_pairs = groups * UNROLL
    lax.fori_loop(0, groups, long_group, 0)
    lax.fori_loop(0, (count - done_pairs + REST - 1) >> 2, short_group, 0)


def filter_levels(skip, levels, base, width, table, field, slab):
    lane = iota((8, LANES), 1)
    line = lane.astype(F32)

    def one_level(k):
        slope = -1.0 / jnp.full((8, LANES), width[base + skip + k].astype(F32), F32)
        grid = field[skip + k]
        top = grid.astype(BF16)
        rest = (grid - top.astype(F32)).astype(BF16)
        mat = table[k, :LANES, :]
        done = nn_dot(jnp.concatenate([top, rest], 1), jnp.concatenate([mat, mat], 0)) + nn_dot(top, table[k, LANES:, :])
        rise = jnp.exp(line * slope)
        fall = jnp.exp((LANES - 1.0 - line) * slope)
        edge = jnp.exp((LANES - line) * slope)
        hop = jnp.exp(LANES * slope)
        for x in range(NX_DEV):
            ahead, behind, here = [], [], []
            for b in range(4):
                row = (4 * x + b) * 8
                here.append(done[row : row + 8, :LANES])
                moments = done[row : row + 8, LANES:]
                turned = pltpu.roll(moments, LANES // 2, 1)
                ahead.append(jnp.where(lane < LANES // 2, moments, turned))
                behind.append(jnp.where(lane < LANES // 2, turned, moments))
            run = ahead[0]
            for b in range(1, 4):
                here[b] = here[b] + rise * run
                run = ahead[b] + hop * run
            bound = edge * run
            run = behind[3]
            for b in (2, 1, 0):
                here[b] = here[b] + fall * run
                run = behind[b] + hop * run
            for b in (3, 2, 1, 0):
                slab[x, b, pl.ds(pl.multiple_of(8 * k, 8), 8), :] = here[b] - bound
                bound = bound * hop

    def group(g, carry):
        for p in range(4):
            one_level(4 * g + p)
        return carry

    lax.fori_loop(0, levels // 4, group, 0)


def field_kernel(sources, wide, nvar, width, first, start, own, oth, far_table, slab, field, table_rest, *scratch):
    table, table_sems, cue, scalar_cue, sem, store, queue, level_of = scratch
    chunks = 2 * (own.shape[1] - 8) // (2 * nvar + 1)
    levels, part = far_table.shape[0], table.shape[0]
    base = start[0]
    fetch = pltpu.make_async_copy(far_table.at[:part], table, table_sems.at[0])
    fetch_rest = pltpu.make_async_copy(far_table.at[part:], table_rest, table_sems.at[1])
    fetch.start()
    fetch_rest.start()
    count = gather_levels(
        sources, nvar, chunks, base, levels, own, oth, cue, scalar_cue, sem, store, queue, level_of
    )
    spread(wide, levels, base, width, first, queue, level_of, count, field)
    fetch.wait()
    fetch_rest.wait()
    filter_levels(0, part, base, width, table, field, slab)


def rest_kernel(width, start, field, table, slab):
    part = table.shape[0]
    filter_levels(part, part, start[0], width, table, field, slab)


def make_field(own, oth, band_width, first, base, table, nvar, levels, wide):
    sources, rows, _ = own.shape
    chunks = 2 * (rows - 8) // (2 * nvar + 1)
    whole = pl.BlockSpec(memory_space=pltpu.VMEM)
    smem = pl.BlockSpec(memory_space=pltpu.SMEM)
    pairs = levels * sources // 2 + UNROLL + 1
    return pl.pallas_call(
        functools.partial(field_kernel, sources, wide, nvar),
        in_specs=[smem] * 3 + [whole] * 2 + [pl.BlockSpec(memory_space=pltpu.HBM)],
        out_specs=(whole, whole, whole),
        out_shape=(
            jax.ShapeDtypeStruct((NX_DEV, 4, nvar * levels, LANES), F32),
            jax.ShapeDtypeStruct((levels + 1, 32 * NX_DEV, LANES), F32),
            jax.ShapeDtypeStruct((levels // 2,) + table.shape[1:], BF16),
        ),
        scratch_shapes=[
            pltpu.VMEM((levels // 2,) + table.shape[1:], BF16),
            pltpu.SemaphoreType.DMA((2,)),
            pltpu.VMEM((CUES * sources + 8, LANES), jnp.int32),
            pltpu.SMEM((CUES * sources + 8, LANES), jnp.int32),
            pltpu.SemaphoreType.DMA,
            pltpu.VMEM((sources, 16 * chunks + 16, LANES), F32),
            pltpu.VMEM((32 * pairs, LANES), F32),
            pltpu.SMEM((pairs + sources,), jnp.int32),
        ],
        compiler_params=pltpu.CompilerParams(vmem_limit_bytes=46 << 20),
        name="field",
    )(band_width, first, base, own, oth, table)


def filter_rest(band_width, base, field, table, shape):
    whole = pl.BlockSpec(memory_space=pltpu.VMEM)
    smem = pl.BlockSpec(memory_space=pltpu.SMEM)
    return pl.pallas_call(
        rest_kernel,
        in_specs=[smem, smem, whole, whole],
        out_specs=whole,
        out_shape=jax.ShapeDtypeStruct(shape, F32),
        compiler_params=pltpu.CompilerParams(vmem_limit_bytes=16 << 20),
        cost_estimate=pl.CostEstimate(flops=1 << 33, bytes_accessed=32 << 20, transcendentals=0),
        name="rest",
    )(band_width, base, field, table)


def mix_kernel(slab, more, high, low, *refs):
    out = refs[-1]
    rows = high.shape[0]
    half = pl.program_id(0)
    for x in range(NX_DEV):
        part = jnp.concatenate([jnp.concatenate([some[x, 2 * half], some[x, 2 * half + 1]], 1) for some in (slab, more)], 0)
        top = part.astype(BF16)
        rest = (part - top.astype(F32)).astype(BF16)
        term = nn_dot(jnp.concatenate([high[...], low[...]], 0), top)
        term = term[:rows] + term[rows:] + nn_dot(high[...], rest)
        if len(refs) == 1:
            out[half, x] = term
        else:
            term = term + refs[0][half, x]
            flat = out.reshape(8 * term.shape[0], LANES)
            for g in range(2):
                flat[pl.ds(4 * g + x, term.shape[0], stride=8), :] = term[:, g * LANES : (g + 1) * LANES]


def mix(slab, more, mats, *before):
    rows = mats[0].shape[0]
    whole = pl.BlockSpec(memory_space=pltpu.VMEM)
    if before:
        shape = (rows, 16, LANES)
        out_spec = pl.BlockSpec((rows, 8, LANES), lambda i: (0, i, 0))
    else:
        shape = (2, NX_DEV, rows, HALF)
        out_spec = whole
    return pl.pallas_call(
        mix_kernel,
        grid=(2,),
        in_specs=[whole] * (4 + len(before)),
        out_specs=out_spec,
        out_shape=jax.ShapeDtypeStruct(shape, F32),
        compiler_params=pltpu.CompilerParams(vmem_limit_bytes=16 << 20),
        name="mix",
    )(slab, more, *mats, *before)


def on_device(innovations, obs_owner, obs_local, obs_level, band_width, vert_scale, sigma, balance):
    groups = lax.axis_size("sub")
    nvar, _ = innovations.shape
    levels = band_width.shape[0]
    swap = [(0, 1), (1, 0)]
    side = lax.axis_index("var").astype(jnp.int32)
    unit = route(side.reshape(1), innovations, obs_owner, obs_level, obs_local, levels)
    half = levels // 2
    base = half * side
    theirs = lax.ppermute(vert_scale, "var", swap)
    own_mats, oth_mats = mix_matrices(side.reshape(1), vert_scale, theirs, sigma, balance)
    first = (lax.axis_index("sub") * NX_DEV).astype(jnp.int32).reshape(1)
    base = base.reshape(1)
    own = [unit]
    for k in range(2, groups, 2):
        own.append(lax.ppermute(unit, "sub", [(i, (i + k) % groups) for i in range(groups)]))
    far = len(own) // 2
    beside = [(i, i ^ 1) for i in range(groups)]
    near = lax.ppermute(unit, "sub", beside)
    own[far], near, own_mats, oth_mats, when = lax.optimization_barrier((own[far], near, own_mats, oth_mats, base))
    table = tables(band_width, when, half)
    own += [near] + [lax.ppermute(held, "sub", beside) for held in own[1:]]
    own[-1], table = lax.optimization_barrier((own[-1], table))
    own = jnp.stack(own)
    oth = lax.ppermute(own, "var", swap)
    slab, grids, table = make_field(own, oth, band_width, first, base, table, nvar, half, NX_DEV * groups)
    swapped = lax.ppermute(slab, "var", swap)
    more = filter_rest(band_width, base, grids, table, slab.shape)
    more_swapped = lax.ppermute(more, "var", swap)
    swapped, more = lax.optimization_barrier((swapped, more))
    out = mix(swapped, more_swapped, oth_mats, mix(slab, more, own_mats))
    out = out.reshape(nvar, levels, NY // LANES, NX_DEV, LANES)
    return jnp.swapaxes(out, 2, 3).reshape(nvar, levels, NX_DEV, NY)


def solution(mesh):
    in_specs = (
        P("var", ("member", "sub")),
        P(("member", "sub"), None),
        P(("member", "sub")),
        P(("member", "sub"), None),
        P(),
        P("var", None),
        P("var", None),
        P("var", None),
    )
    out_specs = P("var", None, ("member", "sub"), None)
    return jax.shard_map(on_device, mesh=mesh, in_specs=in_specs, out_specs=out_specs, check_vma=False)
```

```python
import functools

import jax
import jax.numpy as jnp
from jax import lax
from jax.experimental import pallas as pl
from jax.experimental.pallas import tpu as pltpu
from jax.sharding import PartitionSpec as P

VB = 6
NX_DEV = 4
NY = 512
LANES = 128
HALF = 256
F32 = jnp.float32
BF16 = jnp.bfloat16


def nt_dot(a, b):
    return lax.dot_general(a, b, (((1,), (1,)), ((), ())), preferred_element_type=F32)


def nn_dot(a, b):
    return jnp.dot(a, b, preferred_element_type=F32)


def iota(shape, dim):
    return lax.broadcasted_iota(jnp.int32, shape, dim)


def route_kernel(side, inn_ref, level_ref, owner_ref, local_ref, pay, inn, level, owner, local, sems, hot, pre, dest, left, right):
    pairs = ((level_ref, level), (inn_ref, inn), (owner_ref, owner), (local_ref, local))
    copies = [pltpu.make_async_copy(src, dst, sems.at[k]) for k, (src, dst) in enumerate(pairs)]
    for copy in copies:
        copy.start()
    for copy in copies:
        copy.wait()
    nvar, nobs = inn.shape
    chunks = nobs // LANES
    levels = hot.shape[0] // chunks
    rows = iota((levels, LANES), 0)
    for c in range(chunks):
        hit = jnp.where(rows == level[c : c + 1, :], 1.0, 0.0)
        hot[c * levels : (c + 1) * levels, :] = hit.astype(BF16)
    before = iota((LANES, 2 * LANES), 0) < iota((LANES, 2 * LANES), 1)
    pre[...] = nn_dot(hot[...], jnp.where(before, 1.0, 0.0).astype(BF16))
    count = jnp.zeros((levels, LANES), F32)
    for c in range(chunks):
        count = count + pre[c * levels : (c + 1) * levels, LANES:]
    lower = iota((levels, levels), 1) < iota((levels, levels), 0)
    base = nn_dot(jnp.where(lower, 1.0, 0.0).astype(BF16), count.astype(BF16))
    lane = iota((levels, LANES), 1)
    starts = jnp.sum(jnp.where(lane == rows, base, 0.0), 0, keepdims=True)
    starts = jnp.where(iota((8, LANES), 1) < levels, starts, float(nobs))
    for c in range(chunks):
        part = pre[c * levels : (c + 1) * levels, :]
        slot = jnp.where(rows == level[c : c + 1, :], part[:, :LANES] + base, 0.0)
        dest[c : c + 1, :] = jnp.sum(slot, 0, keepdims=True).astype(jnp.int32)
        base = base + part[:, LANES:]
    place = owner[...] * (NX_DEV * NY) + local[...]
    rows_hi, rows_lo = iota((chunks, LANES), 0), iota((LANES, LANES), 0)
    for c in range(chunks):
        at = slice(c * LANES, (c + 1) * LANES)
        slot = dest[c : c + 1, :]
        mask = rows_hi == slot // LANES
        right[c] = jnp.where(rows_lo == slot % LANES, 1.0, 0.0).astype(BF16)
        pieces = []
        for v in range(nvar):
            value = inn[v : v + 1, at]
            high = value.astype(BF16).astype(F32)
            pieces += [high, value - high]
        spot = place[c : c + 1, :]
        pieces += [(spot // HALF).astype(F32), (spot % HALF).astype(F32)]
        for q, piece in enumerate(pieces):
            left[c, q * chunks : (q + 1) * chunks, :] = jnp.where(mask, piece, 0.0).astype(BF16)
    packed = nt_dot(
        jnp.concatenate([left[c] for c in range(chunks)], 1),
        jnp.concatenate([right[c] for c in range(chunks)], 1),
    )
    for v in range(nvar):
        both = packed[2 * v * chunks : (2 * v + 1) * chunks] + packed[(2 * v + 1) * chunks : (2 * v + 2) * chunks]
        pay[pl.ds(v, chunks, stride=nvar), :] = both
    high, low = packed[2 * nvar * chunks : (2 * nvar + 1) * chunks], packed[(2 * nvar + 1) * chunks :]
    spots = high * float(HALF) + low
    part = chunks // 2
    low_side = jnp.full((part, LANES), side[0], jnp.int32) == 0
    pay[nvar * chunks : nvar * chunks + part, :] = jnp.where(low_side, spots[:part], spots[part:])
    pay[nvar * chunks + part :, :] = starts


def route(side, innovations, owner, level, local, levels):
    nvar, nobs = innovations.shape
    chunks = nobs // LANES
    pieces = 2 * nvar + 2
    return pl.pallas_call(
        route_kernel,
        out_shape=jax.ShapeDtypeStruct((nvar * chunks + chunks // 2 + 8, LANES), F32),
        in_specs=[pl.BlockSpec(memory_space=pltpu.SMEM)] + [pl.BlockSpec(memory_space=pltpu.HBM)] * 4,
        scratch_shapes=[
            pltpu.VMEM((nvar, nobs), F32),
            pltpu.VMEM((chunks, LANES), jnp.int32),
            pltpu.VMEM((chunks, LANES), jnp.int32),
            pltpu.VMEM((chunks, LANES), jnp.int32),
            pltpu.SemaphoreType.DMA((4,)),
            pltpu.VMEM((chunks * levels, LANES), BF16),
            pltpu.VMEM((chunks * levels, 2 * LANES), F32),
            pltpu.VMEM((chunks, LANES), jnp.int32),
            pltpu.VMEM((chunks, pieces * chunks, LANES), BF16),
            pltpu.VMEM((chunks, LANES, LANES), BF16),
        ],
        compiler_params=pltpu.CompilerParams(vmem_limit_bytes=60 << 20),
        name="route",
    )(side, innovations, level.reshape(chunks, LANES), owner.reshape(chunks, LANES), local.reshape(chunks, LANES))


def table_kernel(width, base, table):
    depth = table.shape[0]
    row, col = iota((LANES, LANES), 0), iota((LANES, LANES), 1)
    near = jnp.abs(row - col).astype(F32)
    far = jnp.where(col < LANES // 2, LANES - row, row + 1).astype(F32)
    for k in range(depth):
        rate = width[base[0] + pl.program_id(0) * depth + k].astype(F32)
        for at, dist in ((0, near), (LANES, far)):
            full = jnp.exp(-dist / rate)
            top = full.astype(BF16)
            table[k, :LANES, at : at + LANES] = top
            table[k, LANES:, at : at + LANES] = (full - top.astype(F32)).astype(BF16)


def tables(band_width, base, levels):
    depth = 8
    spec = pl.BlockSpec((depth, 2 * LANES, 2 * LANES), lambda i: (i, 0, 0))
    shape = jax.ShapeDtypeStruct((levels, 2 * LANES, 2 * LANES), BF16)
    return pl.pallas_call(
        table_kernel,
        grid=(levels // depth,),
        in_specs=[pl.BlockSpec(memory_space=pltpu.SMEM)] * 2,
        out_specs=spec,
        out_shape=shape,
        cost_estimate=pl.CostEstimate(flops=1 << 24, bytes_accessed=8 << 20, transcendentals=1 << 20),
        name="tables",
    )(band_width, base)


def pick(table, chosen):
    return lax.dot_general(
        table, chosen, (((0,), (0,)), ((), ())), precision=lax.Precision.HIGHEST, preferred_element_type=F32
    )


def matrix_kernel(side, scale, theirs, sigma, balance, *outs):
    nvar, levels = scale.shape
    both = 2 * nvar
    cols = outs[0].shape[1]
    depth = cols // both
    for k in range(2):
        here = (side[0] + k) % 2
        scales = (scale, theirs) if k == 0 else (theirs, scale)
        unit = iota((nvar, cols), 1) % both
        pairs = [(held[...], jnp.where(unit == iota((nvar, cols), 0) + nvar * j, 1.0, 0.0)) for j, held in enumerate(scales)]
        own = sum(pick(held, chosen) for held, chosen in pairs)
        gap = iota((levels, cols), 0) - depth * here - iota((levels, cols), 1) // both
        other = jnp.sum(jnp.where(gap == 0, own, 0.0), 0, keepdims=True)
        dist = gap.astype(F32)
        corr = jnp.where(jnp.abs(gap) <= VB, jnp.exp(-dist * dist / (2.0 * own * other)), 0.0)
        order = (iota((both, cols), 1) + nvar * here) % both
        chosen = jnp.where(order == iota((both, cols), 0), 1.0, 0.0)
        weight = jnp.dot(balance[...], chosen, precision=lax.Precision.HIGHEST, preferred_element_type=F32)
        for v in range(nvar):
            spread_out = jnp.where(iota((nvar, cols), 0) == v, 1.0, 0.0)
            full = pick(sigma[...], spread_out) * weight[v : v + 1, :] * corr
            top = full.astype(BF16)
            rows = slice(v * levels, (v + 1) * levels)
            outs[2 * k][rows, :] = top
            outs[2 * k + 1][rows, :] = (full - top.astype(F32)).astype(BF16)


def mix_matrices(side, scale, theirs, sigma, balance):
    nvar, levels = scale.shape
    shape = jax.ShapeDtypeStruct((nvar * levels, nvar * levels), BF16)
    whole = pl.BlockSpec(memory_space=pltpu.VMEM)
    outs = pl.pallas_call(
        matrix_kernel,
        in_specs=[pl.BlockSpec(memory_space=pltpu.SMEM)] + [whole] * 4,
        out_specs=(whole,) * 4,
        out_shape=(shape,) * 4,
        compiler_params=pltpu.CompilerParams(vmem_limit_bytes=12 << 20),
        name="matrices",
    )(side, scale, theirs, sigma, balance)
    return outs[:2], outs[2:]


CUES = 4


def make_cues(sources, starts_row, chunks, base, levels, own, cue):
    end = jnp.zeros((1, LANES), jnp.int32)
    goals = []
    for s in range(sources):
        start = own[s, starts_row : starts_row + 1, :]
        size = (pltpu.roll(start, LANES - 1, 1) - start).astype(jnp.int32)
        start = start.astype(jnp.int32)
        off, put = start & (LANES - 1), end & (LANES - 1)
        row = 16 * jnp.minimum(start >> 7, chunks - 1)
        for j, item in enumerate((row, (put - off) & (LANES - 1), off + (put << 7) + ((put + size) << 14))):
            cue[CUES * s + j : CUES * s + j + 1, :] = item
        goals.append(16 * (end >> 7))
        end = end + size
    lane = iota((1, LANES), 1)
    pairs = jnp.where((lane >= base) & (lane < base + levels), (end + 2 * LANES - 1) >> 8, 0).astype(F32)
    earlier = jnp.where(iota((LANES, LANES), 0) < iota((LANES, LANES), 1), 1.0, 0.0).astype(BF16)
    before = nn_dot(jnp.broadcast_to(pairs, (8, LANES)).astype(BF16), earlier)[:1].astype(jnp.int32)
    count = jnp.sum(pairs, 1, keepdims=True)
    for s, goal in enumerate(goals):
        cue[CUES * s + 3 : CUES * s + 4, :] = 32 * before + goal
    last = CUES * sources
    cue[last : last + 1, :] = before
    cue[last + 1 : last + 2, :] = 32 * before + 16 * (end >> 7)
    cue[last + 2 : last + 3, :] = jnp.broadcast_to(count, (1, LANES)).astype(jnp.int32)


def gather_levels(sources, nvar, chunks, base, levels, own, oth, cue, scalar_cue, sem, store, queue, level_of):
    lane = iota((8, LANES), 1)
    sub = iota((8, LANES), 0)
    make_cues(sources, nvar * chunks + chunks // 2, chunks, base, levels, own, cue)
    copy = pltpu.make_async_copy(cue, scalar_cue, sem)
    copy.start()
    nothing = jnp.zeros((8, LANES), F32)
    for s in range(sources):
        for c in range(0, chunks, 2):
            here, there = own[s, 4 * c : 4 * c + 8, :], oth[s, 4 * c : 4 * c + 8, :]
            store[s, 16 * c : 16 * c + 8, :] = jnp.where(sub < 4, here, pltpu.roll(there, 4, 0))
            store[s, 16 * c + 16 : 16 * c + 24, :] = jnp.where(sub < 4, pltpu.roll(here, 4, 0), there)
        part = chunks // 2
        halves = own[s, nvar * chunks : nvar * chunks + part, :], oth[s, nvar * chunks : nvar * chunks + part, :]
        low_side = jnp.full((part, LANES), base, jnp.int32) == 0
        for h in range(2):
            spot = jnp.where(low_side, halves[h], halves[1 - h])
            for c in range(part):
                at = 16 * (h * part + c) + 8
                store[s, at : at + 8, :] = jnp.broadcast_to(spot[c : c + 1, :], (8, LANES))
        store[s, 16 * chunks :, :] = jnp.zeros((16, LANES), F32)
    copy.wait()
    last = CUES * sources

    def tile(start, at):
        return pl.ds(pl.multiple_of(start, 16) + at, 8)

    def per_level(k):
        lev = base + k
        held, held_spot = nothing, nothing
        for s in range(sources):
            row, turn, word, at = (scalar_cue[CUES * s + j, lev] for j in range(4))
            word = jnp.full((8, LANES), word, jnp.int32)
            put, stop = (word >> 7) & (LANES - 1), word >> 14
            first = lane >= (word & (LANES - 1))
            value = jnp.where(first, store[s, tile(row, 0), :], store[s, tile(row, 16), :])
            value = pltpu.roll(value, turn, 1)
            spot = jnp.where(first, store[s, tile(row, 8), :], store[s, tile(row, 24), :])
            spot = pltpu.roll(spot, turn, 1)
            fresh = (lane >= put) & (lane < stop)
            held = jnp.where(fresh, value, held)
            held_spot = jnp.where(fresh, spot, held_spot)
            queue[tile(at, 0), :] = held
            queue[tile(at, 8), :] = held_spot
            late = lane < stop - LANES
            over = stop >= LANES
            held = jnp.where(over, jnp.where(late, value, 0.0), held)
            held_spot = jnp.where(over, jnp.where(late, spot, 0.0), held_spot)
        at = scalar_cue[last + 1, lev]
        queue[tile(at, 0), :] = held
        queue[tile(at, 8), :] = held_spot
        queue[tile(at, 16), :] = nothing
        queue[tile(at, 24), :] = nothing
        pair = scalar_cue[last, lev]
        for p in range(sources // 2):
            level_of[pair + p] = k

    def group(g, carry):
        for p in range(4):
            per_level(4 * g + p)
        return carry

    lax.fori_loop(0, levels // 4, group, 0)
    pair = scalar_cue[last + 2, 0]
    for p in range(UNROLL):
        level_of[pair + p] = levels
        for at in range(0, 32, 8):
            queue[tile(32 * (pair + p), at), :] = nothing
    return pair


UNROLL = 16
REST = 4


def spread(wide, levels, base, width, first, queue, level_of, count, field):
    sub = iota((8, LANES), 0)
    col = first[0] + sub % 4
    reach = jnp.where(sub < 4, col, 2 * wide - col).astype(F32)
    tall = iota((HALF, LANES), 0).astype(F32).astype(BF16)
    one, zero = jnp.ones((HALF, LANES), BF16), jnp.zeros((HALF, LANES), BF16)
    none = jnp.zeros((16, LANES), BF16)

    def clear(k, carry):
        field[k] = jnp.zeros(field.shape[1:], F32)
        return carry

    lax.fori_loop(0, levels + 1, clear, 0)

    def group(first_pair, size):
        for p in range(size):
            parts_of_y = 2 if p % 2 == 0 else 4
            length = NY // parts_of_y
            shift = length.bit_length() - 1
            pair = first_pair + p
            k = level_of[pair]
            rate = width[base + jnp.minimum(k, levels - 1)].astype(F32)
            slope = -1.0 / jnp.full((8, LANES), rate, F32)
            lefts, rights = [], []
            for h in range(2):
                start = pl.multiple_of(32 * pair + 16 * h, 16)
                value = queue[pl.ds(start, 8), :]
                spot = queue[pl.ds(start + 8, 8), :].astype(jnp.int32)
                xpos = (spot >> 9).astype(F32)
                section = ((spot >> shift) & (parts_of_y - 1)).astype(F32)
                ypos = (spot & (length - 1)).astype(F32)
                gain = jnp.exp(jnp.abs(reach - xpos) * slope)
                gain = gain - pltpu.roll(gain, 4, 0)
                section = jnp.concatenate([section, section], 0).astype(BF16)
                inside = [section == jnp.full((16, LANES), q, BF16) for q in range(parts_of_y)]
                tiles = []
                for x in range(NX_DEV):
                    term = value * jnp.broadcast_to(gain[x : x + 1, :], (8, LANES))
                    top = term.astype(BF16).astype(F32)
                    both = jnp.concatenate([top, term - top], 0).astype(BF16)
                    tiles += [jnp.where(inside[q], both, none) for q in range(parts_of_y)]
                lefts.append(jnp.concatenate(tiles, 0))
                mark = jnp.broadcast_to(ypos[:1], (length, LANES)).astype(BF16)
                rights.append(jnp.where(tall[:length] == mark, one[:length], zero[:length]))
            done = nt_dot(jnp.concatenate(lefts, 1), jnp.concatenate(rights, 1))
            parts = []
            for i in range(parts_of_y * NX_DEV):
                total = done[16 * i : 16 * i + 8] + done[16 * i + 8 : 16 * i + 16]
                parts += [total[:, at : at + LANES] for at in range(0, length, LANES)]
            field[k] = field[k] + jnp.concatenate(parts, 0)

    def long_group(g, carry):
        group(g * UNROLL, UNROLL)
        return carry

    def short_group(g, carry):
        group(done_pairs + g * REST, REST)
        return carry

    groups = count >> 4
    done_pairs = groups * UNROLL
    lax.fori_loop(0, groups, long_group, 0)
    lax.fori_loop(0, (count - done_pairs + REST - 1) >> 2, short_group, 0)


def filter_levels(skip, levels, base, width, table, field, slab):
    lane = iota((8, LANES), 1)
    line = lane.astype(F32)

    def one_level(k):
        slope = -1.0 / jnp.full((8, LANES), width[base + skip + k].astype(F32), F32)
        grid = field[skip + k]
        top = grid.astype(BF16)
        rest = (grid - top.astype(F32)).astype(BF16)
        mat = table[k, :LANES, :]
        done = nn_dot(jnp.concatenate([top, rest], 1), jnp.concatenate([mat, mat], 0)) + nn_dot(top, table[k, LANES:, :])
        rise = jnp.exp(line * slope)
        fall = jnp.exp((LANES - 1.0 - line) * slope)
        edge = jnp.exp((LANES - line) * slope)
        hop = jnp.exp(LANES * slope)
        for x in range(NX_DEV):
            ahead, behind, here = [], [], []
            for b in range(4):
                row = (4 * x + b) * 8
                here.append(done[row : row + 8, :LANES])
                moments = done[row : row + 8, LANES:]
                turned = pltpu.roll(moments, LANES // 2, 1)
                ahead.append(jnp.where(lane < LANES // 2, moments, turned))
                behind.append(jnp.where(lane < LANES // 2, turned, moments))
            run = ahead[0]
            for b in range(1, 4):
                here[b] = here[b] + rise * run
                run = ahead[b] + hop * run
            bound = edge * run
            run = behind[3]
            for b in (2, 1, 0):
                here[b] = here[b] + fall * run
                run = behind[b] + hop * run
            for b in (3, 2, 1, 0):
                slab[x, b, pl.ds(pl.multiple_of(8 * k, 8), 8), :] = here[b] - bound
                bound = bound * hop

    def group(g, carry):
        for p in range(8):
            one_level(8 * g + p)
        return carry

    lax.fori_loop(0, levels // 8, group, 0)


def field_kernel(sources, wide, nvar, width, first, start, own, oth, far_table, slab, field, table_rest, *scratch):
    table, table_sems, cue, scalar_cue, sem, store, queue, level_of = scratch
    chunks = 2 * (own.shape[1] - 8) // (2 * nvar + 1)
    levels, part = far_table.shape[0], table.shape[0]
    base = start[0]
    fetch = pltpu.make_async_copy(far_table.at[:part], table, table_sems.at[0])
    fetch_rest = pltpu.make_async_copy(far_table.at[part:], table_rest, table_sems.at[1])
    fetch.start()
    fetch_rest.start()
    count = gather_levels(
        sources, nvar, chunks, base, levels, own, oth, cue, scalar_cue, sem, store, queue, level_of
    )
    spread(wide, levels, base, width, first, queue, level_of, count, field)
    fetch.wait()
    fetch_rest.wait()
    filter_levels(0, part, base, width, table, field, slab)


def rest_kernel(width, start, field, table, slab):
    part = table.shape[0]
    filter_levels(part, part, start[0], width, table, field, slab)


def make_field(own, oth, band_width, first, base, table, nvar, levels, wide):
    sources, rows, _ = own.shape
    chunks = 2 * (rows - 8) // (2 * nvar + 1)
    whole = pl.BlockSpec(memory_space=pltpu.VMEM)
    smem = pl.BlockSpec(memory_space=pltpu.SMEM)
    pairs = levels * sources // 2 + UNROLL + 1
    return pl.pallas_call(
        functools.partial(field_kernel, sources, wide, nvar),
        in_specs=[smem] * 3 + [whole] * 2 + [pl.BlockSpec(memory_space=pltpu.HBM)],
        out_specs=(whole, whole, whole),
        out_shape=(
            jax.ShapeDtypeStruct((NX_DEV, 4, nvar * levels, LANES), F32),
            jax.ShapeDtypeStruct((levels + 1, 32 * NX_DEV, LANES), F32),
            jax.ShapeDtypeStruct((levels // 2,) + table.shape[1:], BF16),
        ),
        scratch_shapes=[
            pltpu.VMEM((levels // 2,) + table.shape[1:], BF16),
            pltpu.SemaphoreType.DMA((2,)),
            pltpu.VMEM((CUES * sources + 8, LANES), jnp.int32),
            pltpu.SMEM((CUES * sources + 8, LANES), jnp.int32),
            pltpu.SemaphoreType.DMA,
            pltpu.VMEM((sources, 16 * chunks + 16, LANES), F32),
            pltpu.VMEM((32 * pairs, LANES), F32),
            pltpu.SMEM((pairs + sources,), jnp.int32),
        ],
        compiler_params=pltpu.CompilerParams(vmem_limit_bytes=46 << 20),
        name="field",
    )(band_width, first, base, own, oth, table)


def filter_rest(band_width, base, field, table, shape):
    whole = pl.BlockSpec(memory_space=pltpu.VMEM)
    smem = pl.BlockSpec(memory_space=pltpu.SMEM)
    return pl.pallas_call(
        rest_kernel,
        in_specs=[smem, smem, whole, whole],
        out_specs=whole,
        out_shape=jax.ShapeDtypeStruct(shape, F32),
        compiler_params=pltpu.CompilerParams(vmem_limit_bytes=16 << 20),
        cost_estimate=pl.CostEstimate(flops=1 << 33, bytes_accessed=32 << 20, transcendentals=0),
        name="rest",
    )(band_width, base, field, table)


def mix_kernel(slab, more, high, low, *refs):
    out = refs[-1]
    rows = high.shape[0]
    half = pl.program_id(0)
    for x in range(NX_DEV):
        part = jnp.concatenate([jnp.concatenate([some[x, 2 * half], some[x, 2 * half + 1]], 1) for some in (slab, more)], 0)
        top = part.astype(BF16)
        rest = (part - top.astype(F32)).astype(BF16)
        term = nn_dot(jnp.concatenate([high[...], low[...]], 0), top)
        term = term[:rows] + term[rows:] + nn_dot(high[...], rest)
        if len(refs) == 1:
            out[half, x] = term
        else:
            term = term + refs[0][half, x]
            flat = out.reshape(8 * term.shape[0], LANES)
            for g in range(2):
                flat[pl.ds(4 * g + x, term.shape[0], stride=8), :] = term[:, g * LANES : (g + 1) * LANES]


def mix(slab, more, mats, *before):
    rows = mats[0].shape[0]
    whole = pl.BlockSpec(memory_space=pltpu.VMEM)
    if before:
        shape = (rows, 16, LANES)
        out_spec = pl.BlockSpec((rows, 8, LANES), lambda i: (0, i, 0))
    else:
        shape = (2, NX_DEV, rows, HALF)
        out_spec = whole
    return pl.pallas_call(
        mix_kernel,
        grid=(2,),
        in_specs=[whole] * (4 + len(before)),
        out_specs=out_spec,
        out_shape=jax.ShapeDtypeStruct(shape, F32),
        compiler_params=pltpu.CompilerParams(vmem_limit_bytes=16 << 20),
        name="mix",
    )(slab, more, *mats, *before)


def on_device(innovations, obs_owner, obs_local, obs_level, band_width, vert_scale, sigma, balance):
    groups = lax.axis_size("sub")
    nvar, _ = innovations.shape
    levels = band_width.shape[0]
    swap = [(0, 1), (1, 0)]
    side = lax.axis_index("var").astype(jnp.int32)
    unit = route(side.reshape(1), innovations, obs_owner, obs_level, obs_local, levels)
    half = levels // 2
    base = half * side
    theirs = lax.ppermute(vert_scale, "var", swap)
    own_mats, oth_mats = mix_matrices(side.reshape(1), vert_scale, theirs, sigma, balance)
    first = (lax.axis_index("sub") * NX_DEV).astype(jnp.int32).reshape(1)
    base = base.reshape(1)
    own = [unit]
    for k in range(2, groups, 2):
        own.append(lax.ppermute(unit, "sub", [(i, (i + k) % groups) for i in range(groups)]))
    far = len(own) // 2
    beside = [(i, i ^ 1) for i in range(groups)]
    near = lax.ppermute(unit, "sub", beside)
    own[far], near, own_mats, oth_mats, when = lax.optimization_barrier((own[far], near, own_mats, oth_mats, base))
    table = tables(band_width, when, half)
    own += [near] + [lax.ppermute(held, "sub", beside) for held in own[1:]]
    own[-1], table = lax.optimization_barrier((own[-1], table))
    own = jnp.stack(own)
    oth = lax.ppermute(own, "var", swap)
    slab, grids, table = make_field(own, oth, band_width, first, base, table, nvar, half, NX_DEV * groups)
    swapped = lax.ppermute(slab, "var", swap)
    more = filter_rest(band_width, base, grids, table, slab.shape)
    more_swapped = lax.ppermute(more, "var", swap)
    swapped, more = lax.optimization_barrier((swapped, more))
    out = mix(swapped, more_swapped, oth_mats, mix(slab, more, own_mats))
    out = out.reshape(nvar, levels, NY // LANES, NX_DEV, LANES)
    return jnp.swapaxes(out, 2, 3).reshape(nvar, levels, NX_DEV, NY)


def solution(mesh):
    in_specs = (
        P("var", ("member", "sub")),
        P(("member", "sub"), None),
        P(("member", "sub")),
        P(("member", "sub"), None),
        P(),
        P("var", None),
        P("var", None),
        P("var", None),
    )
    out_specs = P("var", None, ("member", "sub"), None)
    return jax.shard_map(on_device, mesh=mesh, in_specs=in_specs, out_specs=out_specs, check_vma=False)
```

```python
import functools

import jax
import jax.numpy as jnp
from jax import lax
from jax.experimental import pallas as pl
from jax.experimental.pallas import tpu as pltpu
from jax.sharding import PartitionSpec as P

VB = 6
NX_DEV = 4
NY = 512
LANES = 128
HALF = 256
F32 = jnp.float32
BF16 = jnp.bfloat16


def nt_dot(a, b):
    return lax.dot_general(a, b, (((1,), (1,)), ((), ())), preferred_element_type=F32)


def nn_dot(a, b):
    return jnp.dot(a, b, preferred_element_type=F32)


def iota(shape, dim):
    return lax.broadcasted_iota(jnp.int32, shape, dim)


def route_kernel(side, inn_ref, level_ref, owner_ref, local_ref, pay, inn, level, owner, local, sems, hot, pre, dest, left, right):
    pairs = ((level_ref, level), (inn_ref, inn), (owner_ref, owner), (local_ref, local))
    copies = [pltpu.make_async_copy(src, dst, sems.at[k]) for k, (src, dst) in enumerate(pairs)]
    for copy in copies:
        copy.start()
    for copy in copies:
        copy.wait()
    nvar, nobs = inn.shape
    chunks = nobs // LANES
    levels = hot.shape[0] // chunks
    rows = iota((levels, LANES), 0)
    for c in range(chunks):
        hit = jnp.where(rows == level[c : c + 1, :], 1.0, 0.0)
        hot[c * levels : (c + 1) * levels, :] = hit.astype(BF16)
    before = iota((LANES, 2 * LANES), 0) < iota((LANES, 2 * LANES), 1)
    pre[...] = nn_dot(hot[...], jnp.where(before, 1.0, 0.0).astype(BF16))
    count = jnp.zeros((levels, LANES), F32)
    for c in range(chunks):
        count = count + pre[c * levels : (c + 1) * levels, LANES:]
    lower = iota((levels, levels), 1) < iota((levels, levels), 0)
    base = nn_dot(jnp.where(lower, 1.0, 0.0).astype(BF16), count.astype(BF16))
    lane = iota((levels, LANES), 1)
    starts = jnp.sum(jnp.where(lane == rows, base, 0.0), 0, keepdims=True)
    starts = jnp.where(iota((8, LANES), 1) < levels, starts, float(nobs))
    for c in range(chunks):
        part = pre[c * levels : (c + 1) * levels, :]
        slot = jnp.where(rows == level[c : c + 1, :], part[:, :LANES] + base, 0.0)
        dest[c : c + 1, :] = jnp.sum(slot, 0, keepdims=True).astype(jnp.int32)
        base = base + part[:, LANES:]
    place = owner[...] * (NX_DEV * NY) + local[...]
    rows_hi, rows_lo = iota((chunks, LANES), 0), iota((LANES, LANES), 0)
    for c in range(chunks):
        at = slice(c * LANES, (c + 1) * LANES)
        slot = dest[c : c + 1, :]
        mask = rows_hi == slot // LANES
        right[c] = jnp.where(rows_lo == slot % LANES, 1.0, 0.0).astype(BF16)
        pieces = []
        for v in range(nvar):
            value = inn[v : v + 1, at]
            high = value.astype(BF16).astype(F32)
            pieces += [high, value - high]
        spot = place[c : c + 1, :]
        pieces += [(spot // HALF).astype(F32), (spot % HALF).astype(F32)]
        for q, piece in enumerate(pieces):
            left[c, q * chunks : (q + 1) * chunks, :] = jnp.where(mask, piece, 0.0).astype(BF16)
    packed = nt_dot(
        jnp.concatenate([left[c] for c in range(chunks)], 1),
        jnp.concatenate([right[c] for c in range(chunks)], 1),
    )
    for v in range(nvar):
        both = packed[2 * v * chunks : (2 * v + 1) * chunks] + packed[(2 * v + 1) * chunks : (2 * v + 2) * chunks]
        pay[pl.ds(v, chunks, stride=nvar), :] = both
    high, low = packed[2 * nvar * chunks : (2 * nvar + 1) * chunks], packed[(2 * nvar + 1) * chunks :]
    spots = high * float(HALF) + low
    part = chunks // 2
    low_side = jnp.full((part, LANES), side[0], jnp.int32) == 0
    pay[nvar * chunks : nvar * chunks + part, :] = jnp.where(low_side, spots[:part], spots[part:])
    pay[nvar * chunks + part :, :] = starts


def route(side, innovations, owner, level, local, levels):
    nvar, nobs = innovations.shape
    chunks = nobs // LANES
    pieces = 2 * nvar + 2
    return pl.pallas_call(
        route_kernel,
        out_shape=jax.ShapeDtypeStruct((nvar * chunks + chunks // 2 + 8, LANES), F32),
        in_specs=[pl.BlockSpec(memory_space=pltpu.SMEM)] + [pl.BlockSpec(memory_space=pltpu.HBM)] * 4,
        scratch_shapes=[
            pltpu.VMEM((nvar, nobs), F32),
            pltpu.VMEM((chunks, LANES), jnp.int32),
            pltpu.VMEM((chunks, LANES), jnp.int32),
            pltpu.VMEM((chunks, LANES), jnp.int32),
            pltpu.SemaphoreType.DMA((4,)),
            pltpu.VMEM((chunks * levels, LANES), BF16),
            pltpu.VMEM((chunks * levels, 2 * LANES), F32),
            pltpu.VMEM((chunks, LANES), jnp.int32),
            pltpu.VMEM((chunks, pieces * chunks, LANES), BF16),
            pltpu.VMEM((chunks, LANES, LANES), BF16),
        ],
        compiler_params=pltpu.CompilerParams(vmem_limit_bytes=60 << 20),
        name="route",
    )(side, innovations, level.reshape(chunks, LANES), owner.reshape(chunks, LANES), local.reshape(chunks, LANES))


def table_kernel(width, base, table):
    depth = table.shape[0]
    row, col = iota((LANES, LANES), 0), iota((LANES, LANES), 1)
    near = jnp.abs(row - col).astype(F32)
    far = jnp.where(col < LANES // 2, LANES - row, row + 1).astype(F32)
    for k in range(depth):
        rate = width[base[0] + pl.program_id(0) * depth + k].astype(F32)
        for at, dist in ((0, near), (LANES, far)):
            full = jnp.exp(-dist / rate)
            top = full.astype(BF16)
            table[k, :LANES, at : at + LANES] = top
            table[k, LANES:, at : at + LANES] = (full - top.astype(F32)).astype(BF16)


def tables(band_width, base, levels):
    depth = 8
    spec = pl.BlockSpec((depth, 2 * LANES, 2 * LANES), lambda i: (i, 0, 0))
    shape = jax.ShapeDtypeStruct((levels, 2 * LANES, 2 * LANES), BF16)
    return pl.pallas_call(
        table_kernel,
        grid=(levels // depth,),
        in_specs=[pl.BlockSpec(memory_space=pltpu.SMEM)] * 2,
        out_specs=spec,
        out_shape=shape,
        cost_estimate=pl.CostEstimate(flops=1 << 24, bytes_accessed=8 << 20, transcendentals=1 << 20),
        name="tables",
    )(band_width, base)


def pick(table, chosen):
    return lax.dot_general(
        table, chosen, (((0,), (0,)), ((), ())), precision=lax.Precision.HIGHEST, preferred_element_type=F32
    )


def matrix_kernel(side, scale, theirs, sigma, balance, *outs):
    nvar, levels = scale.shape
    both = 2 * nvar
    cols = outs[0].shape[1]
    depth = cols // both
    for k in range(2):
        here = (side[0] + k) % 2
        scales = (scale, theirs) if k == 0 else (theirs, scale)
        unit = iota((nvar, cols), 1) % both
        pairs = [(held[...], jnp.where(unit == iota((nvar, cols), 0) + nvar * j, 1.0, 0.0)) for j, held in enumerate(scales)]
        own = sum(pick(held, chosen) for held, chosen in pairs)
        gap = iota((levels, cols), 0) - depth * here - iota((levels, cols), 1) // both
        other = jnp.sum(jnp.where(gap == 0, own, 0.0), 0, keepdims=True)
        dist = gap.astype(F32)
        corr = jnp.where(jnp.abs(gap) <= VB, jnp.exp(-dist * dist / (2.0 * own * other)), 0.0)
        order = (iota((both, cols), 1) + nvar * here) % both
        chosen = jnp.where(order == iota((both, cols), 0), 1.0, 0.0)
        weight = jnp.dot(balance[...], chosen, precision=lax.Precision.HIGHEST, preferred_element_type=F32)
        for v in range(nvar):
            spread_out = jnp.where(iota((nvar, cols), 0) == v, 1.0, 0.0)
            full = pick(sigma[...], spread_out) * weight[v : v + 1, :] * corr
            top = full.astype(BF16)
            rows = slice(v * levels, (v + 1) * levels)
            outs[2 * k][rows, :] = top
            outs[2 * k + 1][rows, :] = (full - top.astype(F32)).astype(BF16)


def mix_matrices(side, scale, theirs, sigma, balance):
    nvar, levels = scale.shape
    shape = jax.ShapeDtypeStruct((nvar * levels, nvar * levels), BF16)
    whole = pl.BlockSpec(memory_space=pltpu.VMEM)
    outs = pl.pallas_call(
        matrix_kernel,
        in_specs=[pl.BlockSpec(memory_space=pltpu.SMEM)] + [whole] * 4,
        out_specs=(whole,) * 4,
        out_shape=(shape,) * 4,
        compiler_params=pltpu.CompilerParams(vmem_limit_bytes=12 << 20),
        name="matrices",
    )(side, scale, theirs, sigma, balance)
    return outs[:2], outs[2:]


CUES = 4


def make_cues(sources, starts_row, chunks, base, levels, own, cue):
    end = jnp.zeros((1, LANES), jnp.int32)
    goals = []
    for s in range(sources):
        start = own[s, starts_row : starts_row + 1, :]
        size = (pltpu.roll(start, LANES - 1, 1) - start).astype(jnp.int32)
        start = start.astype(jnp.int32)
        off, put = start & (LANES - 1), end & (LANES - 1)
        row = 16 * jnp.minimum(start >> 7, chunks - 1)
        for j, item in enumerate((row, (put - off) & (LANES - 1), off + (put << 7) + ((put + size) << 14))):
            cue[CUES * s + j : CUES * s + j + 1, :] = item
        goals.append(16 * (end >> 7))
        end = end + size
    lane = iota((1, LANES), 1)
    pairs = jnp.where((lane >= base) & (lane < base + levels), (end + 2 * LANES - 1) >> 8, 0).astype(F32)
    earlier = jnp.where(iota((LANES, LANES), 0) < iota((LANES, LANES), 1), 1.0, 0.0).astype(BF16)
    before = nn_dot(jnp.broadcast_to(pairs, (8, LANES)).astype(BF16), earlier)[:1].astype(jnp.int32)
    count = jnp.sum(pairs, 1, keepdims=True)
    for s, goal in enumerate(goals):
        cue[CUES * s + 3 : CUES * s + 4, :] = 32 * before + goal
    last = CUES * sources
    cue[last : last + 1, :] = before
    cue[last + 1 : last + 2, :] = 32 * before + 16 * (end >> 7)
    cue[last + 2 : last + 3, :] = jnp.broadcast_to(count, (1, LANES)).astype(jnp.int32)


def gather_levels(sources, nvar, chunks, base, levels, own, oth, cue, scalar_cue, sem, store, queue, level_of):
    lane = iota((8, LANES), 1)
    sub = iota((8, LANES), 0)
    make_cues(sources, nvar * chunks + chunks // 2, chunks, base, levels, own, cue)
    copy = pltpu.make_async_copy(cue, scalar_cue, sem)
    copy.start()
    nothing = jnp.zeros((8, LANES), F32)
    for s in range(sources):
        for c in range(0, chunks, 2):
            here, there = own[s, 4 * c : 4 * c + 8, :], oth[s, 4 * c : 4 * c + 8, :]
            store[s, 16 * c : 16 * c + 8, :] = jnp.where(sub < 4, here, pltpu.roll(there, 4, 0))
            store[s, 16 * c + 16 : 16 * c + 24, :] = jnp.where(sub < 4, pltpu.roll(here, 4, 0), there)
        part = chunks // 2
        halves = own[s, nvar * chunks : nvar * chunks + part, :], oth[s, nvar * chunks : nvar * chunks + part, :]
        low_side = jnp.full((part, LANES), base, jnp.int32) == 0
        for h in range(2):
            spot = jnp.where(low_side, halves[h], halves[1 - h])
            for c in range(part):
                at = 16 * (h * part + c) + 8
                store[s, at : at + 8, :] = jnp.broadcast_to(spot[c : c + 1, :], (8, LANES))
        store[s, 16 * chunks :, :] = jnp.zeros((16, LANES), F32)
    copy.wait()
    last = CUES * sources

    def tile(start, at):
        return pl.ds(pl.multiple_of(start, 16) + at, 8)

    def per_level(k):
        lev = base + k
        held, held_spot = nothing, nothing
        for s in range(sources):
            row, turn, word, at = (scalar_cue[CUES * s + j, lev] for j in range(4))
            word = jnp.full((8, LANES), word, jnp.int32)
            put, stop = (word >> 7) & (LANES - 1), word >> 14
            first = lane >= (word & (LANES - 1))
            value = jnp.where(first, store[s, tile(row, 0), :], store[s, tile(row, 16), :])
            value = pltpu.roll(value, turn, 1)
            spot = jnp.where(first, store[s, tile(row, 8), :], store[s, tile(row, 24), :])
            spot = pltpu.roll(spot, turn, 1)
            fresh = (lane >= put) & (lane < stop)
            held = jnp.where(fresh, value, held)
            held_spot = jnp.where(fresh, spot, held_spot)
            queue[tile(at, 0), :] = held
            queue[tile(at, 8), :] = held_spot
            late = lane < stop - LANES
            over = stop >= LANES
            held = jnp.where(over, jnp.where(late, value, 0.0), held)
            held_spot = jnp.where(over, jnp.where(late, spot, 0.0), held_spot)
        at = scalar_cue[last + 1, lev]
        queue[tile(at, 0), :] = held
        queue[tile(at, 8), :] = held_spot
        queue[tile(at, 16), :] = nothing
        queue[tile(at, 24), :] = nothing
        pair = scalar_cue[last, lev]
        for p in range(sources // 2):
            level_of[pair + p] = k

    def group(g, carry):
        for p in range(8):
            per_level(8 * g + p)
        return carry

    lax.fori_loop(0, levels // 8, group, 0)
    pair = scalar_cue[last + 2, 0]
    for p in range(UNROLL):
        level_of[pair + p] = levels
        for at in range(0, 32, 8):
            queue[tile(32 * (pair + p), at), :] = nothing
    return pair


UNROLL = 16
REST = 4


def spread(wide, levels, base, width, first, queue, level_of, count, field):
    sub = iota((8, LANES), 0)
    col = first[0] + sub % 4
    reach = jnp.where(sub < 4, col, 2 * wide - col).astype(F32)
    tall = iota((HALF, LANES), 0).astype(F32).astype(BF16)
    one, zero = jnp.ones((HALF, LANES), BF16), jnp.zeros((HALF, LANES), BF16)
    none = jnp.zeros((16, LANES), BF16)

    def clear(k, carry):
        field[k] = jnp.zeros(field.shape[1:], F32)
        return carry

    lax.fori_loop(0, levels + 1, clear, 0)

    def group(first_pair, size):
        for p in range(size):
            parts_of_y = 2 if p % 2 == 0 else 4
            length = NY // parts_of_y
            shift = length.bit_length() - 1
            pair = first_pair + p
            k = level_of[pair]
            rate = width[base + jnp.minimum(k, levels - 1)].astype(F32)
            slope = -1.0 / jnp.full((8, LANES), rate, F32)
            lefts, rights = [], []
            for h in range(2):
                start = pl.multiple_of(32 * pair + 16 * h, 16)
                value = queue[pl.ds(start, 8), :]
                spot = queue[pl.ds(start + 8, 8), :].astype(jnp.int32)
                xpos = (spot >> 9).astype(F32)
                section = ((spot >> shift) & (parts_of_y - 1)).astype(F32)
                ypos = (spot & (length - 1)).astype(F32)
                gain = jnp.exp(jnp.abs(reach - xpos) * slope)
                gain = gain - pltpu.roll(gain, 4, 0)
                section = jnp.concatenate([section, section], 0).astype(BF16)
                inside = [section == jnp.full((16, LANES), q, BF16) for q in range(parts_of_y)]
                tiles = []
                for x in range(NX_DEV):
                    term = value * jnp.broadcast_to(gain[x : x + 1, :], (8, LANES))
                    top = term.astype(BF16).astype(F32)
                    both = jnp.concatenate([top, term - top], 0).astype(BF16)
                    tiles += [jnp.where(inside[q], both, none) for q in range(parts_of_y)]
                lefts.append(jnp.concatenate(tiles, 0))
                mark = jnp.broadcast_to(ypos[:1], (length, LANES)).astype(BF16)
                rights.append(jnp.where(tall[:length] == mark, one[:length], zero[:length]))
            done = nt_dot(jnp.concatenate(lefts, 1), jnp.concatenate(rights, 1))
            parts = []
            for i in range(parts_of_y * NX_DEV):
                total = done[16 * i : 16 * i + 8] + done[16 * i + 8 : 16 * i + 16]
                parts += [total[:, at : at + LANES] for at in range(0, length, LANES)]
            field[k] = field[k] + jnp.concatenate(parts, 0)

    def long_group(g, carry):
        group(g * UNROLL, UNROLL)
        return carry

    def short_group(g, carry):
        group(done_pairs + g * REST, REST)
        return carry

    groups = count >> 4
    done_pairs = groups * UNROLL
    lax.fori_loop(0, groups, long_group, 0)
    lax.fori_loop(0, (count - done_pairs + REST - 1) >> 2, short_group, 0)


def filter_levels(skip, levels, base, width, table, field, slab):
    lane = iota((8, LANES), 1)
    line = lane.astype(F32)

    def one_level(k):
        slope = -1.0 / jnp.full((8, LANES), width[base + skip + k].astype(F32), F32)
        grid = field[skip + k]
        top = grid.astype(BF16)
        rest = (grid - top.astype(F32)).astype(BF16)
        mat = table[k, :LANES, :]
        done = nn_dot(jnp.concatenate([top, rest], 1), jnp.concatenate([mat, mat], 0)) + nn_dot(top, table[k, LANES:, :])
        rise = jnp.exp(line * slope)
        fall = jnp.exp((LANES - 1.0 - line) * slope)
        edge = jnp.exp((LANES - line) * slope)
        hop = jnp.exp(LANES * slope)
        for x in range(NX_DEV):
            ahead, behind, here = [], [], []
            for b in range(4):
                row = (4 * x + b) * 8
                here.append(done[row : row + 8, :LANES])
                moments = done[row : row + 8, LANES:]
                turned = pltpu.roll(moments, LANES // 2, 1)
                ahead.append(jnp.where(lane < LANES // 2, moments, turned))
                behind.append(jnp.where(lane < LANES // 2, turned, moments))
            run = ahead[0]
            for b in range(1, 4):
                here[b] = here[b] + rise * run
                run = ahead[b] + hop * run
            bound = edge * run
            run = behind[3]
            for b in (2, 1, 0):
                here[b] = here[b] + fall * run
                run = behind[b] + hop * run
            for b in (3, 2, 1, 0):
                slab[x, b, pl.ds(pl.multiple_of(8 * k, 8), 8), :] = here[b] - bound
                bound = bound * hop

    def group(g, carry):
        for p in range(16):
            one_level(16 * g + p)
        return carry

    lax.fori_loop(0, levels // 16, group, 0)


def field_kernel(sources, wide, nvar, width, first, start, own, oth, far_table, slab, field, table_rest, *scratch):
    table, table_sems, cue, scalar_cue, sem, store, queue, level_of = scratch
    chunks = 2 * (own.shape[1] - 8) // (2 * nvar + 1)
    levels, part = far_table.shape[0], table.shape[0]
    base = start[0]
    fetch = pltpu.make_async_copy(far_table.at[:part], table, table_sems.at[0])
    fetch_rest = pltpu.make_async_copy(far_table.at[part:], table_rest, table_sems.at[1])
    fetch.start()
    fetch_rest.start()
    count = gather_levels(
        sources, nvar, chunks, base, levels, own, oth, cue, scalar_cue, sem, store, queue, level_of
    )
    spread(wide, levels, base, width, first, queue, level_of, count, field)
    fetch.wait()
    fetch_rest.wait()
    filter_levels(0, part, base, width, table, field, slab)


def rest_kernel(width, start, field, table, slab):
    part = table.shape[0]
    filter_levels(part, part, start[0], width, table, field, slab)


def make_field(own, oth, band_width, first, base, table, nvar, levels, wide):
    sources, rows, _ = own.shape
    chunks = 2 * (rows - 8) // (2 * nvar + 1)
    whole = pl.BlockSpec(memory_space=pltpu.VMEM)
    smem = pl.BlockSpec(memory_space=pltpu.SMEM)
    pairs = levels * sources // 2 + UNROLL + 1
    return pl.pallas_call(
        functools.partial(field_kernel, sources, wide, nvar),
        in_specs=[smem] * 3 + [whole] * 2 + [pl.BlockSpec(memory_space=pltpu.HBM)],
        out_specs=(whole, whole, whole),
        out_shape=(
            jax.ShapeDtypeStruct((NX_DEV, 4, nvar * levels, LANES), F32),
            jax.ShapeDtypeStruct((levels + 1, 32 * NX_DEV, LANES), F32),
            jax.ShapeDtypeStruct((levels // 2,) + table.shape[1:], BF16),
        ),
        scratch_shapes=[
            pltpu.VMEM((levels // 2,) + table.shape[1:], BF16),
            pltpu.SemaphoreType.DMA((2,)),
            pltpu.VMEM((CUES * sources + 8, LANES), jnp.int32),
            pltpu.SMEM((CUES * sources + 8, LANES), jnp.int32),
            pltpu.SemaphoreType.DMA,
            pltpu.VMEM((sources, 16 * chunks + 16, LANES), F32),
            pltpu.VMEM((32 * pairs, LANES), F32),
            pltpu.SMEM((pairs + sources,), jnp.int32),
        ],
        compiler_params=pltpu.CompilerParams(vmem_limit_bytes=46 << 20),
        name="field",
    )(band_width, first, base, own, oth, table)


def filter_rest(band_width, base, field, table, shape):
    whole = pl.BlockSpec(memory_space=pltpu.VMEM)
    smem = pl.BlockSpec(memory_space=pltpu.SMEM)
    return pl.pallas_call(
        rest_kernel,
        in_specs=[smem, smem, whole, whole],
        out_specs=whole,
        out_shape=jax.ShapeDtypeStruct(shape, F32),
        compiler_params=pltpu.CompilerParams(vmem_limit_bytes=16 << 20),
        cost_estimate=pl.CostEstimate(flops=1 << 33, bytes_accessed=32 << 20, transcendentals=0),
        name="rest",
    )(band_width, base, field, table)


def mix_kernel(slab, more, high, low, *refs):
    out = refs[-1]
    rows = high.shape[0]
    half = pl.program_id(0)
    for x in range(NX_DEV):
        part = jnp.concatenate([jnp.concatenate([some[x, 2 * half], some[x, 2 * half + 1]], 1) for some in (slab, more)], 0)
        top = part.astype(BF16)
        rest = (part - top.astype(F32)).astype(BF16)
        term = nn_dot(jnp.concatenate([high[...], low[...]], 0), top)
        term = term[:rows] + term[rows:] + nn_dot(high[...], rest)
        if len(refs) == 1:
            out[half, x] = term
        else:
            term = term + refs[0][half, x]
            flat = out.reshape(8 * term.shape[0], LANES)
            for g in range(2):
                flat[pl.ds(4 * g + x, term.shape[0], stride=8), :] = term[:, g * LANES : (g + 1) * LANES]


def mix(slab, more, mats, *before):
    rows = mats[0].shape[0]
    whole = pl.BlockSpec(memory_space=pltpu.VMEM)
    if before:
        shape = (rows, 16, LANES)
        out_spec = pl.BlockSpec((rows, 8, LANES), lambda i: (0, i, 0))
    else:
        shape = (2, NX_DEV, rows, HALF)
        out_spec = whole
    return pl.pallas_call(
        mix_kernel,
        grid=(2,),
        in_specs=[whole] * (4 + len(before)),
        out_specs=out_spec,
        out_shape=jax.ShapeDtypeStruct(shape, F32),
        compiler_params=pltpu.CompilerParams(vmem_limit_bytes=16 << 20),
        name="mix",
    )(slab, more, *mats, *before)


def on_device(innovations, obs_owner, obs_local, obs_level, band_width, vert_scale, sigma, balance):
    groups = lax.axis_size("sub")
    nvar, _ = innovations.shape
    levels = band_width.shape[0]
    swap = [(0, 1), (1, 0)]
    side = lax.axis_index("var").astype(jnp.int32)
    unit = route(side.reshape(1), innovations, obs_owner, obs_level, obs_local, levels)
    half = levels // 2
    base = half * side
    theirs = lax.ppermute(vert_scale, "var", swap)
    own_mats, oth_mats = mix_matrices(side.reshape(1), vert_scale, theirs, sigma, balance)
    first = (lax.axis_index("sub") * NX_DEV).astype(jnp.int32).reshape(1)
    base = base.reshape(1)
    own = [unit]
    for k in range(2, groups, 2):
        own.append(lax.ppermute(unit, "sub", [(i, (i + k) % groups) for i in range(groups)]))
    far = len(own) // 2
    beside = [(i, i ^ 1) for i in range(groups)]
    near = lax.ppermute(unit, "sub", beside)
    own[far], near, own_mats, oth_mats, when = lax.optimization_barrier((own[far], near, own_mats, oth_mats, base))
    table = tables(band_width, when, half)
    own += [near] + [lax.ppermute(held, "sub", beside) for held in own[1:]]
    own[-1], table = lax.optimization_barrier((own[-1], table))
    own = jnp.stack(own)
    oth = lax.ppermute(own, "var", swap)
    slab, grids, table = make_field(own, oth, band_width, first, base, table, nvar, half, NX_DEV * groups)
    swapped = lax.ppermute(slab, "var", swap)
    more = filter_rest(band_width, base, grids, table, slab.shape)
    more_swapped = lax.ppermute(more, "var", swap)
    swapped, more = lax.optimization_barrier((swapped, more))
    out = mix(swapped, more_swapped, oth_mats, mix(slab, more, own_mats))
    out = out.reshape(nvar, levels, NY // LANES, NX_DEV, LANES)
    return jnp.swapaxes(out, 2, 3).reshape(nvar, levels, NX_DEV, NY)


def solution(mesh):
    in_specs = (
        P("var", ("member", "sub")),
        P(("member", "sub"), None),
        P(("member", "sub")),
        P(("member", "sub"), None),
        P(),
        P("var", None),
        P("var", None),
        P("var", None),
    )
    out_specs = P("var", None, ("member", "sub"), None)
    return jax.shard_map(on_device, mesh=mesh, in_specs=in_specs, out_specs=out_specs, check_vma=False)
```
